512 devices in a mesh: sp: 8 (over z_lo, core), dp: 64 (over z_hi, y, x).
Axes of the slice: x: 4, y: 4, z: 16 (z_hi: 4, z_lo: 4; z = z_hi * 4 + z_lo), core: 2. Of those that a mesh axis runs over, the one named last changes fastest.
Arguments:
- inputs: bfloat16 [512, 8, 8, 8, 128], P('dp', 'sp'), may hold values from -16 to 16
- cotangent: bfloat16 [512, 8, 8, 8, 128], P('dp', 'sp'), may hold values from -6 to 6
- w_conv: bfloat16 [3456, 128], replicated, may hold values from -0.109375 to 0.109375
- w_down: bfloat16 [1024, 256], replicated, may hold values from -0.1875 to 0.1875
- w_up: bfloat16 [2048, 128], replicated, may hold values from -0.375 to 0.375
Outputs:
- grad_input: bfloat16 [512, 8, 8, 8, 128], P('dp', 'sp')
- weight_grads: float32 [966656], P('dp')
The draws below stay inside these ranges and needn't reach their ends.
All inputs are finite; a program needn't handle non-finite values.
Results may differ from the reference program's by a relative error of at most 0.017.
Values may be sent and summed in bfloat16 or wider, within the bound.
A program may use at most 64 MiB of HBM per device.

```python
import jax
import jax.numpy as jnp
from jax import lax

C1 = 128
C2 = 256
S = 8
CROPS = 512


def with_spikes(array, rng, source, target, parts, factor):
    def block_of(axis_at):
        return (jnp.arange(array.shape[axis_at]) // (array.shape[axis_at] // parts)).reshape((-1,) + (1,) * (array.ndim - 1 - axis_at))

    near = jax.random.permutation(rng, parts)[block_of(target)]
    second = (block_of(target) + parts // 2) % parts
    return jnp.where((block_of(source) == near) | (block_of(source) == second), factor * array, array)


def block_levels(own_key, shape, cuts, low, high):
    gain, own = 1.0, jax.random.fold_in(own_key, 6)
    for position, parts in cuts:
        heights = jnp.exp(jax.random.uniform(jax.random.fold_in(own, position), (parts,), jnp.float32, low / len(cuts), high / len(cuts)))
        gain = gain * jnp.repeat(heights, shape[position] // parts).reshape([-1 if axis == position else 1 for axis in range(len(shape))])
    return gain


def normal_values(key, shape, deviation, most, split=(), held_as=jnp.bfloat16):
    factor_of = block_levels(key, shape, split, -0.22, 0.18) if split else 1.0
    array = jax.random.normal(key, shape, jnp.float32) * deviation * factor_of
    return jnp.minimum(jnp.maximum(array, -most), most).astype(held_as)


def bell_draw_with(own_key, dims, scale, limit, split, heavy, dtype=jnp.bfloat16):
    result = scale * jax.random.normal(own_key, dims, jnp.float32)
    if split:
        result = result * block_levels(own_key, dims, split, -0.22, 0.18)
    return jnp.clip(with_spikes(result, jax.random.fold_in(own_key, 3), *heavy), -limit, limit).astype(dtype)


def setup_inputs(seed: int = 0) -> dict:
    keys = jax.random.split(jax.random.key(seed), 6)
    return {
        "inputs": bell_draw_with(keys[0], (CROPS, S, S, S, C1), 1.0, 16.0, ((0, 64), (1, 8)), (0, 4, 64, 4.0)),
        "cotangent": normal_values(keys[1], (CROPS, S, S, S, C1), 1.0, 6.0, ((0, 64), (1, 8))),
        "w_conv": normal_values(keys[2], (27 * C1, C1), (27 * C1) ** -0.5, 0.109375),
        "w_down": normal_values(keys[3], (8 * C1, C2), (8 * C1) ** -0.5, 0.1875),
        "w_up": normal_values(keys[4], (8 * C2, C1), C2 ** -0.5, 0.375),
    }


def silu_slope(pre_act):
    sigmoid_value = jax.nn.sigmoid(pre_act)
    return sigmoid_value * (1.0 + pre_act * (1.0 - sigmoid_value))

def unfold_taps(padded):
    first_size = padded.shape[1] - 2
    second_size = padded.shape[2] - 2
    third_size = padded.shape[3] - 2
    pieces = [padded[:, i:i + first_size, j:j + second_size, k:k + third_size, :] for i in range(3) for j in range(3) for k in range(3)]
    stacked = jnp.concatenate(pieces, axis=-1)
    return stacked.reshape(-1, stacked.shape[-1])

def to_blocks(volume):
    shape = volume.shape
    folded = volume.reshape(shape[0], shape[1] // 2, 2, shape[2] // 2, 2, shape[3] // 2, 2, shape[4])
    folded = folded.transpose(0, 1, 3, 5, 2, 4, 6, 7)
    return folded.reshape(-1, 8 * shape[4])

def from_blocks(blocked, shape):
    folded = blocked.reshape(shape[0], shape[1] // 2, shape[2] // 2, shape[3] // 2, 2, 2, 2, shape[4])
    folded = folded.transpose(0, 1, 4, 2, 5, 3, 6, 7)
    return folded.reshape(shape)

def flip_taps(w_conv):
    width_in = w_conv.shape[1]
    return w_conv.reshape(27, width_in, width_in)[::-1].transpose(0, 2, 1).reshape(27 * width_in, width_in)

def deep_level(hidden, upstream, w_down, w_up):
    width_in = hidden.shape[-1]
    width_deep = w_down.shape[1]
    hid_blocks = to_blocks(hidden)
    up_blocks = to_blocks(upstream)
    pre_deep = jnp.dot(hid_blocks, w_down, preferred_element_type=jnp.float32)
    deep_act = jax.nn.silu(pre_deep).astype(jnp.bfloat16)
    w_up_back = w_up.reshape(8, width_deep, width_in).transpose(0, 2, 1).reshape(8 * width_in, width_deep)
    grad_act = jnp.dot(up_blocks, w_up_back, preferred_element_type=jnp.float32)
    grad_up = lax.dot_general(deep_act, up_blocks, (((0,), (0,)), ((), ())), preferred_element_type=jnp.float32)
    grad_up = grad_up.reshape(width_deep, 8, width_in).transpose(1, 0, 2).reshape(8 * width_deep, width_in)
    grad_deep = (grad_act * silu_slope(pre_deep)).astype(jnp.bfloat16)
    grad_down = lax.dot_general(hid_blocks, grad_deep, (((0,), (0,)), ((), ())), preferred_element_type=jnp.float32)
    back_blocks = jnp.dot(grad_deep, w_down.T, preferred_element_type=jnp.float32).astype(jnp.bfloat16)
    return (grad_down, grad_up, from_blocks(back_blocks, hidden.shape))

def reference(inputs, cotangent, w_conv, w_down, w_up):
    width_in = w_conv.shape[1]
    w_flip = flip_taps(w_conv)

    def one_crop(carry, pair):
        volume = pair[0][None]
        upstream = pair[1][None]
        padded = jnp.pad(volume, ((0, 0), (1, 1), (1, 1), (1, 1), (0, 0)))
        columns = unfold_taps(padded)
        pre_conv = jnp.dot(columns, w_conv, preferred_element_type=jnp.float32)
        hidden = jax.nn.silu(pre_conv).astype(jnp.bfloat16).reshape(volume.shape)
        grad_down, grad_up, back_down = deep_level(hidden, upstream, w_down, w_up)
        summed = upstream.astype(jnp.float32).reshape(-1, width_in) + back_down.astype(jnp.float32).reshape(-1, width_in)
        grad_pre = (summed * silu_slope(pre_conv)).astype(jnp.bfloat16)
        grad_conv = lax.dot_general(columns, grad_pre, (((0,), (0,)), ((), ())), preferred_element_type=jnp.float32)
        grad_pad = jnp.pad(grad_pre.reshape(volume.shape), ((0, 0), (1, 1), (1, 1), (1, 1), (0, 0)))
        grad_input = jnp.dot(unfold_taps(grad_pad), w_flip, preferred_element_type=jnp.float32).astype(jnp.bfloat16)
        new_carry = (carry[0] + grad_conv, carry[1] + grad_down, carry[2] + grad_up)
        return (new_carry, grad_input.reshape(volume.shape[1:]))
    start = (jnp.zeros(w_conv.shape, jnp.float32), jnp.zeros(w_down.shape, jnp.float32), jnp.zeros(w_up.shape, jnp.float32))
    totals, grad_input = lax.scan(one_crop, start, (inputs, cotangent))
    norm_factor = 1.0 / jnp.sqrt(jnp.float32(CROPS * S * S * S))
    weight_grads = jnp.concatenate([totals[0].reshape(-1), totals[1].reshape(-1), totals[2].reshape(-1)]) * norm_factor
    return (grad_input, weight_grads)
```

```python
import math

import jax
import jax.numpy as jnp
from jax import lax
from jax.experimental import pallas as pl
from jax.experimental.pallas import tpu as pltpu
from jax.sharding import PartitionSpec as P

MESH = pl.DeviceIdType.MESH
BF = jnp.bfloat16
F32 = jnp.float32

STARTS = (0, 14, 29, 43)
OFFSETS = (0, 6, 4, 10)
SHARE = 118


def silu_slope(pre_act):
    sigmoid_value = jax.nn.sigmoid(pre_act)
    return sigmoid_value * (1.0 + pre_act * (1.0 - sigmoid_value))


def unfold_taps(volume):
    padded = jnp.pad(volume, ((0, 0), (1, 1), (1, 1), (1, 1), (0, 0)))
    size = volume.shape[1]
    pieces = [
        padded[:, i : i + size, j : j + size, k : k + size, :]
        for i in range(3)
        for j in range(3)
        for k in range(3)
    ]
    stacked = jnp.concatenate(pieces, axis=-1)
    return stacked.reshape(-1, stacked.shape[-1])


def to_blocks(volume):
    shape = volume.shape
    folded = volume.reshape(
        shape[0], shape[1] // 2, 2, shape[2] // 2, 2, shape[3] // 2, 2, shape[4]
    )
    folded = folded.transpose(0, 1, 3, 5, 2, 4, 6, 7)
    return folded.reshape(-1, 8 * shape[4])


def from_blocks(blocked, shape):
    folded = blocked.reshape(
        shape[0], shape[1] // 2, shape[2] // 2, shape[3] // 2, 2, 2, 2, shape[4]
    )
    folded = folded.transpose(0, 1, 4, 2, 5, 3, 6, 7)
    return folded.reshape(shape)


def flip_taps(w_conv):
    width_in = w_conv.shape[1]
    return (
        w_conv.reshape(27, width_in, width_in)[::-1]
        .transpose(0, 2, 1)
        .reshape(27 * width_in, width_in)
    )


def deep_level(hidden, upstream, w_down, w_up):
    width_in = hidden.shape[-1]
    width_deep = w_down.shape[1]
    hid_blocks = to_blocks(hidden)
    up_blocks = to_blocks(upstream)
    pre_deep = jnp.dot(hid_blocks, w_down, preferred_element_type=F32)
    deep_act = jax.nn.silu(pre_deep).astype(BF)
    w_up_back = (
        w_up.reshape(8, width_deep, width_in).transpose(0, 2, 1).reshape(8 * width_in, width_deep)
    )
    grad_act = jnp.dot(up_blocks, w_up_back, preferred_element_type=F32)
    grad_up = lax.dot_general(
        deep_act, up_blocks, (((0,), (0,)), ((), ())), preferred_element_type=F32
    )
    grad_up = (
        grad_up.reshape(width_deep, 8, width_in)
        .transpose(1, 0, 2)
        .reshape(8 * width_deep, width_in)
    )
    grad_deep = (grad_act * silu_slope(pre_deep)).astype(BF)
    grad_down = lax.dot_general(
        hid_blocks, grad_deep, (((0,), (0,)), ((), ())), preferred_element_type=F32
    )
    back_blocks = jnp.dot(grad_deep, w_down.T, preferred_element_type=F32).astype(BF)
    return (grad_down, grad_up, from_blocks(back_blocks, hidden.shape))


def group_wait(ref, sem):
    pltpu.make_async_copy(ref, ref, sem).wait()


def reduce_kernel(
    scale, g_ref, out_ref, pair_in, pair_sum, first_in, first_sum, second_in, second_sum, z_in, final,
    pair_send, pair_recv, first_send, first_recv, second_send, second_recv, z_send, z_recv, out_send, out_recv,
):
    sp = lax.axis_index("sp")
    dp = lax.axis_index("dp")
    core = lax.rem(sp, 2)
    z_lo = lax.div(sp, 2)
    z_hi = lax.div(dp, 16)
    y = lax.rem(lax.div(dp, 4), 4)
    x = lax.rem(dp, 4)
    z = z_hi * 4 + z_lo
    my_first = x + core * (y - x)
    my_second = y + core * (x - y)
    step_first = 1 + 3 * core
    step_second = 4 - 3 * core

    def first_peer(d):
        there = lax.rem(my_first + d, 4)
        return there, {"sp": sp, "dp": dp + (there - my_first) * step_first}

    def second_peer(d):
        there = lax.rem(my_second + d, 4)
        return there, {"sp": sp, "dp": dp + (there - my_second) * step_second}

    barrier = pltpu.get_barrier_semaphore()

    def greet(device):
        pl.semaphore_signal(barrier, inc=1, device_id=device, device_id_type=MESH)

    for d in range(1, 8):
        greet({"sp": lax.rem(sp + d, 8), "dp": dp})
    for d in range(1, 4):
        greet(first_peer(d)[1])
        greet(second_peer(d)[1])
        for t in range(4):
            greet({"sp": 2 * t + core, "dp": y * 4 + x + lax.rem(z_hi + d, 4) * 16})
    pl.semaphore_wait(barrier, 25)

    def send(src, dst, send_sem, recv_sem, device):
        copy = pltpu.make_async_remote_copy(
            src_ref=src, dst_ref=dst, send_sem=send_sem, recv_sem=recv_sem, device_id=device, device_id_type=MESH
        )
        copy.start()

    sibling = {"sp": sp + 1 - 2 * core, "dp": dp}

    def pair_start(q):
        for xx in range(4):
            src = g_ref.at[pl.ds(4 * q, 4), pl.ds(STARTS[xx] + 8 * (1 - core), 8)]
            send(src, pair_in.at[q, :, xx], pair_send.at[q], pair_recv.at[q], sibling)

    def pair_finish(q):
        group_wait(pair_in.at[q], pair_recv.at[q])
        for yy in range(4):
            for xx in range(4):
                own = g_ref[4 * q + yy, pl.ds(STARTS[xx] + 8 * core, 8)].astype(F32)
                total = own + pair_in[q, yy, xx].astype(F32)
                pair_sum[q, xx + core * (yy - xx), yy + core * (xx - yy)] = total.astype(BF)
        for d in range(1, 4):
            there, device = first_peer(d)
            send(pair_sum.at[q, there], first_in.at[q, 3 - d], first_send.at[q], first_recv.at[q], device)

    def first_finish(q):
        group_wait(first_in.at[q], first_recv.at[q])
        for s in range(4):
            total = pair_sum[q, my_first, s].astype(F32)
            for d in range(3):
                total = total + first_in[q, d, s].astype(F32)
            first_sum[q, s] = total.astype(BF)
        for d in range(1, 4):
            there, device = second_peer(d)
            send(first_sum.at[q, there], second_in.at[q, 3 - d], second_send.at[q], second_recv.at[q], device)

    def second_finish(q):
        group_wait(second_in.at[q], second_recv.at[q])
        total = first_sum[q, my_second].astype(F32)
        for d in range(3):
            total = total + second_in[q, d].astype(F32)
        second_sum[q] = total.astype(BF)
        for t in range(4):
            @pl.when(4 * q + t != z)
            def _():
                slot = lax.rem(z - (4 * q + t) + 16, 16) - 1
                send(
                    second_sum.at[q, pl.ds(2 * t, 2)], z_in.at[slot], z_send.at[q, t], z_recv,
                    {"sp": 2 * t + core, "dp": dp + (q - z_hi) * 16},
                )

    order = (3, 2, 1, 0)
    for q in order:
        pair_start(q)
    for q in order:
        pair_finish(q)
    for q in order:
        first_finish(q)
    for q in order:
        second_finish(q)

    group_wait(z_in, z_recv)
    total = second_sum[z_hi, pl.ds(2 * z_lo, 2)].astype(F32)
    for d in range(15):
        total = total + z_in[d].astype(F32)
    place = 4 * core + z_lo
    final[place] = total * scale
    for d in range(1, 8):
        send(final.at[place], final.at[place], out_send, out_recv, {"sp": lax.rem(sp + d, 8), "dp": dp})
    group_wait(final.at[pl.ds(0, 7)], out_recv)
    rows = final[...].reshape(128, 128)
    for xx in range(4):
        @pl.when(x == xx)
        def _():
            out_ref[...] = rows[OFFSETS[xx] : OFFSETS[xx] + SHARE]

    for q in order:
        group_wait(pair_in.at[q], pair_send.at[q])
        group_wait(first_in.at[q], first_send.at[q])
        group_wait(second_in.at[q], second_send.at[q])
        for t in range(4):
            @pl.when(4 * q + t != z)
            def _():
                group_wait(z_in.at[0], z_send.at[q, t])
    group_wait(final.at[pl.ds(0, 7)], out_send)


def reduce_grads(rows, scale):
    def kernel(*refs):
        reduce_kernel(scale, *refs)

    dma = pltpu.SemaphoreType.DMA
    return pl.pallas_call(
        kernel,
        out_shape=jax.ShapeDtypeStruct((SHARE, 128), F32),
        in_specs=[pl.BlockSpec(memory_space=pltpu.VMEM)],
        out_specs=pl.BlockSpec(memory_space=pltpu.VMEM),
        scratch_shapes=[
            pltpu.VMEM((4, 4, 4, 8, 8, 128), BF),
            pltpu.VMEM((4, 4, 4, 8, 8, 128), BF),
            pltpu.VMEM((4, 3, 4, 8, 8, 128), BF),
            pltpu.VMEM((4, 4, 8, 8, 128), BF),
            pltpu.VMEM((4, 3, 8, 8, 128), BF),
            pltpu.VMEM((4, 8, 8, 128), BF),
            pltpu.VMEM((15, 2, 8, 128), BF),
            pltpu.VMEM((8, 2, 8, 128), F32),
            dma((4,)), dma((4,)), dma((4,)), dma((4,)), dma((4,)), dma((4,)), dma((4, 4)), dma, dma, dma,
        ],
        compiler_params=pltpu.CompilerParams(
            collective_id=0, has_side_effects=True, vmem_limit_bytes=32 * 1024 * 1024
        ),
        name="reduce_grads",
    )(rows)


def per_device(inputs, cotangent, w_conv, w_down, w_up):
    width_in = w_conv.shape[1]
    crop = lax.all_to_all(inputs, "sp", split_axis=0, concat_axis=1, tiled=True)
    upstream = lax.all_to_all(cotangent, "sp", split_axis=0, concat_axis=1, tiled=True)
    columns = unfold_taps(crop)
    pre_conv = jnp.dot(columns, w_conv, preferred_element_type=F32)
    hidden = jax.nn.silu(pre_conv).astype(BF).reshape(crop.shape)
    grad_down, grad_up, back_down = deep_level(hidden, upstream, w_down, w_up)
    summed = upstream.astype(F32).reshape(-1, width_in) + back_down.astype(F32).reshape(-1, width_in)
    grad_pre = (summed * silu_slope(pre_conv)).astype(BF)
    grad_conv = lax.dot_general(
        columns, grad_pre, (((0,), (0,)), ((), ())), preferred_element_type=F32
    )
    grad_input = jnp.dot(
        unfold_taps(grad_pre.reshape(crop.shape)), flip_taps(w_conv), preferred_element_type=F32
    )
    grad_input = grad_input.astype(BF).reshape(crop.shape)
    grad_input = lax.all_to_all(grad_input, "sp", split_axis=1, concat_axis=0, tiled=True)
    rows = jnp.concatenate(
        [grad_conv.astype(BF), grad_down.astype(BF).reshape(-1, 128), grad_up.astype(BF)], axis=0
    ).reshape(16, 59, 8, 128)
    edge = inputs.shape[2]
    crops = inputs.shape[0] * lax.axis_size("dp")
    share = reduce_grads(rows, 1.0 / math.sqrt(crops * edge * edge * edge))
    return (grad_input, share.reshape(-1))


def solution(mesh):
    return jax.shard_map(
        per_device,
        mesh=mesh,
        in_specs=(P("dp", "sp", None, None, None), P("dp", "sp", None, None, None), P(), P(), P()),
        out_specs=(P("dp", "sp", None, None, None), P("dp")),
        check_vma=False,
    )
```

```python
import math

import jax
import jax.numpy as jnp
from jax import lax
from jax.experimental import pallas as pl
from jax.experimental.pallas import tpu as pltpu
from jax.sharding import PartitionSpec as P

MESH = pl.DeviceIdType.MESH
BF = jnp.bfloat16
F32 = jnp.float32

STARTS = (0, 14, 29, 43)
OFFSETS = (0, 6, 4, 10)
SHARE = 118
TILES = 59
DOWN_TILE = 3456 // 8
UP_TILE = 5504 // 8


def dot(a, b):
    return jnp.dot(a, b, preferred_element_type=F32)


def dot_first(a, b):
    return lax.dot_general(a, b, (((0,), (0,)), ((), ())), preferred_element_type=F32)


def dot_last(a, b):
    return lax.dot_general(a, b, (((1,), (1,)), ((), ())), preferred_element_type=F32)


def order_matrices(order_ref, back_ref, twice_ref):
    row = lax.broadcasted_iota(jnp.int32, (128, 128), 0)
    column = lax.broadcasted_iota(jnp.int32, (128, 128), 1)

    def source(r):
        tap, b, c = r >> 4, (r >> 2) & 3, r & 3
        return ((tap >> 2) << 6) + ((2 * b + ((tap >> 1) & 1)) << 3) + 2 * c + (tap & 1)

    order_ref[...] = jnp.where(column == source(row), 1.0, 0.0).astype(BF)
    back_ref[...] = jnp.where(row == source(column), 1.0, 0.0).astype(BF)
    channel = lax.broadcasted_iota(jnp.int32, (128, 256), 0)
    place = lax.broadcasted_iota(jnp.int32, (128, 256), 1)
    twice_ref[...] = jnp.where(channel == (place >> 1), 1.0, 0.0).astype(BF)


def flip_weights(w_conv_ref, w_flip_ref):
    for t in range(27):
        block = w_conv_ref[128 * (26 - t) : 128 * (27 - t), :]
        w_flip_ref[128 * t : 128 * (t + 1), :] = block.astype(F32).T.astype(BF)


def fill_columns(columns_ref, volume):
    lines = volume.reshape(64, 8, 128)
    k_at = lax.broadcasted_iota(jnp.int32, (64, 8, 128), 1)
    zero_line = jnp.zeros((8, 1, 8, 128), F32)
    for k in range(3):
        moved = lines
        if k == 0:
            moved = jnp.where(k_at == 0, 0.0, pltpu.roll(lines, 1, axis=1))
        if k == 2:
            moved = jnp.where(k_at == 7, 0.0, pltpu.roll(lines, 7, axis=1))
        planes = moved.reshape(8, 8, 8, 128)
        for j in range(3):
            shifted = planes
            if j == 0:
                shifted = jnp.concatenate([zero_line, planes[:, :7]], axis=1)
            if j == 2:
                shifted = jnp.concatenate([planes[:, 1:], zero_line], axis=1)
            lane = 128 * (3 * j + k)
            columns_ref[64:576, lane : lane + 128] = shifted.reshape(512, 128).astype(BF)


def convolve(columns_ref, weights_ref):
    total = dot(columns_ref[0:512, :], weights_ref[0:1152, :])
    total += dot(columns_ref[64:576, :], weights_ref[1152:2304, :])
    total += dot(columns_ref[128:640, :], weights_ref[2304:3456, :])
    return total


def to_blocks(order, volume):
    side_by_side = jnp.concatenate([volume[128 * a : 128 * (a + 1)] for a in range(4)], axis=1)
    moved = dot(order, side_by_side).astype(BF)
    return [
        jnp.concatenate(
            [moved[16 * t : 16 * (t + 1), 128 * a : 128 * (a + 1)] for a in range(4)], axis=0
        )
        for t in range(8)
    ]


def from_blocks(back, blocks):
    stacked = jnp.concatenate(
        [
            jnp.concatenate(
                [blocks[16 * a : 16 * (a + 1), 128 * t : 128 * (t + 1)] for a in range(4)], axis=1
            )
            for t in range(8)
        ],
        axis=0,
    )
    moved = dot(back, stacked)
    return jnp.concatenate([moved[:, 128 * a : 128 * (a + 1)] for a in range(4)], axis=0)


def put_rows(rows_ref, tile, values):
    count = values.shape[0] // 8
    values = values.reshape(count, 8, 128).astype(BF)
    done = 0
    while done < count:
        block, place = divmod(tile + done, TILES)
        size = min(count - done, TILES - place)
        rows_ref[block, place : place + size] = values[done : done + size]
        done += size


def logistic_parts(pre):
    s = jax.nn.sigmoid(pre)
    return pre * s, s * (1.0 + pre * (1.0 - s))


def forward(crop_ref, w_conv_ref, columns_ref, slope_ref):
    fill_columns(columns_ref, crop_ref[...].reshape(512, 128).astype(F32))
    hidden, slope = logistic_parts(convolve(columns_ref, w_conv_ref))
    slope_ref[...] = slope
    return hidden.astype(BF)


def deep_forward(hid_taps, w_down_ref):
    pre_deep = dot(jnp.concatenate(hid_taps, axis=1), w_down_ref[...])
    act, slope = logistic_parts(pre_deep)
    return act.astype(BF), slope


def up_grads(rows_ref, deep_act, up_taps):
    for t in range(8):
        put_rows(rows_ref, UP_TILE + 32 * t, dot_first(deep_act, up_taps[t]))


def deep_grads(up_taps, slope, w_up_ref):
    grad_act = dot_last(up_taps[0], w_up_ref[0:256, :])
    for t in range(1, 8):
        grad_act += dot_last(up_taps[t], w_up_ref[256 * t : 256 * (t + 1), :])
    return (grad_act * slope).astype(BF)


def down_grads(rows_ref, hid_taps, twice, grad_deep):
    odd = (lax.broadcasted_iota(jnp.int32, (256, 128), 0) & 1) == 1
    doubled = dot(jnp.concatenate(hid_taps, axis=0), twice).astype(BF)
    for t in range(8):
        both = dot_first(doubled[64 * t : 64 * (t + 1)], grad_deep)
        put_rows(rows_ref, DOWN_TILE + 32 * t, jnp.where(odd, both[:, 128:], both[:, :128]))


def pre_grads(cotangent_ref, grad_deep, w_down_ref, back, slope_ref):
    blocks = dot_last(grad_deep, w_down_ref[...]).astype(BF)
    summed = cotangent_ref[...].reshape(512, 128).astype(F32) + from_blocks(back, blocks)
    return summed * slope_ref[...]


def conv_grads_late(rows_ref, turned_ref, padded_ref, grad_pre):
    padded_ref[64:576, 0:128] = grad_pre
    padded_ref[128:640, 128:256] = grad_pre
    total = dot(turned_ref[...], padded_ref[...])
    for i in (1, 2):
        put_rows(rows_ref, 144 * i, total[:, 128 * (i - 1) : 128 * i])


def conv_grads_early(rows_ref, turned_ref, grad_pre):
    put_rows(rows_ref, 0, dot(turned_ref[:, 0:512], grad_pre))


def group_wait(ref, sem):
    pltpu.make_async_copy(ref, ref, sem).wait()


def step_kernel(
    scale,
    inputs_ref, cotangent_ref, w_conv_any, w_down_any, w_up_any,
    grad_input_ref, share_ref,
    crop, upstream, w_conv, w_down, w_up, w_flip, columns, turned, padded, slope, order, back, twice, rows, grad_out,
    pair_in, pair_sum, first_in, first_sum, second_in, second_sum, z_in, final,
    load_sem, own_sem, crop_send, crop_recv, up_send, up_recv, grad_send, grad_recv,
    pair_send, pair_recv, first_send, first_recv, second_send, second_recv, z_send, z_recv, out_send, out_recv,
):
    sp = lax.axis_index("sp")
    dp = lax.axis_index("dp")
    core = lax.rem(sp, 2)
    z_lo = lax.div(sp, 2)
    z_hi = lax.div(dp, 16)
    y = lax.rem(lax.div(dp, 4), 4)
    x = lax.rem(dp, 4)
    z = z_hi * 4 + z_lo
    my_first = x + core * (y - x)
    my_second = y + core * (x - y)
    step_first = 1 + 3 * core
    step_second = 4 - 3 * core

    def member(d):
        there = lax.rem(sp + d, 8)
        return there, {"sp": there, "dp": dp}

    def first_peer(d):
        there = lax.rem(my_first + d, 4)
        return there, {"sp": sp, "dp": dp + (there - my_first) * step_first}

    def second_peer(d):
        there = lax.rem(my_second + d, 4)
        return there, {"sp": sp, "dp": dp + (there - my_second) * step_second}

    barrier = pltpu.get_barrier_semaphore()

    def greet(device):
        pl.semaphore_signal(barrier, inc=1, device_id=device, device_id_type=MESH)

    def send(src, dst, send_sem, recv_sem, device):
        pltpu.make_async_remote_copy(
            src_ref=src, dst_ref=dst, send_sem=send_sem, recv_sem=recv_sem, device_id=device, device_id_type=MESH
        ).start()

    for d in range(1, 8):
        greet(member(d)[1])
    for d in range(1, 4):
        greet(first_peer(d)[1])
        greet(second_peer(d)[1])
        for t in range(4):
            greet({"sp": 2 * t + core, "dp": y * 4 + x + lax.rem(z_hi + d, 4) * 16})

    loads = [
        pltpu.make_async_copy(inputs_ref.at[sp], crop.at[sp], own_sem.at[0]),
        pltpu.make_async_copy(cotangent_ref.at[sp], upstream.at[sp], own_sem.at[1]),
        pltpu.make_async_copy(w_conv_any, w_conv, load_sem.at[0]),
        pltpu.make_async_copy(w_down_any, w_down, load_sem.at[1]),
        pltpu.make_async_copy(w_up_any, w_up, load_sem.at[2]),
    ]
    for load in loads:
        load.start()
    pl.semaphore_wait(barrier, 25)

    for d in range(1, 8):
        there, device = member(d)
        send(inputs_ref.at[there], crop.at[sp], crop_send, crop_recv.at[7 - d], device)
    for d in range(1, 8):
        there, device = member(d)
        send(cotangent_ref.at[there], upstream.at[sp], up_send, up_recv.at[7 - d], device)

    sibling = {"sp": sp + 1 - 2 * core, "dp": dp}

    def pair_start(q):
        for xx in range(4):
            src = rows.at[pl.ds(4 * q, 4), pl.ds(STARTS[xx] + 8 * (1 - core), 8)]
            send(src, pair_in.at[q, :, xx], pair_send.at[q], pair_recv.at[q], sibling)

    def pair_finish(q):
        group_wait(pair_in.at[q], pair_recv.at[q])
        for yy in range(4):
            for xx in range(4):
                own = rows[4 * q + yy, pl.ds(STARTS[xx] + 8 * core, 8)].astype(F32)
                total = own + pair_in[q, yy, xx].astype(F32)
                pair_sum[q, xx + core * (yy - xx), yy + core * (xx - yy)] = total.astype(BF)
        for d in range(1, 4):
            there, device = first_peer(d)
            send(pair_sum.at[q, there], first_in.at[q, 3 - d], first_send.at[q], first_recv.at[q], device)

    def first_finish(q):
        group_wait(first_in.at[q], first_recv.at[q])
        for s in range(4):
            total = pair_sum[q, my_first, s].astype(F32)
            for d in range(3):
                total = total + first_in[q, d, s].astype(F32)
            first_sum[q, s] = total.astype(BF)
        for d in range(1, 4):
            there, device = second_peer(d)
            send(first_sum.at[q, there], second_in.at[q, 3 - d], second_send.at[q], second_recv.at[q], device)

    def second_finish(q):
        group_wait(second_in.at[q], second_recv.at[q])
        total = first_sum[q, my_second].astype(F32)
        for d in range(3):
            total = total + second_in[q, d].astype(F32)
        second_sum[q] = total.astype(BF)
        for t in range(4):
            @pl.when(4 * q + t != z)
            def _():
                slot = lax.rem(z - (4 * q + t) + 16, 16) - 1
                send(
                    second_sum.at[q, pl.ds(2 * t, 2)], z_in.at[slot], z_send.at[q, t], z_recv,
                    {"sp": 2 * t + core, "dp": dp + (q - z_hi) * 16},
                )

    order_matrices(order, back, twice)
    columns[0:64, :] = jnp.zeros((64, 1152), BF)
    columns[576:640, :] = jnp.zeros((64, 1152), BF)
    padded[0:64, 0:128] = jnp.zeros((64, 128), BF)
    padded[576:640, 0:128] = jnp.zeros((64, 128), BF)
    padded[0:128, 128:256] = jnp.zeros((128, 128), BF)
    loads[2].wait()
    flip_weights(w_conv, w_flip)

    loads[0].wait()
    for d in range(7):
        group_wait(crop.at[0], crop_recv.at[d])
    hidden = forward(crop, w_conv, columns, slope)
    hid_taps = to_blocks(order[...], hidden)
    loads[3].wait()
    deep_act, deep_slope = deep_forward(hid_taps, w_down)
    turned[...] = columns[...].T

    loads[1].wait()
    for d in range(7):
        group_wait(upstream.at[0], up_recv.at[d])
    up_taps = to_blocks(order[...], upstream[...].reshape(512, 128))
    up_grads(rows, deep_act, up_taps)
    pair_start(3)
    loads[4].wait()
    grad_deep = deep_grads(up_taps, deep_slope, w_up)
    down_grads(rows, hid_taps, twice[...], grad_deep)
    pair_start(2)
    grad_pre_wide = pre_grads(upstream, grad_deep, w_down, back[...], slope)
    grad_pre = grad_pre_wide.astype(BF)
    conv_grads_late(rows, turned, padded, grad_pre)
    pair_start(1)
    conv_grads_early(rows, turned, grad_pre)
    pair_start(0)

    pair_finish(3)
    pair_finish(2)
    pair_finish(1)
    pair_finish(0)
    fill_columns(columns, grad_pre.astype(F32))
    grad_out[...] = convolve(columns, w_flip).astype(BF).reshape(8, 64, 128)
    for d in range(1, 8):
        there, device = member(d)
        send(grad_out.at[there], grad_input_ref.at[sp], grad_send, grad_recv.at[7 - d], device)
    own_grad = pltpu.make_async_copy(grad_out.at[sp], grad_input_ref.at[sp], own_sem.at[2])
    own_grad.start()
    for q in (3, 2, 1, 0):
        first_finish(q)
    for q in (3, 2, 1, 0):
        second_finish(q)

    group_wait(z_in, z_recv)
    total = second_sum[z_hi, pl.ds(2 * z_lo, 2)].astype(F32)
    for d in range(15):
        total = total + z_in[d].astype(F32)
    place = 4 * core + z_lo
    final[place] = total * scale
    for d in range(1, 8):
        send(final.at[place], final.at[place], out_send, out_recv, member(d)[1])
    group_wait(final.at[pl.ds(0, 7)], out_recv)
    whole = final[...].reshape(128, 128)
    for xx in range(4):
        @pl.when(x == xx)
        def _():
            share_ref[...] = whole[OFFSETS[xx] : OFFSETS[xx] + SHARE]

    own_grad.wait()
    for d in range(7):
        group_wait(grad_out.at[0], grad_recv.at[d])
    group_wait(crop.at[pl.ds(0, 7)], crop_send)
    group_wait(upstream.at[pl.ds(0, 7)], up_send)
    group_wait(grad_out.at[pl.ds(0, 7)], grad_send)
    for q in (3, 2, 1, 0):
        group_wait(pair_in.at[q], pair_send.at[q])
        group_wait(first_in.at[q], first_send.at[q])
        group_wait(second_in.at[q], second_send.at[q])
        for t in range(4):
            @pl.when(4 * q + t != z)
            def _():
                group_wait(z_in.at[0], z_send.at[q, t])
    group_wait(final.at[pl.ds(0, 7)], out_send)


def per_device(inputs, cotangent, w_conv, w_down, w_up):
    edge = inputs.shape[2]
    crops = inputs.shape[0] * lax.axis_size("dp")
    scale = 1.0 / math.sqrt(crops * edge * edge * edge)

    def kernel(*refs):
        step_kernel(scale, *refs)

    dma = pltpu.SemaphoreType.DMA
    vmem = pltpu.VMEM
    grad_input, share = pl.pallas_call(
        kernel,
        out_shape=(
            jax.ShapeDtypeStruct((8, 64, 128), BF),
            jax.ShapeDtypeStruct((SHARE, 128), F32),
        ),
        in_specs=[pl.BlockSpec(memory_space=pl.ANY)] * 5,
        out_specs=(pl.BlockSpec(memory_space=vmem), pl.BlockSpec(memory_space=vmem)),
        scratch_shapes=[
            vmem((8, 64, 128), BF),
            vmem((8, 64, 128), BF),
            vmem((3456, 128), BF),
            vmem((1024, 256), BF),
            vmem((2048, 128), BF),
            vmem((3456, 128), BF),
            vmem((640, 1152), BF),
            vmem((1152, 640), BF),
            vmem((640, 256), BF),
            vmem((512, 128), F32),
            vmem((128, 128), BF),
            vmem((128, 128), BF),
            vmem((128, 256), BF),
            vmem((16, TILES, 8, 128), BF),
            vmem((8, 64, 128), BF),
            vmem((4, 4, 4, 8, 8, 128), BF),
            vmem((4, 4, 4, 8, 8, 128), BF),
            vmem((4, 3, 4, 8, 8, 128), BF),
            vmem((4, 4, 8, 8, 128), BF),
            vmem((4, 3, 8, 8, 128), BF),
            vmem((4, 8, 8, 128), BF),
            vmem((15, 2, 8, 128), BF),
            vmem((8, 2, 8, 128), F32),
            dma((3,)), dma((3,)), dma, dma((7,)), dma, dma((7,)), dma, dma((7,)),
            dma((4,)), dma((4,)), dma((4,)), dma((4,)), dma((4,)), dma((4,)), dma((4, 4)), dma, dma, dma,
        ],
        compiler_params=pltpu.CompilerParams(
            collective_id=0, has_side_effects=True, vmem_limit_bytes=48 * 1024 * 1024
        ),
        name="whole_step",
    )(inputs.reshape(8, 64, 128), cotangent.reshape(8, 64, 128), w_conv, w_down, w_up)
    return (grad_input.reshape(inputs.shape), share.reshape(-1))


def solution(mesh):
    return jax.shard_map(
        per_device,
        mesh=mesh,
        in_specs=(P("dp", "sp", None, None, None), P("dp", "sp", None, None, None), P(), P(), P()),
        out_specs=(P("dp", "sp", None, None, None), P("dp")),
        check_vma=False,
    )
```

```python
import math

import jax
import jax.numpy as jnp
from jax import lax
from jax.experimental import pallas as pl
from jax.experimental.pallas import tpu as pltpu
from jax.sharding import PartitionSpec as P

MESH = pl.DeviceIdType.MESH
BF = jnp.bfloat16
F32 = jnp.float32

STARTS = (0, 14, 29, 43)
OFFSETS = (0, 6, 4, 10)
SHARE = 118
TILES = 59
DOWN_TILE = 3456 // 8
UP_TILE = 5504 // 8


def dot(a, b):
    return jnp.dot(a, b, preferred_element_type=F32)


def dot_first(a, b):
    return lax.dot_general(a, b, (((0,), (0,)), ((), ())), preferred_element_type=F32)


def dot_last(a, b):
    return lax.dot_general(a, b, (((1,), (1,)), ((), ())), preferred_element_type=F32)


def order_matrices(order_ref, back_ref, twice_ref):
    row = lax.broadcasted_iota(jnp.int32, (128, 128), 0)
    column = lax.broadcasted_iota(jnp.int32, (128, 128), 1)

    def source(r):
        tap, b, c = r >> 4, (r >> 2) & 3, r & 3
        return ((tap >> 2) << 6) + ((2 * b + ((tap >> 1) & 1)) << 3) + 2 * c + (tap & 1)

    order_ref[...] = jnp.where(column == source(row), 1.0, 0.0).astype(BF)
    back_ref[...] = jnp.where(row == source(column), 1.0, 0.0).astype(BF)
    channel = lax.broadcasted_iota(jnp.int32, (128, 256), 0)
    place = lax.broadcasted_iota(jnp.int32, (128, 256), 1)
    twice_ref[...] = jnp.where(channel == (place >> 1), 1.0, 0.0).astype(BF)


def flip_weights(w_conv_ref, w_flip_ref):
    for t in range(27):
        block = w_conv_ref[128 * (26 - t) : 128 * (27 - t), :]
        w_flip_ref[128 * t : 128 * (t + 1), :] = block.astype(F32).T.astype(BF)


def fill_columns(columns_ref, first, planes):
    count = planes.shape[0] // 64
    lines = planes.reshape(8 * count, 8, 128)
    k_at = lax.broadcasted_iota(jnp.int32, (8 * count, 8, 128), 1)
    zero_line = jnp.zeros((count, 1, 8, 128), F32)
    for k in range(3):
        moved = lines
        if k == 0:
            moved = jnp.where(k_at == 0, 0.0, pltpu.roll(lines, 1, axis=1))
        if k == 2:
            moved = jnp.where(k_at == 7, 0.0, pltpu.roll(lines, 7, axis=1))
        moved = moved.reshape(count, 8, 8, 128)
        for j in range(3):
            shifted = moved
            if j == 0:
                shifted = jnp.concatenate([zero_line, moved[:, :7]], axis=1)
            if j == 2:
                shifted = jnp.concatenate([moved[:, 1:], zero_line], axis=1)
            lane = 128 * (3 * j + k)
            columns_ref[first : first + 64 * count, lane : lane + 128] = shifted.reshape(64 * count, 128).astype(BF)


def fill_plane(columns_ref, field_ref, plane, count=1):
    values = field_ref[plane : plane + count].reshape(256 * count, 128).astype(F32)
    fill_columns(columns_ref, 256 * plane, values)


def tap_dot(columns_ref, weights_ref, i):
    return dot(columns_ref[256 * i : 256 * i + 512, :], weights_ref[1152 * i : 1152 * (i + 1), :])


def to_blocks(order, volume):
    side_by_side = jnp.concatenate(
        [
            jnp.concatenate([volume[64 * c : 64 * c + 64], volume[64 * c + 256 : 64 * c + 320]], axis=0)
            for c in range(4)
        ],
        axis=1,
    )
    moved = dot(order, side_by_side).astype(BF)
    return [
        jnp.concatenate(
            [moved[16 * t : 16 * (t + 1), 128 * c : 128 * (c + 1)] for c in range(4)], axis=0
        )
        for t in range(8)
    ]


def from_blocks(back, blocks):
    stacked = jnp.concatenate(
        [
            jnp.concatenate(
                [blocks[16 * c : 16 * (c + 1), 128 * t : 128 * (t + 1)] for c in range(4)], axis=1
            )
            for t in range(8)
        ],
        axis=0,
    )
    moved = dot(back, stacked)
    return jnp.concatenate(
        [moved[64 * p : 64 * (p + 1), 128 * c : 128 * (c + 1)] for p in range(2) for c in range(4)], axis=0
    )


def put_rows(rows_ref, tile, values):
    count = values.shape[0] // 8
    values = values.reshape(count, 8, 128).astype(BF)
    done = 0
    while done < count:
        block, place = divmod(tile + done, TILES)
        size = min(count - done, TILES - place)
        rows_ref[block, place : place + size] = values[done : done + size]
        done += size


def logistic_parts(pre):
    s = jax.nn.sigmoid(pre)
    return pre * s, s * (1.0 + pre * (1.0 - s))


def deep_forward(hid_taps, w_down_ref):
    pre_deep = dot(jnp.concatenate(hid_taps, axis=1), w_down_ref[...])
    act, slope = logistic_parts(pre_deep)
    return act.astype(BF), slope


def up_grads(rows_ref, deep_act, up_taps):
    for t in range(8):
        put_rows(rows_ref, UP_TILE + 32 * t, dot_first(deep_act, up_taps[t]))


def deep_grads(up_taps, slope, w_up_ref):
    grad_act = dot_last(up_taps[0], w_up_ref[0:256, :])
    for t in range(1, 8):
        grad_act += dot_last(up_taps[t], w_up_ref[256 * t : 256 * (t + 1), :])
    return (grad_act * slope).astype(BF)


def down_grads(rows_ref, hid_taps, twice, grad_deep):
    odd = (lax.broadcasted_iota(jnp.int32, (256, 128), 0) & 1) == 1
    doubled = dot(jnp.concatenate(hid_taps, axis=0), twice).astype(BF)
    for t in range(8):
        both = dot_first(doubled[64 * t : 64 * (t + 1)], grad_deep)
        put_rows(rows_ref, DOWN_TILE + 32 * t, jnp.where(odd, both[:, 128:], both[:, :128]))


def pre_grads(cotangent_ref, grad_deep, w_down_ref, back, slope_ref):
    blocks = dot_last(grad_deep, w_down_ref[...]).astype(BF)
    summed = cotangent_ref[...].reshape(512, 128).astype(F32) + from_blocks(back, blocks)
    return summed * slope_ref[...]


def conv_grads(rows_ref, turned_ref, grad_pre, i):
    put_rows(rows_ref, 144 * i, dot(turned_ref[:, 256 * i : 256 * i + 512], grad_pre))


def group_wait(ref, sem):
    pltpu.make_async_copy(ref, ref, sem).wait()


def step_kernel(
    scale,
    inputs_ref, cotangent_ref, w_conv_any, w_down_any, w_up_any,
    grad_input_ref, share_ref,
    field, upstream, w_conv, w_down, w_up, w_flip, columns, turned, slope, order, back, twice, rows,
    grad_field, grad_out,
    pair_in, pair_sum, first_in, first_sum, second_in, second_sum, z_in, final,
    load_sem, own_sem, near_send, near_recv, low_recv, high_recv, halo_send, halo_low, halo_high, grad_send, grad_recv,
    pair_send, pair_recv, first_send, first_recv, second_send, second_recv, z_send, z_recv, out_send, out_recv,
):
    sp = lax.axis_index("sp")
    dp = lax.axis_index("dp")
    core = lax.rem(sp, 2)
    z_lo = lax.div(sp, 2)
    z_hi = lax.div(dp, 16)
    y = lax.rem(lax.div(dp, 4), 4)
    x = lax.rem(dp, 4)
    z = z_hi * 4 + z_lo
    my_first = x + core * (y - x)
    my_second = y + core * (x - y)
    step_first = 1 + 3 * core
    step_second = 4 - 3 * core

    def member(d):
        there = lax.rem(sp + d, 8)
        return there, {"sp": there, "dp": dp}

    def first_peer(d):
        there = lax.rem(my_first + d, 4)
        return there, {"sp": sp, "dp": dp + (there - my_first) * step_first}

    def second_peer(d):
        there = lax.rem(my_second + d, 4)
        return there, {"sp": sp, "dp": dp + (there - my_second) * step_second}

    barrier = pltpu.get_barrier_semaphore()

    def greet(device):
        pl.semaphore_signal(barrier, inc=1, device_id=device, device_id_type=MESH)

    def send(src, dst, send_sem, recv_sem, device):
        pltpu.make_async_remote_copy(
            src_ref=src, dst_ref=dst, send_sem=send_sem, recv_sem=recv_sem, device_id=device, device_id_type=MESH
        ).start()

    for d in range(1, 8):
        greet(member(d)[1])
    for d in range(1, 4):
        greet(first_peer(d)[1])
        greet(second_peer(d)[1])
        for t in range(4):
            greet({"sp": 2 * t + core, "dp": y * 4 + x + lax.rem(z_hi + d, 4) * 16})

    own_crops = pl.ds(4 * core, 4)
    far_crops = pl.ds(4 * (1 - core), 4)
    sibling = {"sp": sp + 1 - 2 * core, "dp": dp}
    side = z_lo - 1 + 2 * core
    has_side = jnp.logical_and(side >= 0, side <= 3)
    loads = [
        pltpu.make_async_copy(inputs_ref.at[own_crops], field.at[1 + core], own_sem.at[0]),
        pltpu.make_async_copy(cotangent_ref.at[own_crops], upstream.at[core], own_sem.at[1]),
        pltpu.make_async_copy(w_conv_any, w_conv, load_sem.at[0]),
        pltpu.make_async_copy(w_down_any, w_down, load_sem.at[1]),
        pltpu.make_async_copy(w_up_any, w_up, load_sem.at[2]),
    ]
    for load in loads:
        load.start()

    @pl.when(z_lo == 0)
    def _():
        field[0] = jnp.zeros((4, 64, 128), BF)
        grad_field[0] = jnp.zeros((4, 64, 128), BF)

    @pl.when(z_lo == 3)
    def _():
        field[3] = jnp.zeros((4, 64, 128), BF)
        grad_field[3] = jnp.zeros((4, 64, 128), BF)

    pl.semaphore_wait(barrier, 25)

    @pl.when(core == 0)
    def _():
        @pl.when(z_lo > 0)
        def _():
            for c in range(2):
                send(inputs_ref.at[pl.ds(4 * c, 4)], field.at[3], near_send.at[1 + c], high_recv, {"sp": sp - 2 + c, "dp": dp})

    @pl.when(core == 1)
    def _():
        @pl.when(z_lo < 3)
        def _():
            for c in range(2):
                send(inputs_ref.at[pl.ds(4 * c, 4)], field.at[0], near_send.at[1 + c], low_recv, {"sp": sp + 1 + c, "dp": dp})

    send(inputs_ref.at[far_crops], field.at[1 + core], near_send.at[0], near_recv.at[0], sibling)
    send(cotangent_ref.at[far_crops], upstream.at[core], near_send.at[3], near_recv.at[1], sibling)

    def pair_start(q):
        for xx in range(4):
            src = rows.at[pl.ds(4 * q, 4), pl.ds(STARTS[xx] + 8 * (1 - core), 8)]
            send(src, pair_in.at[q, :, xx], pair_send.at[q], pair_recv.at[q], sibling)

    def pair_finish(q):
        group_wait(pair_in.at[q], pair_recv.at[q])
        for yy in range(4):
            for xx in range(4):
                own = rows[4 * q + yy, pl.ds(STARTS[xx] + 8 * core, 8)].astype(F32)
                total = own + pair_in[q, yy, xx].astype(F32)
                pair_sum[q, xx + core * (yy - xx), yy + core * (xx - yy)] = total.astype(BF)
        for d in range(1, 4):
            there, device = first_peer(d)
            send(pair_sum.at[q, there], first_in.at[q, 3 - d], first_send.at[q], first_recv.at[q], device)

    def first_finish(q):
        group_wait(first_in.at[q], first_recv.at[q])
        for s in range(4):
            total = pair_sum[q, my_first, s].astype(F32)
            for d in range(3):
                total = total + first_in[q, d, s].astype(F32)
            first_sum[q, s] = total.astype(BF)
        for d in range(1, 4):
            there, device = second_peer(d)
            send(first_sum.at[q, there], second_in.at[q, 3 - d], second_send.at[q], second_recv.at[q], device)

    def second_finish(q):
        group_wait(second_in.at[q], second_recv.at[q])
        total = first_sum[q, my_second].astype(F32)
        for d in range(3):
            total = total + second_in[q, d].astype(F32)
        second_sum[q] = total.astype(BF)
        for t in range(4):
            @pl.when(4 * q + t != z)
            def _():
                slot = lax.rem(z - (4 * q + t) + 16, 16) - 1
                send(
                    second_sum.at[q, pl.ds(2 * t, 2)], z_in.at[slot], z_send.at[q, t], z_recv,
                    {"sp": 2 * t + core, "dp": dp + (q - z_hi) * 16},
                )

    order_matrices(order, back, twice)
    loads[2].wait()
    flip_weights(w_conv, w_flip)

    loads[0].wait()
    group_wait(field.at[0], near_recv.at[0])
    fill_plane(columns, field, 1, 2)
    pre_conv = tap_dot(columns, w_conv, 1)
    turned[:, 256:768] = columns[256:768, :].T

    @pl.when(z_lo > 0)
    def _():
        group_wait(field.at[0], low_recv)

    @pl.when(z_lo < 3)
    def _():
        group_wait(field.at[3], high_recv)

    fill_plane(columns, field, 0)
    fill_plane(columns, field, 3)
    pre_conv += tap_dot(columns, w_conv, 0)
    pre_conv += tap_dot(columns, w_conv, 2)
    hidden, pre_slope = logistic_parts(pre_conv)
    slope[...] = pre_slope
    hid_taps = to_blocks(order[...], hidden.astype(BF))
    loads[3].wait()
    deep_act, deep_slope = deep_forward(hid_taps, w_down)

    loads[1].wait()
    group_wait(upstream.at[0], near_recv.at[1])
    up_taps = to_blocks(order[...], upstream[...].reshape(512, 128))
    up_grads(rows, deep_act, up_taps)
    pair_start(3)
    loads[4].wait()
    grad_deep = deep_grads(up_taps, deep_slope, w_up)
    down_grads(rows, hid_taps, twice[...], grad_deep)
    pair_start(2)
    grad_pre = pre_grads(upstream, grad_deep, w_down, back[...], slope).astype(BF)
    grad_field[1:3] = grad_pre.reshape(2, 4, 64, 128)

    @pl.when(z_lo > 0)
    def _():
        send(grad_field.at[1], grad_field.at[3], halo_send.at[0], halo_high, {"sp": sp - 2, "dp": dp})

    @pl.when(z_lo < 3)
    def _():
        send(grad_field.at[2], grad_field.at[0], halo_send.at[1], halo_low, {"sp": sp + 2, "dp": dp})

    turned[:, 0:256] = columns[0:256, :].T
    turned[:, 768:1024] = columns[768:1024, :].T
    conv_grads(rows, turned, grad_pre, 2)
    conv_grads(rows, turned, grad_pre, 1)
    pair_start(1)
    pair_finish(3)
    conv_grads(rows, turned, grad_pre, 0)
    pair_start(0)

    pair_finish(2)
    fill_plane(columns, grad_field, 1, 2)
    pair_finish(1)
    pair_finish(0)
    first_finish(3)

    @pl.when(z_lo > 0)
    def _():
        group_wait(grad_field.at[0], halo_low)

    @pl.when(z_lo < 3)
    def _():
        group_wait(grad_field.at[3], halo_high)

    fill_plane(columns, grad_field, 0)
    fill_plane(columns, grad_field, 3)
    total = tap_dot(columns, w_flip, 0)
    total += tap_dot(columns, w_flip, 1)
    total += tap_dot(columns, w_flip, 2)
    grad_out[...] = total.astype(BF).reshape(2, 4, 64, 128)
    first_finish(2)
    first_finish(1)
    first_finish(0)
    send(grad_out.at[1 - core], grad_input_ref.at[own_crops], grad_send, grad_recv, sibling)
    own_grad = pltpu.make_async_copy(grad_out.at[core], grad_input_ref.at[own_crops], own_sem.at[2])
    own_grad.start()
    for q in (3, 2, 1, 0):
        second_finish(q)

    group_wait(z_in, z_recv)
    total = second_sum[z_hi, pl.ds(2 * z_lo, 2)].astype(F32)
    for d in range(15):
        total = total + z_in[d].astype(F32)
    place = 4 * core + z_lo
    final[place] = total * scale
    for d in range(1, 8):
        send(final.at[place], final.at[place], out_send, out_recv, member(d)[1])
    group_wait(final.at[pl.ds(0, 7)], out_recv)
    whole = final[...].reshape(128, 128)
    for xx in range(4):
        @pl.when(x == xx)
        def _():
            share_ref[...] = whole[OFFSETS[xx] : OFFSETS[xx] + SHARE]

    own_grad.wait()
    group_wait(grad_out.at[0], grad_recv)
    group_wait(grad_out.at[0], grad_send)
    group_wait(field.at[0], near_send.at[0])
    group_wait(field.at[0], near_send.at[3])

    @pl.when(has_side)
    def _():
        group_wait(field.at[0], near_send.at[1])
        group_wait(field.at[0], near_send.at[2])

    @pl.when(z_lo > 0)
    def _():
        group_wait(grad_field.at[0], halo_send.at[0])

    @pl.when(z_lo < 3)
    def _():
        group_wait(grad_field.at[0], halo_send.at[1])

    for q in (3, 2, 1, 0):
        group_wait(pair_in.at[q], pair_send.at[q])
        group_wait(first_in.at[q], first_send.at[q])
        group_wait(second_in.at[q], second_send.at[q])
        for t in range(4):
            @pl.when(4 * q + t != z)
            def _():
                group_wait(z_in.at[0], z_send.at[q, t])
    group_wait(final.at[pl.ds(0, 7)], out_send)


def per_device(inputs, cotangent, w_conv, w_down, w_up):
    edge = inputs.shape[2]
    crops = inputs.shape[0] * lax.axis_size("dp")
    scale = 1.0 / math.sqrt(crops * edge * edge * edge)

    def kernel(*refs):
        step_kernel(scale, *refs)

    dma = pltpu.SemaphoreType.DMA
    vmem = pltpu.VMEM
    grad_input, share = pl.pallas_call(
        kernel,
        out_shape=(
            jax.ShapeDtypeStruct((8, 64, 128), BF),
            jax.ShapeDtypeStruct((SHARE, 128), F32),
        ),
        in_specs=[pl.BlockSpec(memory_space=pl.ANY)] * 5,
        out_specs=(pl.BlockSpec(memory_space=vmem), pl.BlockSpec(memory_space=vmem)),
        scratch_shapes=[
            vmem((4, 4, 64, 128), BF),
            vmem((2, 4, 64, 128), BF),
            vmem((3456, 128), BF),
            vmem((1024, 256), BF),
            vmem((2048, 128), BF),
            vmem((3456, 128), BF),
            vmem((1024, 1152), BF),
            vmem((1152, 1024), BF),
            vmem((512, 128), F32),
            vmem((128, 128), BF),
            vmem((128, 128), BF),
            vmem((128, 256), BF),
            vmem((16, TILES, 8, 128), BF),
            vmem((4, 4, 64, 128), BF),
            vmem((2, 4, 64, 128), BF),
            vmem((4, 4, 4, 8, 8, 128), BF),
            vmem((4, 4, 4, 8, 8, 128), BF),
            vmem((4, 3, 4, 8, 8, 128), BF),
            vmem((4, 4, 8, 8, 128), BF),
            vmem((4, 3, 8, 8, 128), BF),
            vmem((4, 8, 8, 128), BF),
            vmem((15, 2, 8, 128), BF),
            vmem((8, 2, 8, 128), F32),
            dma((3,)), dma((3,)), dma((4,)), dma((2,)), dma, dma, dma((2,)), dma, dma, dma, dma,
            dma((4,)), dma((4,)), dma((4,)), dma((4,)), dma((4,)), dma((4,)), dma((4, 4)), dma, dma, dma,
        ],
        compiler_params=pltpu.CompilerParams(
            collective_id=0, has_side_effects=True, vmem_limit_bytes=55040 * 1024
        ),
        name="whole_step",
    )(inputs.reshape(8, 64, 128), cotangent.reshape(8, 64, 128), w_conv, w_down, w_up)
    return (grad_input.reshape(inputs.shape), share.reshape(-1))


def solution(mesh):
    return jax.shard_map(
        per_device,
        mesh=mesh,
        in_specs=(P("dp", "sp", None, None, None), P("dp", "sp", None, None, None), P(), P(), P()),
        out_specs=(P("dp", "sp", None, None, None), P("dp")),
        check_vma=False,
    )
```

```python
import math

import jax
import jax.numpy as jnp
from jax import lax
from jax.experimental import pallas as pl
from jax.experimental.pallas import tpu as pltpu
from jax.sharding import PartitionSpec as P

MESH = pl.DeviceIdType.MESH
BF = jnp.bfloat16
F32 = jnp.float32

STARTS = (0, 14, 29, 43)
OFFSETS = (0, 6, 4, 10)
SHARE = 118
TILES = 59
DOWN_TILE = 3456 // 8
UP_TILE = 5504 // 8


def dot(a, b):
    return jnp.dot(a, b, preferred_element_type=F32)


def dot_first(a, b):
    return lax.dot_general(a, b, (((0,), (0,)), ((), ())), preferred_element_type=F32)


def dot_last(a, b):
    return lax.dot_general(a, b, (((1,), (1,)), ((), ())), preferred_element_type=F32)


def order_matrices(order_ref, back_ref, twice_ref):
    row = lax.broadcasted_iota(jnp.int32, (128, 128), 0)
    column = lax.broadcasted_iota(jnp.int32, (128, 128), 1)

    def source(r):
        tap, b, c = r >> 4, (r >> 2) & 3, r & 3
        return ((tap >> 2) << 6) + ((2 * b + ((tap >> 1) & 1)) << 3) + 2 * c + (tap & 1)

    order_ref[...] = jnp.where(column == source(row), 1.0, 0.0).astype(BF)
    back_ref[...] = jnp.where(row == source(column), 1.0, 0.0).astype(BF)
    channel = lax.broadcasted_iota(jnp.int32, (128, 256), 0)
    place = lax.broadcasted_iota(jnp.int32, (128, 256), 1)
    twice_ref[...] = jnp.where(channel == (place >> 1), 1.0, 0.0).astype(BF)


def flip_weights(w_conv_ref, w_flip_ref):
    for t in range(27):
        block = w_conv_ref[128 * (26 - t) : 128 * (27 - t), :]
        w_flip_ref[128 * t : 128 * (t + 1), :] = block.astype(F32).T.astype(BF)


def fill_columns(columns_ref, first, planes):
    count = planes.shape[0] // 64
    lines = planes.reshape(8 * count, 8, 128)
    k_at = lax.broadcasted_iota(jnp.int32, (8 * count, 8, 128), 1)
    zero_line = jnp.zeros((count, 1, 8, 128), F32)
    for k in range(3):
        moved = lines
        if k == 0:
            moved = jnp.where(k_at == 0, 0.0, pltpu.roll(lines, 1, axis=1))
        if k == 2:
            moved = jnp.where(k_at == 7, 0.0, pltpu.roll(lines, 7, axis=1))
        moved = moved.reshape(count, 8, 8, 128)
        for j in range(3):
            shifted = moved
            if j == 0:
                shifted = jnp.concatenate([zero_line, moved[:, :7]], axis=1)
            if j == 2:
                shifted = jnp.concatenate([moved[:, 1:], zero_line], axis=1)
            lane = 128 * (3 * j + k)
            columns_ref[first : first + 64 * count, lane : lane + 128] = shifted.reshape(64 * count, 128).astype(BF)


def fill_plane(columns_ref, field_ref, plane, count=1):
    values = field_ref[plane : plane + count].reshape(256 * count, 128).astype(F32)
    fill_columns(columns_ref, 256 * plane, values)


def tap_dot(columns_ref, weights_ref, i):
    return dot(columns_ref[256 * i : 256 * i + 512, :], weights_ref[1152 * i : 1152 * (i + 1), :])


def to_blocks(order, volume):
    side_by_side = jnp.concatenate(
        [
            jnp.concatenate([volume[64 * c : 64 * c + 64], volume[64 * c + 256 : 64 * c + 320]], axis=0)
            for c in range(4)
        ],
        axis=1,
    )
    moved = dot(order, side_by_side).astype(BF)
    return [
        jnp.concatenate(
            [moved[16 * t : 16 * (t + 1), 128 * c : 128 * (c + 1)] for c in range(4)], axis=0
        )
        for t in range(8)
    ]


def from_blocks(back, blocks):
    stacked = jnp.concatenate(
        [
            jnp.concatenate(
                [blocks[16 * c : 16 * (c + 1), 128 * t : 128 * (t + 1)] for c in range(4)], axis=1
            )
            for t in range(8)
        ],
        axis=0,
    )
    moved = dot(back, stacked)
    return jnp.concatenate(
        [moved[64 * p : 64 * (p + 1), 128 * c : 128 * (c + 1)] for p in range(2) for c in range(4)], axis=0
    )


def put_rows(rows_ref, tile, values):
    count = values.shape[0] // 8
    values = values.reshape(count, 8, 128).astype(BF)
    done = 0
    while done < count:
        block, place = divmod(tile + done, TILES)
        size = min(count - done, TILES - place)
        rows_ref[block, place : place + size] = values[done : done + size]
        done += size


def logistic_parts(pre):
    s = jax.nn.sigmoid(pre)
    return pre * s, s * (1.0 + pre * (1.0 - s))


def deep_forward(hid_taps, w_down_ref):
    pre_deep = dot(jnp.concatenate(hid_taps, axis=1), w_down_ref[...])
    act, slope = logistic_parts(pre_deep)
    return act.astype(BF), slope


def up_grads(rows_ref, deep_act, up_taps):
    for t in range(8):
        put_rows(rows_ref, UP_TILE + 32 * t, dot_first(deep_act, up_taps[t]))


def deep_grads(up_taps, slope, w_up_ref):
    grad_act = dot_last(up_taps[0], w_up_ref[0:256, :])
    for t in range(1, 8):
        grad_act += dot_last(up_taps[t], w_up_ref[256 * t : 256 * (t + 1), :])
    return (grad_act * slope).astype(BF)


def down_grads(rows_ref, hid_taps, twice, grad_deep):
    odd = (lax.broadcasted_iota(jnp.int32, (256, 128), 0) & 1) == 1
    doubled = dot(jnp.concatenate(hid_taps, axis=0), twice).astype(BF)
    for t in range(8):
        both = dot_first(doubled[64 * t : 64 * (t + 1)], grad_deep)
        put_rows(rows_ref, DOWN_TILE + 32 * t, jnp.where(odd, both[:, 128:], both[:, :128]))


def pre_grads(cotangent_ref, grad_deep, w_down_ref, back, slope_ref):
    blocks = dot_last(grad_deep, w_down_ref[...]).astype(BF)
    summed = cotangent_ref[...].reshape(512, 128).astype(F32) + from_blocks(back, blocks)
    return summed * slope_ref[...]


def conv_grads(rows_ref, turned_ref, grad_pre, i):
    put_rows(rows_ref, 144 * i, dot(turned_ref[:, 256 * i : 256 * i + 512], grad_pre))


def group_wait(ref, sem):
    pltpu.make_async_copy(ref, ref, sem).wait()


def step_kernel(
    scale,
    inputs_ref, cotangent_ref, w_conv_any, w_down_any, w_up_any,
    grad_input_ref, share_ref,
    field, upstream, w_conv, w_down, w_up, w_flip, columns, turned, slope, order, back, twice, rows,
    grad_field, grad_out,
    pair_in, pair_sum, first_in, first_sum, second_in, second_sum, z_in, final,
    load_sem, own_sem, near_send, near_recv, low_recv, high_recv, halo_send, halo_low, halo_high, grad_send, grad_recv,
    pair_send, pair_recv, first_send, first_recv, second_send, second_recv, z_send, z_recv, out_send, out_recv,
):
    sp = lax.axis_index("sp")
    dp = lax.axis_index("dp")
    core = lax.rem(sp, 2)
    z_lo = lax.div(sp, 2)
    z_hi = lax.div(dp, 16)
    y = lax.rem(lax.div(dp, 4), 4)
    x = lax.rem(dp, 4)
    z = z_hi * 4 + z_lo
    my_first = x + core * (y - x)
    my_second = y + core * (x - y)
    step_first = 1 + 3 * core
    step_second = 4 - 3 * core

    def member(d):
        there = lax.rem(sp + d, 8)
        return there, {"sp": there, "dp": dp}

    def first_peer(d):
        there = lax.rem(my_first + d, 4)
        return there, {"sp": sp, "dp": dp + (there - my_first) * step_first}

    def second_peer(d):
        there = lax.rem(my_second + d, 4)
        return there, {"sp": sp, "dp": dp + (there - my_second) * step_second}

    barrier = pltpu.get_barrier_semaphore()

    def greet(device):
        pl.semaphore_signal(barrier, inc=1, device_id=device, device_id_type=MESH)

    def send(src, dst, send_sem, recv_sem, device):
        pltpu.make_async_remote_copy(
            src_ref=src, dst_ref=dst, send_sem=send_sem, recv_sem=recv_sem, device_id=device, device_id_type=MESH
        ).start()

    at_end = jnp.logical_or(z_lo == 0, z_lo == 3)

    def along_z(offset):
        there = lax.rem(z + offset + 16, 16)
        return {"sp": 2 * lax.rem(there, 4) + core, "dp": dp + (lax.div(there, 4) - z_hi) * 16}

    for place, offsets in enumerate(((-6, -5, -4, -3, -2, -1, 4), (-6, -2, 3), (6, 2, -3), (6, 5, 4, 3, 2, 1, -4))):
        @pl.when(z_lo == place)
        def _():
            for offset in offsets:
                greet(along_z(offset))
    for d in range(1, 8):
        greet(member(d)[1])
    for d in range(1, 4):
        greet(first_peer(d)[1])
        greet(second_peer(d)[1])

    own_crops = pl.ds(4 * core, 4)
    far_crops = pl.ds(4 * (1 - core), 4)
    sibling = {"sp": sp + 1 - 2 * core, "dp": dp}
    side = z_lo - 1 + 2 * core
    has_side = jnp.logical_and(side >= 0, side <= 3)
    loads = [
        pltpu.make_async_copy(inputs_ref.at[own_crops], field.at[1 + core], own_sem.at[0]),
        pltpu.make_async_copy(cotangent_ref.at[own_crops], upstream.at[core], own_sem.at[1]),
        pltpu.make_async_copy(w_conv_any, w_conv, load_sem.at[0]),
        pltpu.make_async_copy(w_down_any, w_down, load_sem.at[1]),
        pltpu.make_async_copy(w_up_any, w_up, load_sem.at[2]),
    ]
    for load in loads:
        load.start()

    @pl.when(z_lo == 0)
    def _():
        field[0] = jnp.zeros((4, 64, 128), BF)
        grad_field[0] = jnp.zeros((4, 64, 128), BF)

    @pl.when(z_lo == 3)
    def _():
        field[3] = jnp.zeros((4, 64, 128), BF)
        grad_field[3] = jnp.zeros((4, 64, 128), BF)

    pl.semaphore_wait(barrier, 16 + 2 * (z_lo - 1) * (z_lo - 2))

    @pl.when(core == 0)
    def _():
        @pl.when(z_lo > 0)
        def _():
            for c in range(2):
                send(inputs_ref.at[pl.ds(4 * c, 4)], field.at[3], near_send.at[1 + c], high_recv, {"sp": sp - 2 + c, "dp": dp})

    @pl.when(core == 1)
    def _():
        @pl.when(z_lo < 3)
        def _():
            for c in range(2):
                send(inputs_ref.at[pl.ds(4 * c, 4)], field.at[0], near_send.at[1 + c], low_recv, {"sp": sp + 1 + c, "dp": dp})

    send(inputs_ref.at[far_crops], field.at[1 + core], near_send.at[0], near_recv.at[0], sibling)
    send(cotangent_ref.at[far_crops], upstream.at[core], near_send.at[3], near_recv.at[1], sibling)

    def goes_low(place):
        return jnp.logical_or(place == 1, place >= 10)

    def goes_high(place):
        return jnp.logical_or(place == 2, jnp.logical_and(place >= 4, place <= 9))

    def pair_start(q):
        for xx in range(4):
            src = rows.at[pl.ds(4 * q, 4), pl.ds(STARTS[xx] + 8 * (1 - core), 8)]
            send(src, pair_in.at[q, :, xx], pair_send.at[q], pair_recv.at[q], sibling)

    def pair_finish(q):
        group_wait(pair_in.at[q], pair_recv.at[q])
        for yy in range(4):
            for xx in range(4):
                own = rows[4 * q + yy, pl.ds(STARTS[xx] + 8 * core, 8)].astype(F32)
                total = own + pair_in[q, yy, xx].astype(F32)
                pair_sum[q, xx + core * (yy - xx), yy + core * (xx - yy)] = total.astype(BF)
        for d in range(1, 4):
            there, device = first_peer(d)
            send(pair_sum.at[q, there], first_in.at[q, 3 - d], first_send.at[q], first_recv.at[q], device)

    def first_finish(q):
        group_wait(first_in.at[q], first_recv.at[q])
        for s in range(4):
            total = pair_sum[q, my_first, s].astype(F32)
            for d in range(3):
                total = total + first_in[q, d, s].astype(F32)
            first_sum[q, s] = total.astype(BF)
        for d in range(1, 4):
            there, device = second_peer(d)
            send(first_sum.at[q, there], second_in.at[q, 3 - d], second_send.at[q], second_recv.at[q], device)

    def second_finish(q):
        group_wait(second_in.at[q], second_recv.at[q])
        total = first_sum[q, my_second].astype(F32)
        for d in range(3):
            total = total + second_in[q, d].astype(F32)
        second_sum[q] = total.astype(BF)
        place = lax.rem(z - 4 * q + 16, 16)
        there = dp + (q - z_hi) * 16

        @pl.when(goes_low(place))
        def _():
            slot = lax.rem(place + 7, 8) * lax.div(place, 10)
            send(second_sum.at[q], z_in.at[slot], z_send.at[q], z_recv, {"sp": core, "dp": there})

        @pl.when(goes_high(place))
        def _():
            slot = (place - 3) * lax.div(place + 12, 16)
            send(second_sum.at[q], z_in.at[slot], z_send.at[q], z_recv, {"sp": 6 + core, "dp": there})

    order_matrices(order, back, twice)
    loads[2].wait()
    flip_weights(w_conv, w_flip)

    loads[0].wait()
    group_wait(field.at[0], near_recv.at[0])
    fill_plane(columns, field, 1, 2)
    pre_conv = tap_dot(columns, w_conv, 1)
    turned[:, 256:768] = columns[256:768, :].T

    @pl.when(z_lo > 0)
    def _():
        group_wait(field.at[0], low_recv)

    @pl.when(z_lo < 3)
    def _():
        group_wait(field.at[3], high_recv)

    fill_plane(columns, field, 0)
    fill_plane(columns, field, 3)
    pre_conv += tap_dot(columns, w_conv, 0)
    pre_conv += tap_dot(columns, w_conv, 2)
    hidden, pre_slope = logistic_parts(pre_conv)
    slope[...] = pre_slope
    hid_taps = to_blocks(order[...], hidden.astype(BF))
    loads[3].wait()
    deep_act, deep_slope = deep_forward(hid_taps, w_down)

    loads[1].wait()
    group_wait(upstream.at[0], near_recv.at[1])
    up_taps = to_blocks(order[...], upstream[...].reshape(512, 128))
    up_grads(rows, deep_act, up_taps)
    pair_start(3)
    loads[4].wait()
    grad_deep = deep_grads(up_taps, deep_slope, w_up)
    down_grads(rows, hid_taps, twice[...], grad_deep)
    pair_start(2)
    grad_pre = pre_grads(upstream, grad_deep, w_down, back[...], slope).astype(BF)
    grad_field[1:3] = grad_pre.reshape(2, 4, 64, 128)

    @pl.when(z_lo > 0)
    def _():
        send(grad_field.at[1], grad_field.at[3], halo_send.at[0], halo_high, {"sp": sp - 2, "dp": dp})

    @pl.when(z_lo < 3)
    def _():
        send(grad_field.at[2], grad_field.at[0], halo_send.at[1], halo_low, {"sp": sp + 2, "dp": dp})

    turned[:, 0:256] = columns[0:256, :].T
    turned[:, 768:1024] = columns[768:1024, :].T
    conv_grads(rows, turned, grad_pre, 2)
    conv_grads(rows, turned, grad_pre, 1)
    pair_start(1)
    pair_finish(3)
    conv_grads(rows, turned, grad_pre, 0)
    pair_start(0)

    pair_finish(2)
    fill_plane(columns, grad_field, 1, 2)
    pair_finish(1)
    pair_finish(0)

    @pl.when(z_lo > 0)
    def _():
        group_wait(grad_field.at[0], halo_low)

    @pl.when(z_lo < 3)
    def _():
        group_wait(grad_field.at[3], halo_high)

    fill_plane(columns, grad_field, 0)
    fill_plane(columns, grad_field, 3)
    total = tap_dot(columns, w_flip, 0)
    total += tap_dot(columns, w_flip, 1)
    total += tap_dot(columns, w_flip, 2)
    grad_out[...] = total.astype(BF).reshape(2, 4, 64, 128)
    for q in (3, 2, 1, 0):
        first_finish(q)
    send(grad_out.at[1 - core], grad_input_ref.at[own_crops], grad_send, grad_recv, sibling)
    own_grad = pltpu.make_async_copy(grad_out.at[core], grad_input_ref.at[own_crops], own_sem.at[2])
    own_grad.start()
    for q in (3, 2, 1, 0):
        second_finish(q)

    @pl.when(at_end)
    def _():
        group_wait(z_in, z_recv)
        total = second_sum[z_hi].astype(F32)
        for d in range(7):
            total = total + z_in[d].astype(F32)
        end = lax.div(z_lo, 3)
        final[end, core] = total.astype(BF)
        for d in range(1, 8):
            send(final.at[end, core], final.at[end, core], out_send, out_recv, member(d)[1])
        group_wait(z_in.at[pl.ds(0, 3)], out_recv)

    @pl.when(jnp.logical_not(at_end))
    def _():
        group_wait(z_in.at[pl.ds(0, 4)], out_recv)

    whole = (final[0].astype(F32) + final[1].astype(F32)).reshape(128, 128) * scale
    for xx in range(4):
        @pl.when(x == xx)
        def _():
            share_ref[...] = whole[OFFSETS[xx] : OFFSETS[xx] + SHARE]

    own_grad.wait()
    group_wait(grad_out.at[0], grad_recv)
    group_wait(grad_out.at[0], grad_send)
    group_wait(field.at[0], near_send.at[0])
    group_wait(field.at[0], near_send.at[3])

    @pl.when(has_side)
    def _():
        group_wait(field.at[0], near_send.at[1])
        group_wait(field.at[0], near_send.at[2])

    @pl.when(z_lo > 0)
    def _():
        group_wait(grad_field.at[0], halo_send.at[0])

    @pl.when(z_lo < 3)
    def _():
        group_wait(grad_field.at[0], halo_send.at[1])

    for q in (3, 2, 1, 0):
        group_wait(pair_in.at[q], pair_send.at[q])
        group_wait(first_in.at[q], first_send.at[q])
        group_wait(second_in.at[q], second_send.at[q])
        place = lax.rem(z - 4 * q + 16, 16)

        @pl.when(jnp.logical_or(goes_low(place), goes_high(place)))
        def _():
            group_wait(z_in.at[0], z_send.at[q])

    @pl.when(at_end)
    def _():
        group_wait(z_in, out_send)


def per_device(inputs, cotangent, w_conv, w_down, w_up):
    edge = inputs.shape[2]
    crops = inputs.shape[0] * lax.axis_size("dp")
    scale = 1.0 / math.sqrt(crops * edge * edge * edge)

    def kernel(*refs):
        step_kernel(scale, *refs)

    dma = pltpu.SemaphoreType.DMA
    vmem = pltpu.VMEM
    grad_input, share = pl.pallas_call(
        kernel,
        out_shape=(
            jax.ShapeDtypeStruct((8, 64, 128), BF),
            jax.ShapeDtypeStruct((SHARE, 128), F32),
        ),
        in_specs=[pl.BlockSpec(memory_space=pl.ANY)] * 5,
        out_specs=(pl.BlockSpec(memory_space=vmem), pl.BlockSpec(memory_space=vmem)),
        scratch_shapes=[
            vmem((4, 4, 64, 128), BF),
            vmem((2, 4, 64, 128), BF),
            vmem((3456, 128), BF),
            vmem((1024, 256), BF),
            vmem((2048, 128), BF),
            vmem((3456, 128), BF),
            vmem((1024, 1152), BF),
            vmem((1152, 1024), BF),
            vmem((512, 128), F32),
            vmem((128, 128), BF),
            vmem((128, 128), BF),
            vmem((128, 256), BF),
            vmem((16, TILES, 8, 128), BF),
            vmem((4, 4, 64, 128), BF),
            vmem((2, 4, 64, 128), BF),
            vmem((4, 4, 4, 8, 8, 128), BF),
            vmem((4, 4, 4, 8, 8, 128), BF),
            vmem((4, 3, 4, 8, 8, 128), BF),
            vmem((4, 4, 8, 8, 128), BF),
            vmem((4, 3, 8, 8, 128), BF),
            vmem((4, 8, 8, 128), BF),
            vmem((7, 8, 8, 128), BF),
            vmem((2, 2, 8, 8, 128), BF),
            dma((3,)), dma((3,)), dma((4,)), dma((2,)), dma, dma, dma((2,)), dma, dma, dma, dma,
            dma((4,)), dma((4,)), dma((4,)), dma((4,)), dma((4,)), dma((4,)), dma((4,)), dma, dma, dma,
        ],
        compiler_params=pltpu.CompilerParams(
            collective_id=0, has_side_effects=True, vmem_limit_bytes=55040 * 1024
        ),
        name="whole_step",
    )(inputs.reshape(8, 64, 128), cotangent.reshape(8, 64, 128), w_conv, w_down, w_up)
    return (grad_input.reshape(inputs.shape), share.reshape(-1))


def solution(mesh):
    return jax.shard_map(
        per_device,
        mesh=mesh,
        in_specs=(P("dp", "sp", None, None, None), P("dp", "sp", None, None, None), P(), P(), P()),
        out_specs=(P("dp", "sp", None, None, None), P("dp")),
        check_vma=False,
    )
```

```python
import math

import jax
import jax.numpy as jnp
from jax import lax
from jax.experimental import pallas as pl
from jax.experimental.pallas import tpu as pltpu
from jax.sharding import PartitionSpec as P

MESH = pl.DeviceIdType.MESH
BF = jnp.bfloat16
F32 = jnp.float32

STARTS = (0, 14, 29, 43)
OFFSETS = (0, 6, 4, 10)
SHARE = 118
TILES = 59
DOWN_TILE = 3456 // 8
UP_TILE = 5504 // 8


def dot(a, b):
    return jnp.dot(a, b, preferred_element_type=F32)


def dot_first(a, b):
    return lax.dot_general(a, b, (((0,), (0,)), ((), ())), preferred_element_type=F32)


def dot_last(a, b):
    return lax.dot_general(a, b, (((1,), (1,)), ((), ())), preferred_element_type=F32)


def order_matrices(order_ref, back_ref, twice_ref):
    row = lax.broadcasted_iota(jnp.int32, (128, 128), 0)
    column = lax.broadcasted_iota(jnp.int32, (128, 128), 1)

    def source(r):
        tap, b, c = r >> 4, (r >> 2) & 3, r & 3
        return ((tap >> 2) << 6) + ((2 * b + ((tap >> 1) & 1)) << 3) + 2 * c + (tap & 1)

    order_ref[...] = jnp.where(column == source(row), 1.0, 0.0).astype(BF)
    back_ref[...] = jnp.where(row == source(column), 1.0, 0.0).astype(BF)
    channel = lax.broadcasted_iota(jnp.int32, (128, 256), 0)
    place = lax.broadcasted_iota(jnp.int32, (128, 256), 1)
    twice_ref[...] = jnp.where(channel == (place >> 1), 1.0, 0.0).astype(BF)


def flip_weights(w_conv_ref, w_flip_ref):
    for t in range(27):
        block = w_conv_ref[128 * (26 - t) : 128 * (27 - t), :]
        w_flip_ref[128 * t : 128 * (t + 1), :] = block.astype(F32).T.astype(BF)


def fill_columns(columns_ref, first, planes):
    count = planes.shape[0] // 64
    lines = planes.reshape(8 * count, 8, 128)
    k_at = lax.broadcasted_iota(jnp.int32, (8 * count, 8, 128), 1)
    zero_line = jnp.zeros((count, 1, 8, 128), F32)
    for k in range(3):
        moved = lines
        if k == 0:
            moved = jnp.where(k_at == 0, 0.0, pltpu.roll(lines, 1, axis=1))
        if k == 2:
            moved = jnp.where(k_at == 7, 0.0, pltpu.roll(lines, 7, axis=1))
        moved = moved.reshape(count, 8, 8, 128)
        for j in range(3):
            shifted = moved
            if j == 0:
                shifted = jnp.concatenate([zero_line, moved[:, :7]], axis=1)
            if j == 2:
                shifted = jnp.concatenate([moved[:, 1:], zero_line], axis=1)
            lane = 128 * (3 * j + k)
            columns_ref[first : first + 64 * count, lane : lane + 128] = shifted.reshape(64 * count, 128).astype(BF)


def fill_plane(columns_ref, field_ref, plane, count=1):
    values = field_ref[plane : plane + count].reshape(256 * count, 128).astype(F32)
    fill_columns(columns_ref, 256 * plane, values)


def tap_dot(columns_ref, weights_ref, i):
    return dot(columns_ref[256 * i : 256 * i + 512, :], weights_ref[1152 * i : 1152 * (i + 1), :])


def to_blocks(order, volume):
    side_by_side = jnp.concatenate(
        [
            jnp.concatenate([volume[64 * c : 64 * c + 64], volume[64 * c + 256 : 64 * c + 320]], axis=0)
            for c in range(4)
        ],
        axis=1,
    )
    moved = dot(order, side_by_side).astype(BF)
    return [
        jnp.concatenate(
            [moved[16 * t : 16 * (t + 1), 128 * c : 128 * (c + 1)] for c in range(4)], axis=0
        )
        for t in range(8)
    ]


def from_blocks(back, blocks):
    stacked = jnp.concatenate(
        [
            jnp.concatenate(
                [blocks[16 * c : 16 * (c + 1), 128 * t : 128 * (t + 1)] for c in range(4)], axis=1
            )
            for t in range(8)
        ],
        axis=0,
    )
    moved = dot(back, stacked)
    return jnp.concatenate(
        [moved[64 * p : 64 * (p + 1), 128 * c : 128 * (c + 1)] for p in range(2) for c in range(4)], axis=0
    )


def put_rows(rows_ref, tile, values):
    count = values.shape[0] // 8
    values = values.reshape(count, 8, 128).astype(BF)
    done = 0
    while done < count:
        block, place = divmod(tile + done, TILES)
        size = min(count - done, TILES - place)
        rows_ref[block, place : place + size] = values[done : done + size]
        done += size


def logistic_parts(pre):
    s = jax.nn.sigmoid(pre)
    return pre * s, s * (1.0 + pre * (1.0 - s))


def deep_forward(hid_taps, w_down_ref):
    pre_deep = dot(jnp.concatenate(hid_taps, axis=1), w_down_ref[...])
    act, slope = logistic_parts(pre_deep)
    return act.astype(BF), slope


def up_grads(rows_ref, deep_act, up_taps):
    for t in range(8):
        put_rows(rows_ref, UP_TILE + 32 * t, dot_first(deep_act, up_taps[t]))


def deep_grads(up_taps, slope, w_up_ref):
    grad_act = dot_last(up_taps[0], w_up_ref[0:256, :])
    for t in range(1, 8):
        grad_act += dot_last(up_taps[t], w_up_ref[256 * t : 256 * (t + 1), :])
    return (grad_act * slope).astype(BF)


def down_grads(rows_ref, hid_taps, twice, grad_deep):
    odd = (lax.broadcasted_iota(jnp.int32, (256, 128), 0) & 1) == 1
    doubled = dot(jnp.concatenate(hid_taps, axis=0), twice).astype(BF)
    for t in range(8):
        both = dot_first(doubled[64 * t : 64 * (t + 1)], grad_deep)
        put_rows(rows_ref, DOWN_TILE + 32 * t, jnp.where(odd, both[:, 128:], both[:, :128]))


def pre_grads(cotangent_ref, grad_deep, w_down_ref, back, slope_ref):
    blocks = dot_last(grad_deep, w_down_ref[...]).astype(BF)
    summed = cotangent_ref[...].reshape(512, 128).astype(F32) + from_blocks(back, blocks)
    return summed * slope_ref[...]


def conv_grads(rows_ref, turned_ref, grad_pre, i):
    put_rows(rows_ref, 144 * i, dot(turned_ref[:, 256 * i : 256 * i + 512], grad_pre))


def group_wait(ref, sem):
    pltpu.make_async_copy(ref, ref, sem).wait()


def step_kernel(
    scale,
    inputs_ref, cotangent_ref, w_conv_any, w_down_any, w_up_any,
    grad_input_ref, share_ref,
    field, upstream, w_conv, w_down, w_up, w_flip, columns, turned, slope, order, back, twice, rows,
    grad_field, grad_out,
    pair_in, pair_sum, first_in, first_sum, second_in, second_sum, z_in, final,
    load_sem, own_sem, near_send, near_recv, low_recv, high_recv, halo_send, halo_low, halo_high, grad_send, grad_recv,
    pair_send, pair_recv, first_send, first_recv, second_send, second_recv, z_send, z_recv, out_send, out_recv,
):
    sp = lax.axis_index("sp")
    dp = lax.axis_index("dp")
    core = lax.rem(sp, 2)
    z_lo = lax.div(sp, 2)
    z_hi = lax.div(dp, 16)
    y = lax.rem(lax.div(dp, 4), 4)
    x = lax.rem(dp, 4)
    z = z_hi * 4 + z_lo
    turns = [core, 1 - core, core, 1 - core]
    my_first = [x + turn * (y - x) for turn in turns]
    my_second = [y + turn * (x - y) for turn in turns]

    def member(d):
        there = lax.rem(sp + d, 8)
        return there, {"sp": there, "dp": dp}

    def first_peer(q, d):
        there = lax.rem(my_first[q] + d, 4)
        return there, {"sp": sp, "dp": dp + (there - my_first[q]) * (1 + 3 * turns[q])}

    def second_peer(q, d):
        there = lax.rem(my_second[q] + d, 4)
        return there, {"sp": sp, "dp": dp + (there - my_second[q]) * (4 - 3 * turns[q])}

    barrier = pltpu.get_barrier_semaphore()

    def greet(device):
        pl.semaphore_signal(barrier, inc=1, device_id=device, device_id_type=MESH)

    def send(src, dst, send_sem, recv_sem, device):
        pltpu.make_async_remote_copy(
            src_ref=src, dst_ref=dst, send_sem=send_sem, recv_sem=recv_sem, device_id=device, device_id_type=MESH
        ).start()

    at_end = jnp.logical_or(z_lo == 0, z_lo == 3)

    def along_z(offset):
        there = lax.rem(z + offset + 16, 16)
        return {"sp": 2 * lax.rem(there, 4) + core, "dp": dp + (lax.div(there, 4) - z_hi) * 16}

    for place, offsets in enumerate(((-6, -5, -4, -3, -2, -1, 4), (-6, -2, 3), (6, 2, -3), (6, 5, 4, 3, 2, 1, -4))):
        @pl.when(z_lo == place)
        def _():
            for offset in offsets:
                greet(along_z(offset))
    for d in range(1, 8):
        greet(member(d)[1])
    for d in range(1, 4):
        greet(first_peer(0, d)[1])
        greet(second_peer(0, d)[1])

    own_crops = pl.ds(4 * core, 4)
    far_crops = pl.ds(4 * (1 - core), 4)
    sibling = {"sp": sp + 1 - 2 * core, "dp": dp}
    side = z_lo - 1 + 2 * core
    has_side = jnp.logical_and(side >= 0, side <= 3)
    loads = [
        pltpu.make_async_copy(inputs_ref.at[own_crops], field.at[1 + core], own_sem.at[0]),
        pltpu.make_async_copy(cotangent_ref.at[own_crops], upstream.at[core], own_sem.at[1]),
        pltpu.make_async_copy(w_conv_any, w_conv, load_sem.at[0]),
        pltpu.make_async_copy(w_down_any, w_down, load_sem.at[1]),
        pltpu.make_async_copy(w_up_any, w_up, load_sem.at[2]),
    ]
    for load in loads:
        load.start()

    @pl.when(z_lo == 0)
    def _():
        field[0] = jnp.zeros((4, 64, 128), BF)
        grad_field[0] = jnp.zeros((4, 64, 128), BF)

    @pl.when(z_lo == 3)
    def _():
        field[3] = jnp.zeros((4, 64, 128), BF)
        grad_field[3] = jnp.zeros((4, 64, 128), BF)

    pl.semaphore_wait(barrier, 16 + 2 * (z_lo - 1) * (z_lo - 2))

    @pl.when(core == 0)
    def _():
        @pl.when(z_lo > 0)
        def _():
            for c in range(2):
                send(inputs_ref.at[pl.ds(4 * c, 4)], field.at[3], near_send.at[1 + c], high_recv, {"sp": sp - 2 + c, "dp": dp})

    @pl.when(core == 1)
    def _():
        @pl.when(z_lo < 3)
        def _():
            for c in range(2):
                send(inputs_ref.at[pl.ds(4 * c, 4)], field.at[0], near_send.at[1 + c], low_recv, {"sp": sp + 1 + c, "dp": dp})

    send(inputs_ref.at[far_crops], field.at[1 + core], near_send.at[0], near_recv.at[0], sibling)
    send(cotangent_ref.at[far_crops], upstream.at[core], near_send.at[3], near_recv.at[1], sibling)

    def goes_low(place):
        return jnp.logical_or(place == 1, place >= 10)

    def goes_high(place):
        return jnp.logical_or(place == 2, jnp.logical_and(place >= 4, place <= 9))

    def pair_start(q):
        for xx in range(4):
            src = rows.at[pl.ds(4 * q, 4), pl.ds(STARTS[xx] + 8 * (1 - core), 8)]
            send(src, pair_in.at[q, :, xx], pair_send.at[q], pair_recv.at[q], sibling)

    def pair_finish(q):
        group_wait(pair_in.at[q], pair_recv.at[q])
        for yy in range(4):
            for xx in range(4):
                own = rows[4 * q + yy, pl.ds(STARTS[xx] + 8 * core, 8)].astype(F32)
                total = own + pair_in[q, yy, xx].astype(F32)
                pair_sum[q, xx + turns[q] * (yy - xx), yy + turns[q] * (xx - yy)] = total.astype(BF)
        for d in range(1, 4):
            there, device = first_peer(q, d)
            send(pair_sum.at[q, there], first_in.at[q, 3 - d], first_send.at[q], first_recv.at[q], device)

    def first_finish(q):
        group_wait(first_in.at[q], first_recv.at[q])
        for s in range(4):
            total = pair_sum[q, my_first[q], s].astype(F32)
            for d in range(3):
                total = total + first_in[q, d, s].astype(F32)
            first_sum[q, s] = total.astype(BF)
        for d in range(1, 4):
            there, device = second_peer(q, d)
            send(first_sum.at[q, there], second_in.at[q, 3 - d], second_send.at[q], second_recv.at[q], device)

    def second_finish(q):
        group_wait(second_in.at[q], second_recv.at[q])
        total = first_sum[q, my_second[q]].astype(F32)
        for d in range(3):
            total = total + second_in[q, d].astype(F32)
        second_sum[q] = total.astype(BF)
        place = lax.rem(z - 4 * q + 16, 16)
        there = dp + (q - z_hi) * 16

        @pl.when(goes_low(place))
        def _():
            slot = lax.rem(place + 7, 8) * lax.div(place, 10)
            send(second_sum.at[q], z_in.at[slot], z_send.at[q], z_recv, {"sp": core, "dp": there})

        @pl.when(goes_high(place))
        def _():
            slot = (place - 3) * lax.div(place + 12, 16)
            send(second_sum.at[q], z_in.at[slot], z_send.at[q], z_recv, {"sp": 6 + core, "dp": there})

    order_matrices(order, back, twice)
    loads[2].wait()
    flip_weights(w_conv, w_flip)

    loads[0].wait()
    group_wait(field.at[0], near_recv.at[0])
    fill_plane(columns, field, 1, 2)
    pre_conv = tap_dot(columns, w_conv, 1)
    turned[:, 256:768] = columns[256:768, :].T

    @pl.when(z_lo > 0)
    def _():
        group_wait(field.at[0], low_recv)

    @pl.when(z_lo < 3)
    def _():
        group_wait(field.at[3], high_recv)

    fill_plane(columns, field, 0)
    fill_plane(columns, field, 3)
    pre_conv += tap_dot(columns, w_conv, 0)
    pre_conv += tap_dot(columns, w_conv, 2)
    hidden, pre_slope = logistic_parts(pre_conv)
    slope[...] = pre_slope
    hid_taps = to_blocks(order[...], hidden.astype(BF))
    loads[3].wait()
    deep_act, deep_slope = deep_forward(hid_taps, w_down)

    loads[1].wait()
    group_wait(upstream.at[0], near_recv.at[1])
    up_taps = to_blocks(order[...], upstream[...].reshape(512, 128))
    up_grads(rows, deep_act, up_taps)
    pair_start(3)
    loads[4].wait()
    grad_deep = deep_grads(up_taps, deep_slope, w_up)
    down_grads(rows, hid_taps, twice[...], grad_deep)
    pair_start(2)
    grad_pre = pre_grads(upstream, grad_deep, w_down, back[...], slope).astype(BF)
    grad_field[1:3] = grad_pre.reshape(2, 4, 64, 128)

    @pl.when(z_lo > 0)
    def _():
        send(grad_field.at[1], grad_field.at[3], halo_send.at[0], halo_high, {"sp": sp - 2, "dp": dp})

    @pl.when(z_lo < 3)
    def _():
        send(grad_field.at[2], grad_field.at[0], halo_send.at[1], halo_low, {"sp": sp + 2, "dp": dp})

    turned[:, 0:256] = columns[0:256, :].T
    turned[:, 768:1024] = columns[768:1024, :].T
    conv_grads(rows, turned, grad_pre, 2)
    conv_grads(rows, turned, grad_pre, 1)
    pair_start(1)
    pair_finish(3)
    conv_grads(rows, turned, grad_pre, 0)
    pair_start(0)

    pair_finish(2)
    fill_plane(columns, grad_field, 1, 2)
    pair_finish(1)
    pair_finish(0)

    @pl.when(z_lo > 0)
    def _():
        group_wait(grad_field.at[0], halo_low)

    @pl.when(z_lo < 3)
    def _():
        group_wait(grad_field.at[3], halo_high)

    fill_plane(columns, grad_field, 0)
    fill_plane(columns, grad_field, 3)
    total = tap_dot(columns, w_flip, 0)
    total += tap_dot(columns, w_flip, 1)
    total += tap_dot(columns, w_flip, 2)
    grad_out[...] = total.astype(BF).reshape(2, 4, 64, 128)
    for q in (3, 2, 1, 0):
        first_finish(q)
    send(grad_out.at[1 - core], grad_input_ref.at[own_crops], grad_send, grad_recv, sibling)
    own_grad = pltpu.make_async_copy(grad_out.at[core], grad_input_ref.at[own_crops], own_sem.at[2])
    own_grad.start()
    for q in (3, 2, 1, 0):
        second_finish(q)

    @pl.when(at_end)
    def _():
        group_wait(z_in, z_recv)
        total = second_sum[z_hi].astype(F32)
        for d in range(7):
            total = total + z_in[d].astype(F32)
        end = lax.div(z_lo, 3)
        final[end, core] = total.astype(BF)
        for d in range(1, 8):
            send(final.at[end, core], final.at[end, core], out_send, out_recv, member(d)[1])
        group_wait(z_in.at[pl.ds(0, 3)], out_recv)

    @pl.when(jnp.logical_not(at_end))
    def _():
        group_wait(z_in.at[pl.ds(0, 4)], out_recv)

    whole = (final[0].astype(F32) + final[1].astype(F32)).reshape(128, 128) * scale
    for xx in range(4):
        @pl.when(x == xx)
        def _():
            share_ref[...] = whole[OFFSETS[xx] : OFFSETS[xx] + SHARE]

    own_grad.wait()
    group_wait(grad_out.at[0], grad_recv)
    group_wait(grad_out.at[0], grad_send)
    group_wait(field.at[0], near_send.at[0])
    group_wait(field.at[0], near_send.at[3])

    @pl.when(has_side)
    def _():
        group_wait(field.at[0], near_send.at[1])
        group_wait(field.at[0], near_send.at[2])

    @pl.when(z_lo > 0)
    def _():
        group_wait(grad_field.at[0], halo_send.at[0])

    @pl.when(z_lo < 3)
    def _():
        group_wait(grad_field.at[0], halo_send.at[1])

    for q in (3, 2, 1, 0):
        group_wait(pair_in.at[q], pair_send.at[q])
        group_wait(first_in.at[q], first_send.at[q])
        group_wait(second_in.at[q], second_send.at[q])
        place = lax.rem(z - 4 * q + 16, 16)

        @pl.when(jnp.logical_or(goes_low(place), goes_high(place)))
        def _():
            group_wait(z_in.at[0], z_send.at[q])

    @pl.when(at_end)
    def _():
        group_wait(z_in, out_send)


def store_kernel(grad_input_ref, share_ref, grad_input_out, share_out, sem):
    copies = [
        pltpu.make_async_copy(grad_input_ref, grad_input_out, sem.at[0]),
        pltpu.make_async_copy(share_ref, share_out, sem.at[1]),
    ]
    for copy in copies:
        copy.start()
    for copy in copies:
        copy.wait()


def per_device(inputs, cotangent, w_conv, w_down, w_up):
    edge = inputs.shape[2]
    crops = inputs.shape[0] * lax.axis_size("dp")
    scale = 1.0 / math.sqrt(crops * edge * edge * edge)

    def kernel(*refs):
        step_kernel(scale, *refs)

    dma = pltpu.SemaphoreType.DMA
    vmem = pltpu.VMEM
    grad_input, share = pl.pallas_call(
        kernel,
        out_shape=(
            jax.ShapeDtypeStruct((8, 64, 128), BF),
            jax.ShapeDtypeStruct((SHARE, 128), F32),
        ),
        in_specs=[pl.BlockSpec(memory_space=pl.ANY)] * 5,
        out_specs=(pl.BlockSpec(memory_space=vmem), pl.BlockSpec(memory_space=vmem)),
        scratch_shapes=[
            vmem((4, 4, 64, 128), BF),
            vmem((2, 4, 64, 128), BF),
            vmem((3456, 128), BF),
            vmem((1024, 256), BF),
            vmem((2048, 128), BF),
            vmem((3456, 128), BF),
            vmem((1024, 1152), BF),
            vmem((1152, 1024), BF),
            vmem((512, 128), F32),
            vmem((128, 128), BF),
            vmem((128, 128), BF),
            vmem((128, 256), BF),
            vmem((16, TILES, 8, 128), BF),
            vmem((4, 4, 64, 128), BF),
            vmem((2, 4, 64, 128), BF),
            vmem((4, 4, 4, 8, 8, 128), BF),
            vmem((4, 4, 4, 8, 8, 128), BF),
            vmem((4, 3, 4, 8, 8, 128), BF),
            vmem((4, 4, 8, 8, 128), BF),
            vmem((4, 3, 8, 8, 128), BF),
            vmem((4, 8, 8, 128), BF),
            vmem((7, 8, 8, 128), BF),
            vmem((2, 2, 8, 8, 128), BF),
            dma((3,)), dma((3,)), dma((4,)), dma((2,)), dma, dma, dma((2,)), dma, dma, dma, dma,
            dma((4,)), dma((4,)), dma((4,)), dma((4,)), dma((4,)), dma((4,)), dma((4,)), dma, dma, dma,
        ],
        compiler_params=pltpu.CompilerParams(
            collective_id=0, has_side_effects=True, vmem_limit_bytes=55040 * 1024
        ),
        name="whole_step",
    )(inputs.reshape(8, 64, 128), cotangent.reshape(8, 64, 128), w_conv, w_down, w_up)
    grad_input, share = pl.pallas_call(
        store_kernel,
        out_shape=(
            jax.ShapeDtypeStruct((8, 64, 128), BF),
            jax.ShapeDtypeStruct((SHARE, 128), F32),
        ),
        in_specs=[pl.BlockSpec(memory_space=pl.ANY)] * 2,
        out_specs=(pl.BlockSpec(memory_space=pl.ANY),) * 2,
        scratch_shapes=[dma((2,))],
        compiler_params=pltpu.CompilerParams(vmem_limit_bytes=1024 * 1024),
        name="store",
    )(grad_input, share)
    return (grad_input.reshape(inputs.shape), share.reshape(-1))


def solution(mesh):
    return jax.shard_map(
        per_device,
        mesh=mesh,
        in_specs=(P("dp", "sp", None, None, None), P("dp", "sp", None, None, None), P(), P(), P()),
        out_specs=(P("dp", "sp", None, None, None), P("dp")),
        check_vma=False,
    )
```

```python
import math

import jax
import jax.numpy as jnp
from jax import lax
from jax.experimental import pallas as pl
from jax.experimental.pallas import tpu as pltpu
from jax.sharding import PartitionSpec as P

MESH = pl.DeviceIdType.MESH
BF = jnp.bfloat16
F32 = jnp.float32

STARTS = (0, 14, 29, 43)
OFFSETS = (0, 6, 4, 10)
SHARE = 118
TILES = 59
DOWN_TILE = 3456 // 8
UP_TILE = 5504 // 8


def dot(a, b):
    return jnp.dot(a, b, preferred_element_type=F32)


def dot_first(a, b):
    return lax.dot_general(a, b, (((0,), (0,)), ((), ())), preferred_element_type=F32)


def dot_last(a, b):
    return lax.dot_general(a, b, (((1,), (1,)), ((), ())), preferred_element_type=F32)


def order_matrices(order_ref, back_ref, twice_ref):
    row = lax.broadcasted_iota(jnp.int32, (128, 128), 0)
    column = lax.broadcasted_iota(jnp.int32, (128, 128), 1)

    def source(r):
        tap, b, c = r >> 4, (r >> 2) & 3, r & 3
        return ((tap >> 2) << 6) + ((2 * b + ((tap >> 1) & 1)) << 3) + 2 * c + (tap & 1)

    order_ref[...] = jnp.where(column == source(row), 1.0, 0.0).astype(BF)
    back_ref[...] = jnp.where(row == source(column), 1.0, 0.0).astype(BF)
    channel = lax.broadcasted_iota(jnp.int32, (128, 256), 0)
    place = lax.broadcasted_iota(jnp.int32, (128, 256), 1)
    twice_ref[...] = jnp.where(channel == (place >> 1), 1.0, 0.0).astype(BF)


def flip_weights(w_conv_ref, w_flip_ref):
    for t in range(27):
        block = w_conv_ref[128 * (26 - t) : 128 * (27 - t), :]
        w_flip_ref[128 * t : 128 * (t + 1), :] = block.astype(F32).T.astype(BF)


def fill_columns(columns_ref, first, planes):
    count = planes.shape[0] // 64
    lines = planes.reshape(8 * count, 8, 128)
    k_at = lax.broadcasted_iota(jnp.int32, (8 * count, 8, 128), 1)
    zero_line = jnp.zeros((count, 1, 8, 128), F32)
    for k in range(3):
        moved = lines
        if k == 0:
            moved = jnp.where(k_at == 0, 0.0, pltpu.roll(lines, 1, axis=1))
        if k == 2:
            moved = jnp.where(k_at == 7, 0.0, pltpu.roll(lines, 7, axis=1))
        moved = moved.reshape(count, 8, 8, 128)
        for j in range(3):
            shifted = moved
            if j == 0:
                shifted = jnp.concatenate([zero_line, moved[:, :7]], axis=1)
            if j == 2:
                shifted = jnp.concatenate([moved[:, 1:], zero_line], axis=1)
            lane = 128 * (3 * j + k)
            columns_ref[first : first + 64 * count, lane : lane + 128] = shifted.reshape(64 * count, 128).astype(BF)


def fill_plane(columns_ref, field_ref, plane, count=1):
    values = field_ref[plane : plane + count].reshape(256 * count, 128).astype(F32)
    fill_columns(columns_ref, 256 * plane, values)


def tap_dot(columns_ref, weights_ref, i):
    return dot(columns_ref[256 * i : 256 * i + 512, :], weights_ref[1152 * i : 1152 * (i + 1), :])


def to_blocks(order, volume):
    side_by_side = jnp.concatenate(
        [
            jnp.concatenate([volume[64 * c : 64 * c + 64], volume[64 * c + 256 : 64 * c + 320]], axis=0)
            for c in range(4)
        ],
        axis=1,
    )
    moved = dot(order, side_by_side).astype(BF)
    return [
        jnp.concatenate(
            [moved[16 * t : 16 * (t + 1), 128 * c : 128 * (c + 1)] for c in range(4)], axis=0
        )
        for t in range(8)
    ]


def from_blocks(back, blocks):
    stacked = jnp.concatenate(
        [
            jnp.concatenate(
                [blocks[16 * c : 16 * (c + 1), 128 * t : 128 * (t + 1)] for c in range(4)], axis=1
            )
            for t in range(8)
        ],
        axis=0,
    )
    moved = dot(back, stacked)
    return jnp.concatenate(
        [moved[64 * p : 64 * (p + 1), 128 * c : 128 * (c + 1)] for p in range(2) for c in range(4)], axis=0
    )


def put_rows(rows_ref, tile, values):
    count = values.shape[0] // 8
    values = values.reshape(count, 8, 128).astype(BF)
    done = 0
    while done < count:
        block, place = divmod(tile + done, TILES)
        size = min(count - done, TILES - place)
        rows_ref[block, place : place + size] = values[done : done + size]
        done += size


def logistic_parts(pre):
    s = jax.nn.sigmoid(pre)
    return pre * s, s * (1.0 + pre * (1.0 - s))


def deep_forward(hid_taps, w_down_ref):
    pre_deep = dot(jnp.concatenate(hid_taps, axis=1), w_down_ref[...])
    act, slope = logistic_parts(pre_deep)
    return act.astype(BF), slope


def up_grads(rows_ref, deep_act, up_taps):
    for t in range(8):
        put_rows(rows_ref, UP_TILE + 32 * t, dot_first(deep_act, up_taps[t]))


def deep_grads(up_taps, slope, w_up_ref):
    grad_act = dot_last(up_taps[0], w_up_ref[0:256, :])
    for t in range(1, 8):
        grad_act += dot_last(up_taps[t], w_up_ref[256 * t : 256 * (t + 1), :])
    return (grad_act * slope).astype(BF)


def down_grads(rows_ref, hid_taps, twice, grad_deep):
    odd = (lax.broadcasted_iota(jnp.int32, (256, 128), 0) & 1) == 1
    doubled = dot(jnp.concatenate(hid_taps, axis=0), twice).astype(BF)
    for t in range(8):
        both = dot_first(doubled[64 * t : 64 * (t + 1)], grad_deep)
        put_rows(rows_ref, DOWN_TILE + 32 * t, jnp.where(odd, both[:, 128:], both[:, :128]))


def pre_grads(cotangent_ref, grad_deep, w_down_ref, back, slope_ref):
    blocks = dot_last(grad_deep, w_down_ref[...]).astype(BF)
    summed = cotangent_ref[...].reshape(512, 128).astype(F32) + from_blocks(back, blocks)
    return summed * slope_ref[...]


def conv_grads(rows_ref, turned_ref, grad_pre, i):
    put_rows(rows_ref, 144 * i, dot(turned_ref[:, 256 * i : 256 * i + 512], grad_pre))


def group_wait(ref, sem):
    pltpu.make_async_copy(ref, ref, sem).wait()


def remote(src, dst, send_sem, recv_sem, device):
    pltpu.make_async_remote_copy(
        src_ref=src, dst_ref=dst, send_sem=send_sem, recv_sem=recv_sem, device_id=device, device_id_type=MESH
    ).start()


def planes_kernel(
    inputs_ref, cotangent_ref, w_conv_any, field, upstream, w_conv,
    load_sem, near_send, near_recv, low_recv, high_recv,
):
    sp = lax.axis_index("sp")
    dp = lax.axis_index("dp")
    core = lax.rem(sp, 2)
    z_lo = lax.div(sp, 2)
    below = lax.div(z_lo + 3, 4)
    above = 1 - lax.div(z_lo, 3)
    sibling = {"sp": sp + 1 - 2 * core, "dp": dp}
    barrier = pltpu.get_barrier_semaphore()

    def greet(there):
        pl.semaphore_signal(barrier, inc=1, device_id={"sp": there, "dp": dp}, device_id_type=MESH)

    @pl.when(z_lo > 0)
    def _():
        greet(2 * z_lo - 1)

        @pl.when(core == 0)
        def _():
            greet(sp - 2)

    @pl.when(z_lo < 3)
    def _():
        greet(2 * z_lo + 2)

        @pl.when(core == 1)
        def _():
            greet(sp + 2)

    greet(sp + 1 - 2 * core)
    own_crops = pl.ds(4 * core, 4)
    far_crops = pl.ds(4 * (1 - core), 4)
    loads = [
        pltpu.make_async_copy(inputs_ref.at[own_crops], field.at[1 + core], load_sem.at[0]),
        pltpu.make_async_copy(cotangent_ref.at[own_crops], upstream.at[core], load_sem.at[1]),
        pltpu.make_async_copy(w_conv_any, w_conv, load_sem.at[2]),
    ]
    for load in loads:
        load.start()
    pl.semaphore_wait(barrier, 1 + below * (2 - core) + above * (1 + core))

    @pl.when(core == 0)
    def _():
        @pl.when(z_lo > 0)
        def _():
            for c in range(2):
                remote(inputs_ref.at[pl.ds(4 * c, 4)], field.at[3], near_send.at[1 + c], high_recv, {"sp": sp - 2 + c, "dp": dp})

    @pl.when(core == 1)
    def _():
        @pl.when(z_lo < 3)
        def _():
            for c in range(2):
                remote(inputs_ref.at[pl.ds(4 * c, 4)], field.at[0], near_send.at[1 + c], low_recv, {"sp": sp + 1 + c, "dp": dp})

    remote(inputs_ref.at[far_crops], field.at[1 + core], near_send.at[0], near_recv.at[0], sibling)
    remote(cotangent_ref.at[far_crops], upstream.at[core], near_send.at[3], near_recv.at[1], sibling)

    @pl.when(z_lo == 0)
    def _():
        field[0] = jnp.zeros((4, 64, 128), BF)

    @pl.when(z_lo == 3)
    def _():
        field[3] = jnp.zeros((4, 64, 128), BF)

    for load in loads:
        load.wait()
    group_wait(field.at[0], near_recv.at[0])
    group_wait(field.at[0], near_recv.at[1])
    group_wait(field.at[0], near_send.at[0])
    group_wait(field.at[0], near_send.at[3])
    side = z_lo - 1 + 2 * core

    @pl.when(jnp.logical_and(side >= 0, side <= 3))
    def _():
        group_wait(field.at[0], near_send.at[1])
        group_wait(field.at[0], near_send.at[2])

    @pl.when(z_lo > 0)
    def _():
        group_wait(field.at[0], low_recv)

    @pl.when(z_lo < 3)
    def _():
        group_wait(field.at[3], high_recv)


def step_kernel(
    scale,
    field, upstream, w_conv, w_down, w_up,
    grad_input_ref, share_ref,
    w_flip, columns, turned, slope, order, back, twice, rows,
    grad_field, grad_out,
    pair_in, pair_sum, first_in, first_sum, second_in, second_sum, z_in, final,
    own_sem, halo_send, halo_low, halo_high, grad_send, grad_recv,
    pair_send, pair_recv, first_send, first_recv, second_send, second_recv, z_send, z_recv, out_send, out_recv,
):
    sp = lax.axis_index("sp")
    dp = lax.axis_index("dp")
    core = lax.rem(sp, 2)
    z_lo = lax.div(sp, 2)
    z_hi = lax.div(dp, 16)
    y = lax.rem(lax.div(dp, 4), 4)
    x = lax.rem(dp, 4)
    z = z_hi * 4 + z_lo
    turns = [core, 1 - core, core, 1 - core]
    my_first = [x + turn * (y - x) for turn in turns]
    my_second = [y + turn * (x - y) for turn in turns]

    def member(d):
        there = lax.rem(sp + d, 8)
        return there, {"sp": there, "dp": dp}

    def first_peer(q, d):
        there = lax.rem(my_first[q] + d, 4)
        return there, {"sp": sp, "dp": dp + (there - my_first[q]) * (1 + 3 * turns[q])}

    def second_peer(q, d):
        there = lax.rem(my_second[q] + d, 4)
        return there, {"sp": sp, "dp": dp + (there - my_second[q]) * (4 - 3 * turns[q])}

    barrier = pltpu.get_barrier_semaphore()

    def greet(device):
        pl.semaphore_signal(barrier, inc=1, device_id=device, device_id_type=MESH)

    at_end = jnp.logical_or(z_lo == 0, z_lo == 3)

    def along_z(offset):
        there = lax.rem(z + offset + 16, 16)
        return {"sp": 2 * lax.rem(there, 4) + core, "dp": dp + (lax.div(there, 4) - z_hi) * 16}

    for place, offsets in enumerate(((-6, -5, -4, -3, -2, -1, 4), (-6, -2, 3), (6, 2, -3), (6, 5, 4, 3, 2, 1, -4))):
        @pl.when(z_lo == place)
        def _():
            for offset in offsets:
                greet(along_z(offset))
    for d in range(1, 8):
        greet(member(d)[1])
    for d in range(1, 4):
        greet(first_peer(0, d)[1])
        greet(second_peer(0, d)[1])

    own_crops = pl.ds(4 * core, 4)
    sibling = {"sp": sp + 1 - 2 * core, "dp": dp}
    def goes_low(place):
        return jnp.logical_or(place == 1, place >= 10)

    def goes_high(place):
        return jnp.logical_or(place == 2, jnp.logical_and(place >= 4, place <= 9))

    def pair_start(q):
        for xx in range(4):
            src = rows.at[pl.ds(4 * q, 4), pl.ds(STARTS[xx] + 8 * (1 - core), 8)]
            remote(src, pair_in.at[q, :, xx], pair_send.at[q], pair_recv.at[q], sibling)

    def pair_finish(q):
        group_wait(pair_in.at[q], pair_recv.at[q])
        for yy in range(4):
            for xx in range(4):
                own = rows[4 * q + yy, pl.ds(STARTS[xx] + 8 * core, 8)].astype(F32)
                total = own + pair_in[q, yy, xx].astype(F32)
                pair_sum[q, xx + turns[q] * (yy - xx), yy + turns[q] * (xx - yy)] = total.astype(BF)
        for d in range(1, 4):
            there, device = first_peer(q, d)
            remote(pair_sum.at[q, there], first_in.at[q, 3 - d], first_send.at[q], first_recv.at[q], device)

    def first_finish(q):
        group_wait(first_in.at[q], first_recv.at[q])
        for s in range(4):
            total = pair_sum[q, my_first[q], s].astype(F32)
            for d in range(3):
                total = total + first_in[q, d, s].astype(F32)
            first_sum[q, s] = total.astype(BF)
        for d in range(1, 4):
            there, device = second_peer(q, d)
            remote(first_sum.at[q, there], second_in.at[q, 3 - d], second_send.at[q], second_recv.at[q], device)

    def second_finish(q):
        group_wait(second_in.at[q], second_recv.at[q])
        total = first_sum[q, my_second[q]].astype(F32)
        for d in range(3):
            total = total + second_in[q, d].astype(F32)
        second_sum[q] = total.astype(BF)
        place = lax.rem(z - 4 * q + 16, 16)
        there = dp + (q - z_hi) * 16

        @pl.when(goes_low(place))
        def _():
            slot = lax.rem(place + 7, 8) * lax.div(place, 10)
            remote(second_sum.at[q], z_in.at[slot], z_send.at[q], z_recv, {"sp": core, "dp": there})

        @pl.when(goes_high(place))
        def _():
            slot = (place - 3) * lax.div(place + 12, 16)
            remote(second_sum.at[q], z_in.at[slot], z_send.at[q], z_recv, {"sp": 6 + core, "dp": there})

    @pl.when(z_lo == 0)
    def _():
        grad_field[0] = jnp.zeros((4, 64, 128), BF)

    @pl.when(z_lo == 3)
    def _():
        grad_field[3] = jnp.zeros((4, 64, 128), BF)

    order_matrices(order, back, twice)
    fill_plane(columns, field, 0, 4)
    pre_conv = tap_dot(columns, w_conv, 0)
    pre_conv += tap_dot(columns, w_conv, 1)
    pre_conv += tap_dot(columns, w_conv, 2)
    hidden, pre_slope = logistic_parts(pre_conv)
    slope[...] = pre_slope
    hid_taps = to_blocks(order[...], hidden.astype(BF))
    deep_act, deep_slope = deep_forward(hid_taps, w_down)
    turned[...] = columns[...].T
    up_taps = to_blocks(order[...], upstream[...].reshape(512, 128))
    grad_deep = deep_grads(up_taps, deep_slope, w_up)
    up_grads(rows, deep_act, up_taps)
    grad_pre = pre_grads(upstream, grad_deep, w_down, back[...], slope).astype(BF)
    grad_field[1:3] = grad_pre.reshape(2, 4, 64, 128)
    down_grads(rows, hid_taps, twice[...], grad_deep)
    for i in (2, 1, 0):
        conv_grads(rows, turned, grad_pre, i)
    flip_weights(w_conv, w_flip)

    pl.semaphore_wait(barrier, 16 + 2 * (z_lo - 1) * (z_lo - 2))
    for q in (3, 2, 1, 0):
        pair_start(q)

    @pl.when(z_lo > 0)
    def _():
        remote(grad_field.at[1], grad_field.at[3], halo_send.at[0], halo_high, {"sp": sp - 2, "dp": dp})

    @pl.when(z_lo < 3)
    def _():
        remote(grad_field.at[2], grad_field.at[0], halo_send.at[1], halo_low, {"sp": sp + 2, "dp": dp})

    for q in (3, 2, 1, 0):
        pair_finish(q)
    fill_plane(columns, grad_field, 1, 2)

    @pl.when(z_lo > 0)
    def _():
        group_wait(grad_field.at[0], halo_low)

    @pl.when(z_lo < 3)
    def _():
        group_wait(grad_field.at[3], halo_high)

    fill_plane(columns, grad_field, 0)
    fill_plane(columns, grad_field, 3)
    total = tap_dot(columns, w_flip, 0)
    total += tap_dot(columns, w_flip, 1)
    total += tap_dot(columns, w_flip, 2)
    grad_out[...] = total.astype(BF).reshape(2, 4, 64, 128)
    for q in (3, 2, 1, 0):
        first_finish(q)
    remote(grad_out.at[1 - core], grad_input_ref.at[own_crops], grad_send, grad_recv, sibling)
    own_grad = pltpu.make_async_copy(grad_out.at[core], grad_input_ref.at[own_crops], own_sem)
    own_grad.start()
    for q in (3, 2, 1, 0):
        second_finish(q)

    @pl.when(at_end)
    def _():
        group_wait(z_in, z_recv)
        total = second_sum[z_hi].astype(F32)
        for d in range(7):
            total = total + z_in[d].astype(F32)
        end = lax.div(z_lo, 3)
        final[end, core] = total.astype(BF)
        for d in range(1, 8):
            remote(final.at[end, core], final.at[end, core], out_send, out_recv, member(d)[1])
        group_wait(z_in.at[pl.ds(0, 3)], out_recv)

    @pl.when(jnp.logical_not(at_end))
    def _():
        group_wait(z_in.at[pl.ds(0, 4)], out_recv)

    whole = (final[0].astype(F32) + final[1].astype(F32)).reshape(128, 128) * scale
    for xx in range(4):
        @pl.when(x == xx)
        def _():
            share_ref[...] = whole[OFFSETS[xx] : OFFSETS[xx] + SHARE]

    own_grad.wait()
    group_wait(grad_out.at[0], grad_recv)
    group_wait(grad_out.at[0], grad_send)
    @pl.when(z_lo > 0)
    def _():
        group_wait(grad_field.at[0], halo_send.at[0])

    @pl.when(z_lo < 3)
    def _():
        group_wait(grad_field.at[0], halo_send.at[1])

    for q in (3, 2, 1, 0):
        group_wait(pair_in.at[q], pair_send.at[q])
        group_wait(first_in.at[q], first_send.at[q])
        group_wait(second_in.at[q], second_send.at[q])
        place = lax.rem(z - 4 * q + 16, 16)

        @pl.when(jnp.logical_or(goes_low(place), goes_high(place)))
        def _():
            group_wait(z_in.at[0], z_send.at[q])

    @pl.when(at_end)
    def _():
        group_wait(z_in, out_send)


def store_kernel(grad_input_ref, share_ref, grad_input_out, share_out, sem):
    copies = [
        pltpu.make_async_copy(grad_input_ref, grad_input_out, sem.at[0]),
        pltpu.make_async_copy(share_ref, share_out, sem.at[1]),
    ]
    for copy in copies:
        copy.start()
    for copy in copies:
        copy.wait()


def per_device(inputs, cotangent, w_conv, w_down, w_up):
    edge = inputs.shape[2]
    crops = inputs.shape[0] * lax.axis_size("dp")
    scale = 1.0 / math.sqrt(crops * edge * edge * edge)

    def kernel(*refs):
        step_kernel(scale, *refs)

    dma = pltpu.SemaphoreType.DMA
    vmem = pltpu.VMEM
    field, upstream, w_conv = pl.pallas_call(
        planes_kernel,
        out_shape=(
            jax.ShapeDtypeStruct((4, 4, 64, 128), BF),
            jax.ShapeDtypeStruct((2, 4, 64, 128), BF),
            jax.ShapeDtypeStruct((3456, 128), BF),
        ),
        in_specs=[pl.BlockSpec(memory_space=pl.ANY)] * 3,
        out_specs=(pl.BlockSpec(memory_space=vmem),) * 3,
        scratch_shapes=[dma((3,)), dma((4,)), dma((2,)), dma, dma],
        compiler_params=pltpu.CompilerParams(
            collective_id=0, has_side_effects=True, vmem_limit_bytes=16 * 1024 * 1024
        ),
        name="planes",
    )(
        pltpu.with_memory_space_constraint(inputs.reshape(8, 64, 128), pltpu.HBM),
        pltpu.with_memory_space_constraint(cotangent.reshape(8, 64, 128), pltpu.HBM),
        pltpu.with_memory_space_constraint(w_conv, pltpu.HBM),
    )
    grad_input, share = pl.pallas_call(
        kernel,
        out_shape=(
            jax.ShapeDtypeStruct((8, 64, 128), BF),
            jax.ShapeDtypeStruct((SHARE, 128), F32),
        ),
        in_specs=[pl.BlockSpec(memory_space=vmem)] * 5,
        out_specs=(pl.BlockSpec(memory_space=vmem), pl.BlockSpec(memory_space=vmem)),
        scratch_shapes=[
            vmem((3456, 128), BF),
            vmem((1024, 1152), BF),
            vmem((1152, 1024), BF),
            vmem((512, 128), F32),
            vmem((128, 128), BF),
            vmem((128, 128), BF),
            vmem((128, 256), BF),
            vmem((16, TILES, 8, 128), BF),
            vmem((4, 4, 64, 128), BF),
            vmem((2, 4, 64, 128), BF),
            vmem((4, 4, 4, 8, 8, 128), BF),
            vmem((4, 4, 4, 8, 8, 128), BF),
            vmem((4, 3, 4, 8, 8, 128), BF),
            vmem((4, 4, 8, 8, 128), BF),
            vmem((4, 3, 8, 8, 128), BF),
            vmem((4, 8, 8, 128), BF),
            vmem((7, 8, 8, 128), BF),
            vmem((2, 2, 8, 8, 128), BF),
            dma, dma((2,)), dma, dma, dma, dma,
            dma((4,)), dma((4,)), dma((4,)), dma((4,)), dma((4,)), dma((4,)), dma((4,)), dma, dma, dma,
        ],
        compiler_params=pltpu.CompilerParams(
            collective_id=1, has_side_effects=True, vmem_limit_bytes=48 * 1024 * 1024
        ),
        name="whole_step",
    )(field, upstream, w_conv, w_down, w_up)
    grad_input, share = pl.pallas_call(
        store_kernel,
        out_shape=(
            jax.ShapeDtypeStruct((8, 64, 128), BF),
            jax.ShapeDtypeStruct((SHARE, 128), F32),
        ),
        in_specs=[pl.BlockSpec(memory_space=pl.ANY)] * 2,
        out_specs=(pl.BlockSpec(memory_space=pl.ANY),) * 2,
        scratch_shapes=[dma((2,))],
        compiler_params=pltpu.CompilerParams(vmem_limit_bytes=1024 * 1024),
        name="store",
    )(grad_input, share)
    return (grad_input.reshape(inputs.shape), share.reshape(-1))


def solution(mesh):
    return jax.shard_map(
        per_device,
        mesh=mesh,
        in_specs=(P("dp", "sp", None, None, None), P("dp", "sp", None, None, None), P(), P(), P()),
        out_specs=(P("dp", "sp", None, None, None), P("dp")),
        check_vma=False,
    )
```

```python
import math

import jax
import jax.numpy as jnp
from jax import lax
from jax.experimental import pallas as pl
from jax.experimental.pallas import tpu as pltpu
from jax.sharding import PartitionSpec as P

MESH = pl.DeviceIdType.MESH
BF = jnp.bfloat16
F32 = jnp.float32

STARTS = (0, 14, 29, 43)
OFFSETS = (0, 6, 4, 10)
SHARE = 118
TILES = 59
DOWN_TILE = 3456 // 8
UP_TILE = 5504 // 8


def dot(a, b):
    return jnp.dot(a, b, preferred_element_type=F32)


def dot_first(a, b):
    return lax.dot_general(a, b, (((0,), (0,)), ((), ())), preferred_element_type=F32)


def dot_last(a, b):
    return lax.dot_general(a, b, (((1,), (1,)), ((), ())), preferred_element_type=F32)


def order_matrices(order_ref, back_ref, twice_ref):
    row = lax.broadcasted_iota(jnp.int32, (128, 128), 0)
    column = lax.broadcasted_iota(jnp.int32, (128, 128), 1)

    def source(r):
        tap, b, c = r >> 4, (r >> 2) & 3, r & 3
        return ((tap >> 2) << 6) + ((2 * b + ((tap >> 1) & 1)) << 3) + 2 * c + (tap & 1)

    order_ref[...] = jnp.where(column == source(row), 1.0, 0.0).astype(BF)
    back_ref[...] = jnp.where(row == source(column), 1.0, 0.0).astype(BF)
    channel = lax.broadcasted_iota(jnp.int32, (128, 256), 0)
    place = lax.broadcasted_iota(jnp.int32, (128, 256), 1)
    twice_ref[...] = jnp.where(channel == (place >> 1), 1.0, 0.0).astype(BF)


def flip_weights(w_conv_ref, w_flip_ref):
    for t in range(27):
        block = w_conv_ref[128 * (26 - t) : 128 * (27 - t), :]
        w_flip_ref[128 * t : 128 * (t + 1), :] = block.astype(F32).T.astype(BF)


def fill_columns(columns_ref, first, planes):
    count = planes.shape[0] // 64
    lines = planes.reshape(8 * count, 8, 128)
    k_at = lax.broadcasted_iota(jnp.int32, (8 * count, 8, 128), 1)
    zero_line = jnp.zeros((count, 1, 8, 128), F32)
    for k in range(3):
        moved = lines
        if k == 0:
            moved = jnp.where(k_at == 0, 0.0, pltpu.roll(lines, 1, axis=1))
        if k == 2:
            moved = jnp.where(k_at == 7, 0.0, pltpu.roll(lines, 7, axis=1))
        moved = moved.reshape(count, 8, 8, 128)
        for j in range(3):
            shifted = moved
            if j == 0:
                shifted = jnp.concatenate([zero_line, moved[:, :7]], axis=1)
            if j == 2:
                shifted = jnp.concatenate([moved[:, 1:], zero_line], axis=1)
            lane = 128 * (3 * j + k)
            columns_ref[first : first + 64 * count, lane : lane + 128] = shifted.reshape(64 * count, 128).astype(BF)


def fill_plane(columns_ref, field_ref, plane, count=1):
    values = field_ref[plane : plane + count].reshape(256 * count, 128).astype(F32)
    fill_columns(columns_ref, 256 * plane, values)


def tap_dot(columns_ref, weights_ref, i):
    return dot(columns_ref[256 * i : 256 * i + 512, :], weights_ref[1152 * i : 1152 * (i + 1), :])


def to_blocks(order, volume):
    side_by_side = jnp.concatenate(
        [
            jnp.concatenate([volume[64 * c : 64 * c + 64], volume[64 * c + 256 : 64 * c + 320]], axis=0)
            for c in range(4)
        ],
        axis=1,
    )
    moved = dot(order, side_by_side).astype(BF)
    return [
        jnp.concatenate(
            [moved[16 * t : 16 * (t + 1), 128 * c : 128 * (c + 1)] for c in range(4)], axis=0
        )
        for t in range(8)
    ]


def from_blocks(back, blocks):
    stacked = jnp.concatenate(
        [
            jnp.concatenate(
                [blocks[16 * c : 16 * (c + 1), 128 * t : 128 * (t + 1)] for c in range(4)], axis=1
            )
            for t in range(8)
        ],
        axis=0,
    )
    moved = dot(back, stacked)
    return jnp.concatenate(
        [moved[64 * p : 64 * (p + 1), 128 * c : 128 * (c + 1)] for p in range(2) for c in range(4)], axis=0
    )


def put_rows(rows_ref, tile, values):
    count = values.shape[0] // 8
    values = values.reshape(count, 8, 128).astype(BF)
    done = 0
    while done < count:
        block, place = divmod(tile + done, TILES)
        size = min(count - done, TILES - place)
        rows_ref[block, place : place + size] = values[done : done + size]
        done += size


def logistic_parts(pre):
    s = jax.nn.sigmoid(pre)
    return pre * s, s * (1.0 + pre * (1.0 - s))


def deep_forward(hid_taps, w_down_ref):
    pre_deep = dot(jnp.concatenate(hid_taps, axis=1), w_down_ref[...])
    act, slope = logistic_parts(pre_deep)
    return act.astype(BF), slope


def up_grads(rows_ref, deep_act, up_taps):
    for t in range(8):
        put_rows(rows_ref, UP_TILE + 32 * t, dot_first(deep_act, up_taps[t]))


def deep_grads(up_taps, slope, w_up_ref):
    grad_act = dot_last(up_taps[0], w_up_ref[0:256, :])
    for t in range(1, 8):
        grad_act += dot_last(up_taps[t], w_up_ref[256 * t : 256 * (t + 1), :])
    return (grad_act * slope).astype(BF)


def down_grads(rows_ref, hid_taps, twice, grad_deep):
    odd = (lax.broadcasted_iota(jnp.int32, (256, 128), 0) & 1) == 1
    doubled = dot(jnp.concatenate(hid_taps, axis=0), twice).astype(BF)
    for t in range(8):
        both = dot_first(doubled[64 * t : 64 * (t + 1)], grad_deep)
        put_rows(rows_ref, DOWN_TILE + 32 * t, jnp.where(odd, both[:, 128:], both[:, :128]))


def pre_grads(cotangent_ref, grad_deep, w_down_ref, back, slope_ref):
    blocks = dot_last(grad_deep, w_down_ref[...]).astype(BF)
    summed = cotangent_ref[...].reshape(512, 128).astype(F32) + from_blocks(back, blocks)
    return summed * slope_ref[...]


def conv_grads(rows_ref, turned_ref, grad_pre, i):
    put_rows(rows_ref, 144 * i, dot(turned_ref[:, 256 * i : 256 * i + 512], grad_pre))


def group_wait(ref, sem):
    pltpu.make_async_copy(ref, ref, sem).wait()


def remote(src, dst, send_sem, recv_sem, device):
    pltpu.make_async_remote_copy(
        src_ref=src, dst_ref=dst, send_sem=send_sem, recv_sem=recv_sem, device_id=device, device_id_type=MESH
    ).start()


def planes_kernel(
    inputs_ref, cotangent_ref, w_conv_any, field, upstream, w_conv,
    load_sem, near_send, near_recv, low_recv, high_recv,
):
    sp = lax.axis_index("sp")
    dp = lax.axis_index("dp")
    core = lax.rem(sp, 2)
    z_lo = lax.div(sp, 2)
    below = lax.div(z_lo + 3, 4)
    above = 1 - lax.div(z_lo, 3)
    sibling = {"sp": sp + 1 - 2 * core, "dp": dp}
    barrier = pltpu.get_barrier_semaphore()

    def greet(there):
        pl.semaphore_signal(barrier, inc=1, device_id={"sp": there, "dp": dp}, device_id_type=MESH)

    @pl.when(z_lo > 0)
    def _():
        greet(2 * z_lo - 1)

        @pl.when(core == 0)
        def _():
            greet(sp - 2)

    @pl.when(z_lo < 3)
    def _():
        greet(2 * z_lo + 2)

        @pl.when(core == 1)
        def _():
            greet(sp + 2)

    greet(sp + 1 - 2 * core)
    own_crops = pl.ds(4 * core, 4)
    far_crops = pl.ds(4 * (1 - core), 4)
    loads = [
        pltpu.make_async_copy(inputs_ref.at[own_crops], field.at[1 + core], load_sem.at[0]),
        pltpu.make_async_copy(cotangent_ref.at[own_crops], upstream.at[core], load_sem.at[1]),
        pltpu.make_async_copy(w_conv_any, w_conv, load_sem.at[2]),
    ]
    for load in loads:
        load.start()
    pl.semaphore_wait(barrier, 1 + below * (2 - core) + above * (1 + core))

    @pl.when(core == 0)
    def _():
        @pl.when(z_lo > 0)
        def _():
            for c in range(2):
                remote(inputs_ref.at[pl.ds(4 * c, 4)], field.at[3], near_send.at[1 + c], high_recv, {"sp": sp - 2 + c, "dp": dp})

    @pl.when(core == 1)
    def _():
        @pl.when(z_lo < 3)
        def _():
            for c in range(2):
                remote(inputs_ref.at[pl.ds(4 * c, 4)], field.at[0], near_send.at[1 + c], low_recv, {"sp": sp + 1 + c, "dp": dp})

    remote(inputs_ref.at[far_crops], field.at[1 + core], near_send.at[0], near_recv.at[0], sibling)
    remote(cotangent_ref.at[far_crops], upstream.at[core], near_send.at[3], near_recv.at[1], sibling)

    @pl.when(z_lo == 0)
    def _():
        field[0] = jnp.zeros((4, 64, 128), BF)

    @pl.when(z_lo == 3)
    def _():
        field[3] = jnp.zeros((4, 64, 128), BF)

    for load in loads:
        load.wait()
    group_wait(field.at[0], near_recv.at[0])
    group_wait(field.at[0], near_recv.at[1])
    group_wait(field.at[0], near_send.at[0])
    group_wait(field.at[0], near_send.at[3])
    side = z_lo - 1 + 2 * core

    @pl.when(jnp.logical_and(side >= 0, side <= 3))
    def _():
        group_wait(field.at[0], near_send.at[1])
        group_wait(field.at[0], near_send.at[2])

    @pl.when(z_lo > 0)
    def _():
        group_wait(field.at[0], low_recv)

    @pl.when(z_lo < 3)
    def _():
        group_wait(field.at[3], high_recv)


def step_kernel(
    scale,
    field, upstream, w_conv, w_down, w_up,
    grad_input_ref, share_ref,
    w_flip, columns, turned, slope, order, back, twice, rows,
    grad_field, grad_out,
    pair_in, pair_sum, first_in, first_sum, second_in, second_sum, z_in, final,
    own_sem, halo_send, halo_low, halo_high, grad_send, grad_recv,
    pair_send, pair_recv, first_send, first_recv, second_send, second_recv, z_send, z_recv, out_send, out_recv,
):
    sp = lax.axis_index("sp")
    dp = lax.axis_index("dp")
    core = lax.rem(sp, 2)
    z_lo = lax.div(sp, 2)
    z_hi = lax.div(dp, 16)
    y = lax.rem(lax.div(dp, 4), 4)
    x = lax.rem(dp, 4)
    z = z_hi * 4 + z_lo
    turns = [core, 1 - core, core, 1 - core]
    my_first = [x + turn * (y - x) for turn in turns]
    my_second = [y + turn * (x - y) for turn in turns]

    def member(d):
        there = lax.rem(sp + d, 8)
        return there, {"sp": there, "dp": dp}

    def first_peer(q, d):
        there = lax.rem(my_first[q] + d, 4)
        return there, {"sp": sp, "dp": dp + (there - my_first[q]) * (1 + 3 * turns[q])}

    def second_peer(q, d):
        there = lax.rem(my_second[q] + d, 4)
        return there, {"sp": sp, "dp": dp + (there - my_second[q]) * (4 - 3 * turns[q])}

    barrier = pltpu.get_barrier_semaphore()

    def greet(device):
        pl.semaphore_signal(barrier, inc=1, device_id=device, device_id_type=MESH)

    at_end = jnp.logical_or(z_lo == 0, z_lo == 3)

    def along_z(offset):
        there = lax.rem(z + offset + 16, 16)
        return {"sp": 2 * lax.rem(there, 4) + core, "dp": dp + (lax.div(there, 4) - z_hi) * 16}

    for place, offsets in enumerate(((-6, -5, -4, -3, -2, -1, 4), (-6, -2, 3), (6, 2, -3), (6, 5, 4, 3, 2, 1, -4))):
        @pl.when(z_lo == place)
        def _():
            for offset in offsets:
                greet(along_z(offset))
    for d in range(1, 8):
        greet(member(d)[1])
    for d in range(1, 4):
        greet(first_peer(0, d)[1])
        greet(second_peer(0, d)[1])

    own_crops = pl.ds(4 * core, 4)
    sibling = {"sp": sp + 1 - 2 * core, "dp": dp}
    def goes_low(place):
        return jnp.logical_or(place == 1, place >= 10)

    def goes_high(place):
        return jnp.logical_or(place == 2, jnp.logical_and(place >= 4, place <= 9))

    def pair_start(q):
        for xx in range(4):
            src = rows.at[pl.ds(4 * q, 4), pl.ds(STARTS[xx] + 8 * (1 - core), 8)]
            remote(src, pair_in.at[q, :, xx], pair_send.at[q], pair_recv.at[q], sibling)

    def pair_finish(q):
        group_wait(pair_in.at[q], pair_recv.at[q])
        for yy in range(4):
            for xx in range(4):
                own = rows[4 * q + yy, pl.ds(STARTS[xx] + 8 * core, 8)].astype(F32)
                total = own + pair_in[q, yy, xx].astype(F32)
                pair_sum[q, xx + turns[q] * (yy - xx), yy + turns[q] * (xx - yy)] = total.astype(BF)
        for d in (2, 1, 3):
            there, device = first_peer(q, d)
            remote(pair_sum.at[q, there], first_in.at[q, 3 - d], first_send.at[q], first_recv.at[q], device)

    def first_finish(q):
        group_wait(first_in.at[q], first_recv.at[q])
        for s in range(4):
            total = pair_sum[q, my_first[q], s].astype(F32)
            for d in range(3):
                total = total + first_in[q, d, s].astype(F32)
            first_sum[q, s] = total.astype(BF)
        for d in (2, 1, 3):
            there, device = second_peer(q, d)
            remote(first_sum.at[q, there], second_in.at[q, 3 - d], second_send.at[q], second_recv.at[q], device)

    def second_finish(q):
        group_wait(second_in.at[q], second_recv.at[q])
        total = first_sum[q, my_second[q]].astype(F32)
        for d in range(3):
            total = total + second_in[q, d].astype(F32)
        second_sum[q] = total.astype(BF)
        place = lax.rem(z - 4 * q + 16, 16)
        there = dp + (q - z_hi) * 16

        @pl.when(goes_low(place))
        def _():
            slot = lax.rem(place + 7, 8) * lax.div(place, 10)
            remote(second_sum.at[q], z_in.at[slot], z_send.at[q], z_recv, {"sp": core, "dp": there})

        @pl.when(goes_high(place))
        def _():
            slot = (place - 3) * lax.div(place + 12, 16)
            remote(second_sum.at[q], z_in.at[slot], z_send.at[q], z_recv, {"sp": 6 + core, "dp": there})

    @pl.when(z_lo == 0)
    def _():
        grad_field[0] = jnp.zeros((4, 64, 128), BF)

    @pl.when(z_lo == 3)
    def _():
        grad_field[3] = jnp.zeros((4, 64, 128), BF)

    order_matrices(order, back, twice)
    fill_plane(columns, field, 0, 4)
    pre_conv = tap_dot(columns, w_conv, 0)
    pre_conv += tap_dot(columns, w_conv, 1)
    pre_conv += tap_dot(columns, w_conv, 2)
    hidden, pre_slope = logistic_parts(pre_conv)
    slope[...] = pre_slope
    hid_taps = to_blocks(order[...], hidden.astype(BF))
    deep_act, deep_slope = deep_forward(hid_taps, w_down)
    turned[...] = columns[...].T
    up_taps = to_blocks(order[...], upstream[...].reshape(512, 128))
    grad_deep = deep_grads(up_taps, deep_slope, w_up)
    grad_pre = pre_grads(upstream, grad_deep, w_down, back[...], slope).astype(BF)
    grad_field[1:3] = grad_pre.reshape(2, 4, 64, 128)
    for i in (0, 1):
        conv_grads(rows, turned, grad_pre, i)

    pl.semaphore_wait(barrier, 16 + 2 * (z_lo - 1) * (z_lo - 2))
    pair_start(0)
    conv_grads(rows, turned, grad_pre, 2)
    down_grads(rows, hid_taps, twice[...], grad_deep)
    pair_start(1)
    up_grads(rows, deep_act, up_taps)
    pair_start(2)
    pair_start(3)

    @pl.when(z_lo > 0)
    def _():
        remote(grad_field.at[1], grad_field.at[3], halo_send.at[0], halo_high, {"sp": sp - 2, "dp": dp})

    @pl.when(z_lo < 3)
    def _():
        remote(grad_field.at[2], grad_field.at[0], halo_send.at[1], halo_low, {"sp": sp + 2, "dp": dp})

    pair_finish(0)
    pair_finish(1)
    flip_weights(w_conv, w_flip)
    fill_plane(columns, grad_field, 1, 2)

    @pl.when(z_lo > 0)
    def _():
        group_wait(grad_field.at[0], halo_low)

    @pl.when(z_lo < 3)
    def _():
        group_wait(grad_field.at[3], halo_high)

    fill_plane(columns, grad_field, 0)
    fill_plane(columns, grad_field, 3)
    total = tap_dot(columns, w_flip, 0)
    total += tap_dot(columns, w_flip, 1)
    total += tap_dot(columns, w_flip, 2)
    grad_out[...] = total.astype(BF).reshape(2, 4, 64, 128)
    first_finish(0)
    pair_finish(2)
    first_finish(1)
    pair_finish(3)
    remote(grad_out.at[1 - core], grad_input_ref.at[own_crops], grad_send, grad_recv, sibling)
    own_grad = pltpu.make_async_copy(grad_out.at[core], grad_input_ref.at[own_crops], own_sem)
    own_grad.start()
    second_finish(0)
    first_finish(2)
    second_finish(1)
    first_finish(3)
    second_finish(2)
    second_finish(3)

    @pl.when(at_end)
    def _():
        group_wait(z_in, z_recv)
        total = second_sum[z_hi].astype(F32)
        for d in range(7):
            total = total + z_in[d].astype(F32)
        end = lax.div(z_lo, 3)
        final[end, core] = total.astype(BF)
        for step in range(3):
            for c in range(2):
                there = 2 * (3 - step - end * (3 - 2 * step)) + c
                remote(final.at[end, core], final.at[end, core], out_send, out_recv, {"sp": there, "dp": dp})
        remote(final.at[end, core], final.at[end, core], out_send, out_recv, sibling)
        group_wait(z_in.at[pl.ds(0, 3)], out_recv)

    @pl.when(jnp.logical_not(at_end))
    def _():
        group_wait(z_in.at[pl.ds(0, 4)], out_recv)

    whole = (final[0].astype(F32) + final[1].astype(F32)).reshape(128, 128) * scale
    for xx in range(4):
        @pl.when(x == xx)
        def _():
            share_ref[...] = whole[OFFSETS[xx] : OFFSETS[xx] + SHARE]

    own_grad.wait()
    group_wait(grad_out.at[0], grad_recv)
    group_wait(grad_out.at[0], grad_send)
    @pl.when(z_lo > 0)
    def _():
        group_wait(grad_field.at[0], halo_send.at[0])

    @pl.when(z_lo < 3)
    def _():
        group_wait(grad_field.at[0], halo_send.at[1])

    for q in (3, 2, 1, 0):
        group_wait(pair_in.at[q], pair_send.at[q])
        group_wait(first_in.at[q], first_send.at[q])
        group_wait(second_in.at[q], second_send.at[q])
        place = lax.rem(z - 4 * q + 16, 16)

        @pl.when(jnp.logical_or(goes_low(place), goes_high(place)))
        def _():
            group_wait(z_in.at[0], z_send.at[q])

    @pl.when(at_end)
    def _():
        group_wait(z_in, out_send)


def store_kernel(grad_input_ref, share_ref, grad_input_out, share_out, sem):
    copies = [
        pltpu.make_async_copy(grad_input_ref, grad_input_out, sem.at[0]),
        pltpu.make_async_copy(share_ref, share_out, sem.at[1]),
    ]
    for copy in copies:
        copy.start()
    for copy in copies:
        copy.wait()


def per_device(inputs, cotangent, w_conv, w_down, w_up):
    edge = inputs.shape[2]
    crops = inputs.shape[0] * lax.axis_size("dp")
    scale = 1.0 / math.sqrt(crops * edge * edge * edge)

    def kernel(*refs):
        step_kernel(scale, *refs)

    dma = pltpu.SemaphoreType.DMA
    vmem = pltpu.VMEM
    field, upstream, w_conv = pl.pallas_call(
        planes_kernel,
        out_shape=(
            jax.ShapeDtypeStruct((4, 4, 64, 128), BF),
            jax.ShapeDtypeStruct((2, 4, 64, 128), BF),
            jax.ShapeDtypeStruct((3456, 128), BF),
        ),
        in_specs=[pl.BlockSpec(memory_space=pl.ANY)] * 3,
        out_specs=(pl.BlockSpec(memory_space=vmem),) * 3,
        scratch_shapes=[dma((3,)), dma((4,)), dma((2,)), dma, dma],
        compiler_params=pltpu.CompilerParams(
            collective_id=0, has_side_effects=True, vmem_limit_bytes=16 * 1024 * 1024
        ),
        name="planes",
    )(
        pltpu.with_memory_space_constraint(inputs.reshape(8, 64, 128), pltpu.HBM),
        pltpu.with_memory_space_constraint(cotangent.reshape(8, 64, 128), pltpu.HBM),
        pltpu.with_memory_space_constraint(w_conv, pltpu.HBM),
    )
    grad_input, share = pl.pallas_call(
        kernel,
        out_shape=(
            jax.ShapeDtypeStruct((8, 64, 128), BF),
            jax.ShapeDtypeStruct((SHARE, 128), F32),
        ),
        in_specs=[pl.BlockSpec(memory_space=vmem)] * 5,
        out_specs=(pl.BlockSpec(memory_space=vmem), pl.BlockSpec(memory_space=vmem)),
        scratch_shapes=[
            vmem((3456, 128), BF),
            vmem((1024, 1152), BF),
            vmem((1152, 1024), BF),
            vmem((512, 128), F32),
            vmem((128, 128), BF),
            vmem((128, 128), BF),
            vmem((128, 256), BF),
            vmem((16, TILES, 8, 128), BF),
            vmem((4, 4, 64, 128), BF),
            vmem((2, 4, 64, 128), BF),
            vmem((4, 4, 4, 8, 8, 128), BF),
            vmem((4, 4, 4, 8, 8, 128), BF),
            vmem((4, 3, 4, 8, 8, 128), BF),
            vmem((4, 4, 8, 8, 128), BF),
            vmem((4, 3, 8, 8, 128), BF),
            vmem((4, 8, 8, 128), BF),
            vmem((7, 8, 8, 128), BF),
            vmem((2, 2, 8, 8, 128), BF),
            dma, dma((2,)), dma, dma, dma, dma,
            dma((4,)), dma((4,)), dma((4,)), dma((4,)), dma((4,)), dma((4,)), dma((4,)), dma, dma, dma,
        ],
        compiler_params=pltpu.CompilerParams(
            collective_id=1, has_side_effects=True, vmem_limit_bytes=48 * 1024 * 1024
        ),
        name="whole_step",
    )(field, upstream, w_conv, w_down, w_up)
    grad_input, share = pl.pallas_call(
        store_kernel,
        out_shape=(
            jax.ShapeDtypeStruct((8, 64, 128), BF),
            jax.ShapeDtypeStruct((SHARE, 128), F32),
        ),
        in_specs=[pl.BlockSpec(memory_space=pl.ANY)] * 2,
        out_specs=(pl.BlockSpec(memory_space=pl.ANY),) * 2,
        scratch_shapes=[dma((2,))],
        compiler_params=pltpu.CompilerParams(vmem_limit_bytes=1024 * 1024),
        name="store",
    )(grad_input, share)
    return (grad_input.reshape(inputs.shape), share.reshape(-1))


def solution(mesh):
    return jax.shard_map(
        per_device,
        mesh=mesh,
        in_specs=(P("dp", "sp", None, None, None), P("dp", "sp", None, None, None), P(), P(), P()),
        out_specs=(P("dp", "sp", None, None, None), P("dp")),
        check_vma=False,
    )
```

```python
import math

import jax
import jax.numpy as jnp
from jax import lax
from jax.experimental import pallas as pl
from jax.experimental.pallas import tpu as pltpu
from jax.sharding import PartitionSpec as P

MESH = pl.DeviceIdType.MESH
BF = jnp.bfloat16
F32 = jnp.float32

STARTS = (0, 14, 29, 43)
OFFSETS = (0, 6, 4, 10)
SHARE = 118
TILES = 59
DOWN_TILE = 3456 // 8
UP_TILE = 5504 // 8


def dot(a, b):
    return jnp.dot(a, b, preferred_element_type=F32)


def dot_first(a, b):
    return lax.dot_general(a, b, (((0,), (0,)), ((), ())), preferred_element_type=F32)


def dot_last(a, b):
    return lax.dot_general(a, b, (((1,), (1,)), ((), ())), preferred_element_type=F32)


def order_matrices(order_ref, back_ref, twice_ref):
    row = lax.broadcasted_iota(jnp.int32, (128, 128), 0)
    column = lax.broadcasted_iota(jnp.int32, (128, 128), 1)

    def source(r):
        tap, b, c = r >> 4, (r >> 2) & 3, r & 3
        return ((tap >> 2) << 6) + ((2 * b + ((tap >> 1) & 1)) << 3) + 2 * c + (tap & 1)

    order_ref[...] = jnp.where(column == source(row), 1.0, 0.0).astype(BF)
    back_ref[...] = jnp.where(row == source(column), 1.0, 0.0).astype(BF)
    channel = lax.broadcasted_iota(jnp.int32, (128, 256), 0)
    place = lax.broadcasted_iota(jnp.int32, (128, 256), 1)
    twice_ref[...] = jnp.where(channel == (place >> 1), 1.0, 0.0).astype(BF)


def flip_weights(w_conv_ref, w_flip_ref):
    for t in range(27):
        block = w_conv_ref[128 * (26 - t) : 128 * (27 - t), :]
        w_flip_ref[128 * t : 128 * (t + 1), :] = block.astype(F32).T.astype(BF)


def fill_columns(columns_ref, first, planes):
    count = planes.shape[0] // 64
    lines = planes.reshape(8 * count, 8, 128)
    k_at = lax.broadcasted_iota(jnp.int32, (8 * count, 8, 128), 1)
    zero_line = jnp.zeros((count, 1, 8, 128), F32)
    for k in range(3):
        moved = lines
        if k == 0:
            moved = jnp.where(k_at == 0, 0.0, pltpu.roll(lines, 1, axis=1))
        if k == 2:
            moved = jnp.where(k_at == 7, 0.0, pltpu.roll(lines, 7, axis=1))
        moved = moved.reshape(count, 8, 8, 128)
        for j in range(3):
            shifted = moved
            if j == 0:
                shifted = jnp.concatenate([zero_line, moved[:, :7]], axis=1)
            if j == 2:
                shifted = jnp.concatenate([moved[:, 1:], zero_line], axis=1)
            lane = 128 * (3 * j + k)
            columns_ref[first : first + 64 * count, lane : lane + 128] = shifted.reshape(64 * count, 128).astype(BF)


def fill_plane(columns_ref, field_ref, plane, count=1):
    values = field_ref[plane : plane + count].reshape(256 * count, 128).astype(F32)
    fill_columns(columns_ref, 256 * plane, values)


def tap_dot(columns_ref, weights_ref, i):
    return dot(columns_ref[256 * i : 256 * i + 512, :], weights_ref[1152 * i : 1152 * (i + 1), :])


def to_blocks(order, volume):
    side_by_side = jnp.concatenate(
        [
            jnp.concatenate([volume[64 * c : 64 * c + 64], volume[64 * c + 256 : 64 * c + 320]], axis=0)
            for c in range(4)
        ],
        axis=1,
    )
    moved = dot(order, side_by_side).astype(BF)
    return [
        jnp.concatenate(
            [moved[16 * t : 16 * (t + 1), 128 * c : 128 * (c + 1)] for c in range(4)], axis=0
        )
        for t in range(8)
    ]


def from_blocks(back, blocks):
    stacked = jnp.concatenate(
        [
            jnp.concatenate(
                [blocks[16 * c : 16 * (c + 1), 128 * t : 128 * (t + 1)] for c in range(4)], axis=1
            )
            for t in range(8)
        ],
        axis=0,
    )
    moved = dot(back, stacked)
    return jnp.concatenate(
        [moved[64 * p : 64 * (p + 1), 128 * c : 128 * (c + 1)] for p in range(2) for c in range(4)], axis=0
    )


def put_rows(rows_ref, tile, values):
    count = values.shape[0] // 8
    values = values.reshape(count, 8, 128).astype(BF)
    done = 0
    while done < count:
        block, place = divmod(tile + done, TILES)
        size = min(count - done, TILES - place)
        rows_ref[block, place : place + size] = values[done : done + size]
        done += size


def logistic_parts(pre):
    s = jax.nn.sigmoid(pre)
    return pre * s, s * (1.0 + pre * (1.0 - s))


def deep_forward(hid_taps, w_down_ref):
    pre_deep = dot(jnp.concatenate(hid_taps, axis=1), w_down_ref[...])
    act, slope = logistic_parts(pre_deep)
    return act.astype(BF), slope


def up_grads(rows_ref, deep_act, up_taps):
    for t in range(8):
        put_rows(rows_ref, UP_TILE + 32 * t, dot_first(deep_act, up_taps[t]))


def deep_grads(up_taps, slope, w_up_ref):
    grad_act = dot_last(up_taps[0], w_up_ref[0:256, :])
    for t in range(1, 8):
        grad_act += dot_last(up_taps[t], w_up_ref[256 * t : 256 * (t + 1), :])
    return (grad_act * slope).astype(BF)


def down_grads(rows_ref, hid_taps, twice, grad_deep):
    odd = (lax.broadcasted_iota(jnp.int32, (256, 128), 0) & 1) == 1
    doubled = dot(jnp.concatenate(hid_taps, axis=0), twice).astype(BF)
    for t in range(8):
        both = dot_first(doubled[64 * t : 64 * (t + 1)], grad_deep)
        put_rows(rows_ref, DOWN_TILE + 32 * t, jnp.where(odd, both[:, 128:], both[:, :128]))


def pre_grads(cotangent_ref, grad_deep, w_down_ref, back, slope_ref):
    blocks = dot_last(grad_deep, w_down_ref[...]).astype(BF)
    summed = cotangent_ref[...].reshape(512, 128).astype(F32) + from_blocks(back, blocks)
    return summed * slope_ref[...]


def conv_grads(rows_ref, turned_ref, grad_pre, i):
    put_rows(rows_ref, 144 * i, dot(turned_ref[:, 256 * i : 256 * i + 512], grad_pre))


def group_wait(ref, sem):
    pltpu.make_async_copy(ref, ref, sem).wait()


def remote(src, dst, send_sem, recv_sem, device):
    pltpu.make_async_remote_copy(
        src_ref=src, dst_ref=dst, send_sem=send_sem, recv_sem=recv_sem, device_id=device, device_id_type=MESH
    ).start()


def planes_kernel(
    inputs_ref, cotangent_ref, w_conv_any, w_down_any, w_up_any, columns, middle, upstream, w_conv, w_down, w_up,
    field, load_sem, near_send, near_recv, low_recv, high_recv,
):
    sp = lax.axis_index("sp")
    dp = lax.axis_index("dp")
    core = lax.rem(sp, 2)
    z_lo = lax.div(sp, 2)
    below = lax.div(z_lo + 3, 4)
    above = 1 - lax.div(z_lo, 3)
    sibling = {"sp": sp + 1 - 2 * core, "dp": dp}
    barrier = pltpu.get_barrier_semaphore()

    def greet(there):
        pl.semaphore_signal(barrier, inc=1, device_id={"sp": there, "dp": dp}, device_id_type=MESH)

    @pl.when(z_lo > 0)
    def _():
        greet(2 * z_lo - 1)

        @pl.when(core == 0)
        def _():
            greet(sp - 2)

    @pl.when(z_lo < 3)
    def _():
        greet(2 * z_lo + 2)

        @pl.when(core == 1)
        def _():
            greet(sp + 2)

    greet(sp + 1 - 2 * core)
    own_crops = pl.ds(4 * core, 4)
    far_crops = pl.ds(4 * (1 - core), 4)
    loads = [
        pltpu.make_async_copy(inputs_ref.at[own_crops], field.at[1 + core], load_sem.at[0]),
        pltpu.make_async_copy(cotangent_ref.at[own_crops], upstream.at[core], load_sem.at[1]),
        pltpu.make_async_copy(w_conv_any, w_conv, load_sem.at[2]),
        pltpu.make_async_copy(w_down_any, w_down, load_sem.at[3]),
        pltpu.make_async_copy(w_up_any, w_up, load_sem.at[4]),
    ]
    for load in loads:
        load.start()
    pl.semaphore_wait(barrier, 1 + below * (2 - core) + above * (1 + core))

    @pl.when(core == 0)
    def _():
        @pl.when(z_lo > 0)
        def _():
            for c in range(2):
                remote(inputs_ref.at[pl.ds(4 * c, 4)], field.at[3], near_send.at[1 + c], high_recv, {"sp": sp - 2 + c, "dp": dp})

    @pl.when(core == 1)
    def _():
        @pl.when(z_lo < 3)
        def _():
            for c in range(2):
                remote(inputs_ref.at[pl.ds(4 * c, 4)], field.at[0], near_send.at[1 + c], low_recv, {"sp": sp + 1 + c, "dp": dp})

    remote(inputs_ref.at[far_crops], field.at[1 + core], near_send.at[0], near_recv.at[0], sibling)
    remote(cotangent_ref.at[far_crops], upstream.at[core], near_send.at[3], near_recv.at[1], sibling)

    @pl.when(z_lo == 0)
    def _():
        field[0] = jnp.zeros((4, 64, 128), BF)

    @pl.when(z_lo == 3)
    def _():
        field[3] = jnp.zeros((4, 64, 128), BF)

    for load in loads:
        load.wait()
    group_wait(field.at[0], near_recv.at[0])
    fill_plane(columns, field, 1, 2)
    middle[...] = tap_dot(columns, w_conv, 1)
    group_wait(field.at[0], near_recv.at[1])
    group_wait(field.at[0], near_send.at[0])
    group_wait(field.at[0], near_send.at[3])
    side = z_lo - 1 + 2 * core

    @pl.when(jnp.logical_and(side >= 0, side <= 3))
    def _():
        group_wait(field.at[0], near_send.at[1])
        group_wait(field.at[0], near_send.at[2])

    @pl.when(z_lo > 0)
    def _():
        group_wait(field.at[0], low_recv)

    @pl.when(z_lo < 3)
    def _():
        group_wait(field.at[3], high_recv)

    fill_plane(columns, field, 0)
    fill_plane(columns, field, 3)


def step_kernel(
    scale,
    planes, middle, upstream, w_conv, w_down, w_up,
    grad_input_ref, share_ref,
    w_flip, columns, turned, slope, order, back, twice, rows,
    grad_field, grad_out,
    pair_in, pair_sum, first_in, first_sum, second_in, second_sum, z_in, final,
    own_sem, halo_send, halo_low, halo_high, grad_send, grad_recv,
    pair_send, pair_recv, first_send, first_recv, second_send, second_recv, z_send, z_recv, out_send, out_recv,
):
    sp = lax.axis_index("sp")
    dp = lax.axis_index("dp")
    core = lax.rem(sp, 2)
    z_lo = lax.div(sp, 2)
    z_hi = lax.div(dp, 16)
    y = lax.rem(lax.div(dp, 4), 4)
    x = lax.rem(dp, 4)
    z = z_hi * 4 + z_lo
    turns = [core, 1 - core, core, 1 - core]
    my_first = [x + turn * (y - x) for turn in turns]
    my_second = [y + turn * (x - y) for turn in turns]

    def member(d):
        there = lax.rem(sp + d, 8)
        return there, {"sp": there, "dp": dp}

    def first_peer(q, d):
        there = lax.rem(my_first[q] + d, 4)
        return there, {"sp": sp, "dp": dp + (there - my_first[q]) * (1 + 3 * turns[q])}

    def second_peer(q, d):
        there = lax.rem(my_second[q] + d, 4)
        return there, {"sp": sp, "dp": dp + (there - my_second[q]) * (4 - 3 * turns[q])}

    barrier = pltpu.get_barrier_semaphore()

    def greet(device):
        pl.semaphore_signal(barrier, inc=1, device_id=device, device_id_type=MESH)

    at_end = jnp.logical_or(z_lo == 0, z_lo == 3)

    def along_z(offset):
        there = lax.rem(z + offset + 16, 16)
        return {"sp": 2 * lax.rem(there, 4) + core, "dp": dp + (lax.div(there, 4) - z_hi) * 16}

    for place, offsets in enumerate(((-6, -5, -4, -3, -2, -1, 4), (-6, -2, 3), (6, 2, -3), (6, 5, 4, 3, 2, 1, -4))):
        @pl.when(z_lo == place)
        def _():
            for offset in offsets:
                greet(along_z(offset))
    for d in range(1, 8):
        greet(member(d)[1])
    for d in range(1, 4):
        greet(first_peer(0, d)[1])
        greet(second_peer(0, d)[1])

    own_crops = pl.ds(4 * core, 4)
    sibling = {"sp": sp + 1 - 2 * core, "dp": dp}
    def goes_low(place):
        return jnp.logical_or(place == 1, place >= 10)

    def goes_high(place):
        return jnp.logical_or(place == 2, jnp.logical_and(place >= 4, place <= 9))

    def pair_start(q):
        for xx in range(4):
            src = rows.at[pl.ds(4 * q, 4), pl.ds(STARTS[xx] + 8 * (1 - core), 8)]
            remote(src, pair_in.at[q, :, xx], pair_send.at[q], pair_recv.at[q], sibling)

    def pair_finish(q):
        group_wait(pair_in.at[q], pair_recv.at[q])
        for yy in range(4):
            for xx in range(4):
                own = rows[4 * q + yy, pl.ds(STARTS[xx] + 8 * core, 8)].astype(F32)
                total = own + pair_in[q, yy, xx].astype(F32)
                pair_sum[q, xx + turns[q] * (yy - xx), yy + turns[q] * (xx - yy)] = total.astype(BF)
        for d in (2, 1, 3):
            there, device = first_peer(q, d)
            remote(pair_sum.at[q, there], first_in.at[q, 3 - d], first_send.at[q], first_recv.at[q], device)

    def first_finish(q):
        group_wait(first_in.at[q], first_recv.at[q])
        for s in range(4):
            total = pair_sum[q, my_first[q], s].astype(F32)
            for d in range(3):
                total = total + first_in[q, d, s].astype(F32)
            first_sum[q, s] = total.astype(BF)
        for d in (2, 1, 3):
            there, device = second_peer(q, d)
            remote(first_sum.at[q, there], second_in.at[q, 3 - d], second_send.at[q], second_recv.at[q], device)

    def second_finish(q):
        group_wait(second_in.at[q], second_recv.at[q])
        total = first_sum[q, my_second[q]].astype(F32)
        for d in range(3):
            total = total + second_in[q, d].astype(F32)
        second_sum[q] = total.astype(BF)
        place = lax.rem(z - 4 * q + 16, 16)
        there = dp + (q - z_hi) * 16

        @pl.when(goes_low(place))
        def _():
            slot = lax.rem(place + 7, 8) * lax.div(place, 10)
            remote(second_sum.at[q], z_in.at[slot], z_send.at[q], z_recv, {"sp": core, "dp": there})

        @pl.when(goes_high(place))
        def _():
            slot = (place - 3) * lax.div(place + 12, 16)
            remote(second_sum.at[q], z_in.at[slot], z_send.at[q], z_recv, {"sp": 6 + core, "dp": there})

    @pl.when(z_lo == 0)
    def _():
        grad_field[0] = jnp.zeros((4, 64, 128), BF)

    @pl.when(z_lo == 3)
    def _():
        grad_field[3] = jnp.zeros((4, 64, 128), BF)

    order_matrices(order, back, twice)
    pre_conv = middle[...] + tap_dot(planes, w_conv, 0)
    pre_conv += tap_dot(planes, w_conv, 2)
    hidden, pre_slope = logistic_parts(pre_conv)
    slope[...] = pre_slope
    hid_taps = to_blocks(order[...], hidden.astype(BF))
    deep_act, deep_slope = deep_forward(hid_taps, w_down)
    turned[...] = planes[...].T
    up_taps = to_blocks(order[...], upstream[...].reshape(512, 128))
    grad_deep = deep_grads(up_taps, deep_slope, w_up)
    grad_pre = pre_grads(upstream, grad_deep, w_down, back[...], slope).astype(BF)
    grad_field[1:3] = grad_pre.reshape(2, 4, 64, 128)
    for i in (0, 1):
        conv_grads(rows, turned, grad_pre, i)

    pl.semaphore_wait(barrier, 16 + 2 * (z_lo - 1) * (z_lo - 2))
    pair_start(0)
    conv_grads(rows, turned, grad_pre, 2)
    down_grads(rows, hid_taps, twice[...], grad_deep)
    pair_start(1)
    up_grads(rows, deep_act, up_taps)
    pair_start(2)
    pair_start(3)

    @pl.when(z_lo > 0)
    def _():
        remote(grad_field.at[1], grad_field.at[3], halo_send.at[0], halo_high, {"sp": sp - 2, "dp": dp})

    @pl.when(z_lo < 3)
    def _():
        remote(grad_field.at[2], grad_field.at[0], halo_send.at[1], halo_low, {"sp": sp + 2, "dp": dp})

    pair_finish(0)
    pair_finish(1)
    flip_weights(w_conv, w_flip)
    fill_plane(columns, grad_field, 1, 2)

    @pl.when(z_lo > 0)
    def _():
        group_wait(grad_field.at[0], halo_low)

    @pl.when(z_lo < 3)
    def _():
        group_wait(grad_field.at[3], halo_high)

    fill_plane(columns, grad_field, 0)
    fill_plane(columns, grad_field, 3)
    total = tap_dot(columns, w_flip, 0)
    total += tap_dot(columns, w_flip, 1)
    total += tap_dot(columns, w_flip, 2)
    grad_out[...] = total.astype(BF).reshape(2, 4, 64, 128)
    first_finish(0)
    pair_finish(2)
    first_finish(1)
    pair_finish(3)
    remote(grad_out.at[1 - core], grad_input_ref.at[own_crops], grad_send, grad_recv, sibling)
    own_grad = pltpu.make_async_copy(grad_out.at[core], grad_input_ref.at[own_crops], own_sem)
    own_grad.start()
    second_finish(0)
    first_finish(2)
    second_finish(1)
    first_finish(3)
    second_finish(2)
    second_finish(3)

    @pl.when(at_end)
    def _():
        group_wait(z_in, z_recv)
        total = second_sum[z_hi].astype(F32)
        for d in range(7):
            total = total + z_in[d].astype(F32)
        end = lax.div(z_lo, 3)
        final[end, core] = total.astype(BF)
        for step in range(3):
            for c in range(2):
                there = 2 * (3 - step - end * (3 - 2 * step)) + c
                remote(final.at[end, core], final.at[end, core], out_send, out_recv, {"sp": there, "dp": dp})
        remote(final.at[end, core], final.at[end, core], out_send, out_recv, sibling)
        group_wait(z_in.at[pl.ds(0, 3)], out_recv)

    @pl.when(jnp.logical_not(at_end))
    def _():
        group_wait(z_in.at[pl.ds(0, 4)], out_recv)

    whole = (final[0].astype(F32) + final[1].astype(F32)).reshape(128, 128) * scale
    for xx in range(4):
        @pl.when(x == xx)
        def _():
            share_ref[...] = whole[OFFSETS[xx] : OFFSETS[xx] + SHARE]

    own_grad.wait()
    group_wait(grad_out.at[0], grad_recv)
    group_wait(grad_out.at[0], grad_send)
    @pl.when(z_lo > 0)
    def _():
        group_wait(grad_field.at[0], halo_send.at[0])

    @pl.when(z_lo < 3)
    def _():
        group_wait(grad_field.at[0], halo_send.at[1])

    for q in (3, 2, 1, 0):
        group_wait(pair_in.at[q], pair_send.at[q])
        group_wait(first_in.at[q], first_send.at[q])
        group_wait(second_in.at[q], second_send.at[q])
        place = lax.rem(z - 4 * q + 16, 16)

        @pl.when(jnp.logical_or(goes_low(place), goes_high(place)))
        def _():
            group_wait(z_in.at[0], z_send.at[q])

    @pl.when(at_end)
    def _():
        group_wait(z_in, out_send)


def store_kernel(grad_input_ref, share_ref, grad_input_out, share_out, sem):
    copies = [
        pltpu.make_async_copy(grad_input_ref, grad_input_out, sem.at[0]),
        pltpu.make_async_copy(share_ref, share_out, sem.at[1]),
    ]
    for copy in copies:
        copy.start()
    for copy in copies:
        copy.wait()


def per_device(inputs, cotangent, w_conv, w_down, w_up):
    edge = inputs.shape[2]
    crops = inputs.shape[0] * lax.axis_size("dp")
    scale = 1.0 / math.sqrt(crops * edge * edge * edge)

    def kernel(*refs):
        step_kernel(scale, *refs)

    dma = pltpu.SemaphoreType.DMA
    vmem = pltpu.VMEM
    planes, middle, upstream, w_conv, w_down, w_up = pl.pallas_call(
        planes_kernel,
        out_shape=(
            jax.ShapeDtypeStruct((1024, 1152), BF),
            jax.ShapeDtypeStruct((512, 128), F32),
            jax.ShapeDtypeStruct((2, 4, 64, 128), BF),
            jax.ShapeDtypeStruct((3456, 128), BF),
            jax.ShapeDtypeStruct((1024, 256), BF),
            jax.ShapeDtypeStruct((2048, 128), BF),
        ),
        in_specs=[pl.BlockSpec(memory_space=pl.ANY)] * 5,
        out_specs=(pl.BlockSpec(memory_space=vmem),) * 6,
        scratch_shapes=[vmem((4, 4, 64, 128), BF), dma((5,)), dma((4,)), dma((2,)), dma, dma],
        compiler_params=pltpu.CompilerParams(
            collective_id=0, has_side_effects=True, vmem_limit_bytes=16 * 1024 * 1024
        ),
        name="planes",
    )(
        pltpu.with_memory_space_constraint(inputs.reshape(8, 64, 128), pltpu.HBM),
        pltpu.with_memory_space_constraint(cotangent.reshape(8, 64, 128), pltpu.HBM),
        pltpu.with_memory_space_constraint(w_conv, pltpu.HBM),
        pltpu.with_memory_space_constraint(w_down, pltpu.HBM),
        pltpu.with_memory_space_constraint(w_up, pltpu.HBM),
    )
    grad_input, share = pl.pallas_call(
        kernel,
        out_shape=(
            jax.ShapeDtypeStruct((8, 64, 128), BF),
            jax.ShapeDtypeStruct((SHARE, 128), F32),
        ),
        in_specs=[pl.BlockSpec(memory_space=vmem)] * 6,
        out_specs=(pl.BlockSpec(memory_space=vmem), pl.BlockSpec(memory_space=vmem)),
        scratch_shapes=[
            vmem((3456, 128), BF),
            vmem((1024, 1152), BF),
            vmem((1152, 1024), BF),
            vmem((512, 128), F32),
            vmem((128, 128), BF),
            vmem((128, 128), BF),
            vmem((128, 256), BF),
            vmem((16, TILES, 8, 128), BF),
            vmem((4, 4, 64, 128), BF),
            vmem((2, 4, 64, 128), BF),
            vmem((4, 4, 4, 8, 8, 128), BF),
            vmem((4, 4, 4, 8, 8, 128), BF),
            vmem((4, 3, 4, 8, 8, 128), BF),
            vmem((4, 4, 8, 8, 128), BF),
            vmem((4, 3, 8, 8, 128), BF),
            vmem((4, 8, 8, 128), BF),
            vmem((7, 8, 8, 128), BF),
            vmem((2, 2, 8, 8, 128), BF),
            dma, dma((2,)), dma, dma, dma, dma,
            dma((4,)), dma((4,)), dma((4,)), dma((4,)), dma((4,)), dma((4,)), dma((4,)), dma, dma, dma,
        ],
        compiler_params=pltpu.CompilerParams(
            collective_id=1, has_side_effects=True, vmem_limit_bytes=48 * 1024 * 1024
        ),
        name="whole_step",
    )(planes, middle, upstream, w_conv, w_down, w_up)
    grad_input, share = pl.pallas_call(
        store_kernel,
        out_shape=(
            jax.ShapeDtypeStruct((8, 64, 128), BF),
            jax.ShapeDtypeStruct((SHARE, 128), F32),
        ),
        in_specs=[pl.BlockSpec(memory_space=pl.ANY)] * 2,
        out_specs=(pl.BlockSpec(memory_space=pl.ANY),) * 2,
        scratch_shapes=[dma((2,))],
        compiler_params=pltpu.CompilerParams(vmem_limit_bytes=1024 * 1024),
        name="store",
    )(grad_input, share)
    return (grad_input.reshape(inputs.shape), share.reshape(-1))


def solution(mesh):
    return jax.shard_map(
        per_device,
        mesh=mesh,
        in_specs=(P("dp", "sp", None, None, None), P("dp", "sp", None, None, None), P(), P(), P()),
        out_specs=(P("dp", "sp", None, None, None), P("dp")),
        check_vma=False,
    )
```

```python
import math

import jax
import jax.numpy as jnp
from jax import lax
from jax.experimental import pallas as pl
from jax.experimental.pallas import tpu as pltpu
from jax.sharding import PartitionSpec as P

MESH = pl.DeviceIdType.MESH
BF = jnp.bfloat16
F32 = jnp.float32

STARTS = (0, 14, 29, 43)
OFFSETS = (0, 6, 4, 10)
SHARE = 118
TILES = 59
DOWN_TILE = 3456 // 8
UP_TILE = 5504 // 8


def dot(a, b):
    return jnp.dot(a, b, preferred_element_type=F32)


def dot_first(a, b):
    return lax.dot_general(a, b, (((0,), (0,)), ((), ())), preferred_element_type=F32)


def dot_last(a, b):
    return lax.dot_general(a, b, (((1,), (1,)), ((), ())), preferred_element_type=F32)


def order_matrices(order_ref, back_ref, twice_ref):
    row = lax.broadcasted_iota(jnp.int32, (128, 128), 0)
    column = lax.broadcasted_iota(jnp.int32, (128, 128), 1)

    def source(r):
        tap, b, c = r >> 4, (r >> 2) & 3, r & 3
        return ((tap >> 2) << 6) + ((2 * b + ((tap >> 1) & 1)) << 3) + 2 * c + (tap & 1)

    order_ref[...] = jnp.where(column == source(row), 1.0, 0.0).astype(BF)
    back_ref[...] = jnp.where(row == source(column), 1.0, 0.0).astype(BF)
    channel = lax.broadcasted_iota(jnp.int32, (128, 256), 0)
    place = lax.broadcasted_iota(jnp.int32, (128, 256), 1)
    twice_ref[...] = jnp.where(channel == (place >> 1), 1.0, 0.0).astype(BF)


def flip_weights(w_conv_ref, w_flip_ref):
    for t in range(27):
        block = w_conv_ref[128 * (26 - t) : 128 * (27 - t), :]
        w_flip_ref[128 * t : 128 * (t + 1), :] = block.astype(F32).T.astype(BF)


def fill_columns(columns_ref, first, planes):
    count = planes.shape[0] // 64
    lines = planes.reshape(8 * count, 8, 128)
    k_at = lax.broadcasted_iota(jnp.int32, (8 * count, 8, 128), 1)
    zero_line = jnp.zeros((count, 1, 8, 128), F32)
    for k in range(3):
        moved = lines
        if k == 0:
            moved = jnp.where(k_at == 0, 0.0, pltpu.roll(lines, 1, axis=1))
        if k == 2:
            moved = jnp.where(k_at == 7, 0.0, pltpu.roll(lines, 7, axis=1))
        moved = moved.reshape(count, 8, 8, 128)
        for j in range(3):
            shifted = moved
            if j == 0:
                shifted = jnp.concatenate([zero_line, moved[:, :7]], axis=1)
            if j == 2:
                shifted = jnp.concatenate([moved[:, 1:], zero_line], axis=1)
            lane = 128 * (3 * j + k)
            columns_ref[first : first + 64 * count, lane : lane + 128] = shifted.reshape(64 * count, 128).astype(BF)


def fill_plane(columns_ref, field_ref, plane, count=1):
    values = field_ref[plane : plane + count].reshape(256 * count, 128).astype(F32)
    fill_columns(columns_ref, 256 * plane, values)


def tap_dot(columns_ref, weights_ref, i):
    return dot(columns_ref[256 * i : 256 * i + 512, :], weights_ref[1152 * i : 1152 * (i + 1), :])


def to_blocks(order, volume):
    side_by_side = jnp.concatenate(
        [
            jnp.concatenate([volume[64 * c : 64 * c + 64], volume[64 * c + 256 : 64 * c + 320]], axis=0)
            for c in range(4)
        ],
        axis=1,
    )
    moved = dot(order, side_by_side).astype(BF)
    return [
        jnp.concatenate(
            [moved[16 * t : 16 * (t + 1), 128 * c : 128 * (c + 1)] for c in range(4)], axis=0
        )
        for t in range(8)
    ]


def from_blocks(back, blocks):
    stacked = jnp.concatenate(
        [
            jnp.concatenate(
                [blocks[16 * c : 16 * (c + 1), 128 * t : 128 * (t + 1)] for c in range(4)], axis=1
            )
            for t in range(8)
        ],
        axis=0,
    )
    moved = dot(back, stacked)
    return jnp.concatenate(
        [moved[64 * p : 64 * (p + 1), 128 * c : 128 * (c + 1)] for p in range(2) for c in range(4)], axis=0
    )


def put_rows(rows_ref, tile, values):
    count = values.shape[0] // 8
    values = values.reshape(count, 8, 128).astype(BF)
    done = 0
    while done < count:
        block, place = divmod(tile + done, TILES)
        size = min(count - done, TILES - place)
        rows_ref[block, place : place + size] = values[done : done + size]
        done += size


def logistic_parts(pre):
    s = jax.nn.sigmoid(pre)
    return pre * s, s * (1.0 + pre * (1.0 - s))


def deep_forward(hid_taps, w_down_ref):
    pre_deep = dot(jnp.concatenate(hid_taps, axis=1), w_down_ref[...])
    act, slope = logistic_parts(pre_deep)
    return act.astype(BF), slope


def up_grads(rows_ref, deep_act, up_taps):
    for t in range(8):
        put_rows(rows_ref, UP_TILE + 32 * t, dot_first(deep_act, up_taps[t]))


def deep_grads(up_taps, slope, w_up_ref):
    grad_act = dot_last(up_taps[0], w_up_ref[0:256, :])
    for t in range(1, 8):
        grad_act += dot_last(up_taps[t], w_up_ref[256 * t : 256 * (t + 1), :])
    return (grad_act * slope).astype(BF)


def down_grads(rows_ref, hid_taps, twice, grad_deep):
    odd = (lax.broadcasted_iota(jnp.int32, (256, 128), 0) & 1) == 1
    doubled = dot(jnp.concatenate(hid_taps, axis=0), twice).astype(BF)
    for t in range(8):
        both = dot_first(doubled[64 * t : 64 * (t + 1)], grad_deep)
        put_rows(rows_ref, DOWN_TILE + 32 * t, jnp.where(odd, both[:, 128:], both[:, :128]))


def pre_grads(cotangent_ref, grad_deep, w_down_ref, back, slope_ref):
    blocks = dot_last(grad_deep, w_down_ref[...]).astype(BF)
    summed = cotangent_ref[...].reshape(512, 128).astype(F32) + from_blocks(back, blocks)
    return summed * slope_ref[...]


def conv_grads(rows_ref, turned_ref, grad_pre, i):
    put_rows(rows_ref, 144 * i, dot(turned_ref[:, 256 * i : 256 * i + 512], grad_pre))


def group_wait(ref, sem):
    pltpu.make_async_copy(ref, ref, sem).wait()


def remote(src, dst, send_sem, recv_sem, device):
    pltpu.make_async_remote_copy(
        src_ref=src, dst_ref=dst, send_sem=send_sem, recv_sem=recv_sem, device_id=device, device_id_type=MESH
    ).start()


def planes_kernel(
    inputs_ref, cotangent_ref, w_conv_any, w_down_any, w_up_any, columns, middle, upstream, w_conv, w_down, w_up,
    order, back, twice, field, load_sem, near_send, near_recv, low_recv, high_recv,
):
    sp = lax.axis_index("sp")
    dp = lax.axis_index("dp")
    core = lax.rem(sp, 2)
    z_lo = lax.div(sp, 2)
    below = lax.div(z_lo + 3, 4)
    above = 1 - lax.div(z_lo, 3)
    sibling = {"sp": sp + 1 - 2 * core, "dp": dp}
    barrier = pltpu.get_barrier_semaphore()

    def greet(there):
        pl.semaphore_signal(barrier, inc=1, device_id={"sp": there, "dp": dp}, device_id_type=MESH)

    @pl.when(z_lo > 0)
    def _():
        greet(2 * z_lo - 1)

        @pl.when(core == 0)
        def _():
            greet(sp - 2)

    @pl.when(z_lo < 3)
    def _():
        greet(2 * z_lo + 2)

        @pl.when(core == 1)
        def _():
            greet(sp + 2)

    greet(sp + 1 - 2 * core)
    own_crops = pl.ds(4 * core, 4)
    far_crops = pl.ds(4 * (1 - core), 4)
    loads = [
        pltpu.make_async_copy(inputs_ref.at[own_crops], field.at[1 + core], load_sem.at[0]),
        pltpu.make_async_copy(cotangent_ref.at[own_crops], upstream.at[core], load_sem.at[1]),
        pltpu.make_async_copy(w_conv_any, w_conv, load_sem.at[2]),
        pltpu.make_async_copy(w_down_any, w_down, load_sem.at[3]),
        pltpu.make_async_copy(w_up_any, w_up, load_sem.at[4]),
    ]
    for load in loads:
        load.start()
    pl.semaphore_wait(barrier, 1 + below * (2 - core) + above * (1 + core))

    @pl.when(core == 0)
    def _():
        @pl.when(z_lo > 0)
        def _():
            for c in range(2):
                remote(inputs_ref.at[pl.ds(4 * c, 4)], field.at[3], near_send.at[1 + c], high_recv, {"sp": sp - 2 + c, "dp": dp})

    @pl.when(core == 1)
    def _():
        @pl.when(z_lo < 3)
        def _():
            for c in range(2):
                remote(inputs_ref.at[pl.ds(4 * c, 4)], field.at[0], near_send.at[1 + c], low_recv, {"sp": sp + 1 + c, "dp": dp})

    remote(inputs_ref.at[far_crops], field.at[1 + core], near_send.at[0], near_recv.at[0], sibling)
    remote(cotangent_ref.at[far_crops], upstream.at[core], near_send.at[3], near_recv.at[1], sibling)

    @pl.when(z_lo == 0)
    def _():
        field[0] = jnp.zeros((4, 64, 128), BF)

    @pl.when(z_lo == 3)
    def _():
        field[3] = jnp.zeros((4, 64, 128), BF)

    order_matrices(order, back, twice)
    for load in loads:
        load.wait()
    group_wait(field.at[0], near_recv.at[0])
    fill_plane(columns, field, 1, 2)
    middle[...] = tap_dot(columns, w_conv, 1)
    group_wait(field.at[0], near_recv.at[1])
    group_wait(field.at[0], near_send.at[0])
    group_wait(field.at[0], near_send.at[3])
    side = z_lo - 1 + 2 * core

    @pl.when(jnp.logical_and(side >= 0, side <= 3))
    def _():
        group_wait(field.at[0], near_send.at[1])
        group_wait(field.at[0], near_send.at[2])

    @pl.when(z_lo > 0)
    def _():
        group_wait(field.at[0], low_recv)

    @pl.when(z_lo < 3)
    def _():
        group_wait(field.at[3], high_recv)

    fill_plane(columns, field, 0)
    fill_plane(columns, field, 3)


def step_kernel(
    scale,
    planes, middle, upstream, w_conv, w_down, w_up, order, back, twice,
    grad_input_ref, share_ref,
    w_flip, columns, turned, slope, rows,
    grad_field, grad_out,
    pair_in, pair_sum, first_in, first_sum, second_in, second_sum, z_in, final,
    own_sem, halo_send, halo_low, halo_high, grad_send, grad_recv,
    pair_send, pair_recv, first_send, first_recv, second_send, second_recv, z_send, z_recv, out_send, out_recv,
):
    sp = lax.axis_index("sp")
    dp = lax.axis_index("dp")
    core = lax.rem(sp, 2)
    z_lo = lax.div(sp, 2)
    z_hi = lax.div(dp, 16)
    y = lax.rem(lax.div(dp, 4), 4)
    x = lax.rem(dp, 4)
    z = z_hi * 4 + z_lo
    turns = [core, 1 - core, core, 1 - core]
    my_first = [x + turn * (y - x) for turn in turns]
    my_second = [y + turn * (x - y) for turn in turns]

    def member(d):
        there = lax.rem(sp + d, 8)
        return there, {"sp": there, "dp": dp}

    def first_peer(q, d):
        there = lax.rem(my_first[q] + d, 4)
        return there, {"sp": sp, "dp": dp + (there - my_first[q]) * (1 + 3 * turns[q])}

    def second_peer(q, d):
        there = lax.rem(my_second[q] + d, 4)
        return there, {"sp": sp, "dp": dp + (there - my_second[q]) * (4 - 3 * turns[q])}

    barrier = pltpu.get_barrier_semaphore()

    def greet(device):
        pl.semaphore_signal(barrier, inc=1, device_id=device, device_id_type=MESH)

    at_end = jnp.logical_or(z_lo == 0, z_lo == 3)

    def along_z(offset):
        there = lax.rem(z + offset + 16, 16)
        return {"sp": 2 * lax.rem(there, 4) + core, "dp": dp + (lax.div(there, 4) - z_hi) * 16}

    for place, offsets in enumerate(((-6, -5, -4, -3, -2, -1, 4), (-6, -2, 3), (6, 2, -3), (6, 5, 4, 3, 2, 1, -4))):
        @pl.when(z_lo == place)
        def _():
            for offset in offsets:
                greet(along_z(offset))
    for d in range(1, 8):
        greet(member(d)[1])
    for d in range(1, 4):
        greet(first_peer(0, d)[1])
        greet(second_peer(0, d)[1])

    own_crops = pl.ds(4 * core, 4)
    sibling = {"sp": sp + 1 - 2 * core, "dp": dp}
    def goes_low(place):
        return jnp.logical_or(place == 1, place >= 10)

    def goes_high(place):
        return jnp.logical_or(place == 2, jnp.logical_and(place >= 4, place <= 9))

    def pair_start(q):
        for xx in range(4):
            src = rows.at[pl.ds(4 * q, 4), pl.ds(STARTS[xx] + 8 * (1 - core), 8)]
            remote(src, pair_in.at[q, :, xx], pair_send.at[q], pair_recv.at[q], sibling)

    def pair_finish(q):
        group_wait(pair_in.at[q], pair_recv.at[q])
        for yy in range(4):
            for xx in range(4):
                own = rows[4 * q + yy, pl.ds(STARTS[xx] + 8 * core, 8)].astype(F32)
                total = own + pair_in[q, yy, xx].astype(F32)
                pair_sum[q, xx + turns[q] * (yy - xx), yy + turns[q] * (xx - yy)] = total.astype(BF)
        for d in (2, 1, 3):
            there, device = first_peer(q, d)
            remote(pair_sum.at[q, there], first_in.at[q, 3 - d], first_send.at[q], first_recv.at[q], device)

    def first_finish(q):
        group_wait(first_in.at[q], first_recv.at[q])
        for s in range(4):
            total = pair_sum[q, my_first[q], s].astype(F32)
            for d in range(3):
                total = total + first_in[q, d, s].astype(F32)
            first_sum[q, s] = total.astype(BF)
        for d in (2, 1, 3):
            there, device = second_peer(q, d)
            remote(first_sum.at[q, there], second_in.at[q, 3 - d], second_send.at[q], second_recv.at[q], device)

    def second_finish(q):
        group_wait(second_in.at[q], second_recv.at[q])
        total = first_sum[q, my_second[q]].astype(F32)
        for d in range(3):
            total = total + second_in[q, d].astype(F32)
        second_sum[q] = total.astype(BF)
        place = lax.rem(z - 4 * q + 16, 16)
        there = dp + (q - z_hi) * 16

        @pl.when(goes_low(place))
        def _():
            slot = lax.rem(place + 7, 8) * lax.div(place, 10)
            remote(second_sum.at[q], z_in.at[slot], z_send.at[q], z_recv, {"sp": core, "dp": there})

        @pl.when(goes_high(place))
        def _():
            slot = (place - 3) * lax.div(place + 12, 16)
            remote(second_sum.at[q], z_in.at[slot], z_send.at[q], z_recv, {"sp": 6 + core, "dp": there})

    @pl.when(z_lo == 0)
    def _():
        grad_field[0] = jnp.zeros((4, 64, 128), BF)

    @pl.when(z_lo == 3)
    def _():
        grad_field[3] = jnp.zeros((4, 64, 128), BF)

    pre_conv = middle[...] + tap_dot(planes, w_conv, 0)
    pre_conv += tap_dot(planes, w_conv, 2)
    hidden, pre_slope = logistic_parts(pre_conv)
    slope[...] = pre_slope
    hid_taps = to_blocks(order[...], hidden.astype(BF))
    deep_act, deep_slope = deep_forward(hid_taps, w_down)
    turned[...] = planes[...].T
    up_taps = to_blocks(order[...], upstream[...].reshape(512, 128))
    grad_deep = deep_grads(up_taps, deep_slope, w_up)
    grad_pre = pre_grads(upstream, grad_deep, w_down, back[...], slope).astype(BF)
    grad_field[1:3] = grad_pre.reshape(2, 4, 64, 128)
    for i in (0, 1):
        conv_grads(rows, turned, grad_pre, i)

    pl.semaphore_wait(barrier, 16 + 2 * (z_lo - 1) * (z_lo - 2))
    pair_start(0)
    conv_grads(rows, turned, grad_pre, 2)
    down_grads(rows, hid_taps, twice[...], grad_deep)
    pair_start(1)
    up_grads(rows, deep_act, up_taps)
    pair_start(2)
    pair_start(3)

    @pl.when(z_lo > 0)
    def _():
        remote(grad_field.at[1], grad_field.at[3], halo_send.at[0], halo_high, {"sp": sp - 2, "dp": dp})

    @pl.when(z_lo < 3)
    def _():
        remote(grad_field.at[2], grad_field.at[0], halo_send.at[1], halo_low, {"sp": sp + 2, "dp": dp})

    pair_finish(0)
    pair_finish(1)
    flip_weights(w_conv, w_flip)
    fill_plane(columns, grad_field, 1, 2)

    @pl.when(z_lo > 0)
    def _():
        group_wait(grad_field.at[0], halo_low)

    @pl.when(z_lo < 3)
    def _():
        group_wait(grad_field.at[3], halo_high)

    fill_plane(columns, grad_field, 0)
    fill_plane(columns, grad_field, 3)
    total = tap_dot(columns, w_flip, 0)
    total += tap_dot(columns, w_flip, 1)
    total += tap_dot(columns, w_flip, 2)
    grad_out[...] = total.astype(BF).reshape(2, 4, 64, 128)
    first_finish(0)
    pair_finish(2)
    first_finish(1)
    pair_finish(3)
    remote(grad_out.at[1 - core], grad_input_ref.at[own_crops], grad_send, grad_recv, sibling)
    own_grad = pltpu.make_async_copy(grad_out.at[core], grad_input_ref.at[own_crops], own_sem)
    own_grad.start()
    second_finish(0)
    first_finish(2)
    second_finish(1)
    first_finish(3)
    second_finish(2)
    second_finish(3)

    @pl.when(at_end)
    def _():
        group_wait(z_in, z_recv)
        total = second_sum[z_hi].astype(F32)
        for d in range(7):
            total = total + z_in[d].astype(F32)
        end = lax.div(z_lo, 3)
        final[end, core] = total.astype(BF)
        for step in range(3):
            for c in range(2):
                there = 2 * (3 - step - end * (3 - 2 * step)) + c
                remote(final.at[end, core], final.at[end, core], out_send, out_recv, {"sp": there, "dp": dp})
        remote(final.at[end, core], final.at[end, core], out_send, out_recv, sibling)
        group_wait(z_in.at[pl.ds(0, 3)], out_recv)

    @pl.when(jnp.logical_not(at_end))
    def _():
        group_wait(z_in.at[pl.ds(0, 4)], out_recv)

    whole = (final[0].astype(F32) + final[1].astype(F32)).reshape(128, 128) * scale
    for xx in range(4):
        @pl.when(x == xx)
        def _():
            share_ref[...] = whole[OFFSETS[xx] : OFFSETS[xx] + SHARE]

    own_grad.wait()
    group_wait(grad_out.at[0], grad_recv)
    group_wait(grad_out.at[0], grad_send)
    @pl.when(z_lo > 0)
    def _():
        group_wait(grad_field.at[0], halo_send.at[0])

    @pl.when(z_lo < 3)
    def _():
        group_wait(grad_field.at[0], halo_send.at[1])

    for q in (3, 2, 1, 0):
        group_wait(pair_in.at[q], pair_send.at[q])
        group_wait(first_in.at[q], first_send.at[q])
        group_wait(second_in.at[q], second_send.at[q])
        place = lax.rem(z - 4 * q + 16, 16)

        @pl.when(jnp.logical_or(goes_low(place), goes_high(place)))
        def _():
            group_wait(z_in.at[0], z_send.at[q])

    @pl.when(at_end)
    def _():
        group_wait(z_in, out_send)


def store_kernel(grad_input_ref, share_ref, grad_input_out, share_out, sem):
    copies = [
        pltpu.make_async_copy(grad_input_ref, grad_input_out, sem.at[0]),
        pltpu.make_async_copy(share_ref, share_out, sem.at[1]),
    ]
    for copy in copies:
        copy.start()
    for copy in copies:
        copy.wait()


def per_device(inputs, cotangent, w_conv, w_down, w_up):
    edge = inputs.shape[2]
    crops = inputs.shape[0] * lax.axis_size("dp")
    scale = 1.0 / math.sqrt(crops * edge * edge * edge)

    def kernel(*refs):
        step_kernel(scale, *refs)

    dma = pltpu.SemaphoreType.DMA
    vmem = pltpu.VMEM
    held = pl.pallas_call(
        planes_kernel,
        out_shape=(
            jax.ShapeDtypeStruct((1024, 1152), BF),
            jax.ShapeDtypeStruct((512, 128), F32),
            jax.ShapeDtypeStruct((2, 4, 64, 128), BF),
            jax.ShapeDtypeStruct((3456, 128), BF),
            jax.ShapeDtypeStruct((1024, 256), BF),
            jax.ShapeDtypeStruct((2048, 128), BF),
            jax.ShapeDtypeStruct((128, 128), BF),
            jax.ShapeDtypeStruct((128, 128), BF),
            jax.ShapeDtypeStruct((128, 256), BF),
        ),
        in_specs=[pl.BlockSpec(memory_space=pl.ANY)] * 5,
        out_specs=(pl.BlockSpec(memory_space=vmem),) * 9,
        scratch_shapes=[vmem((4, 4, 64, 128), BF), dma((5,)), dma((4,)), dma((2,)), dma, dma],
        compiler_params=pltpu.CompilerParams(
            collective_id=0, has_side_effects=True, vmem_limit_bytes=16 * 1024 * 1024
        ),
        name="planes",
    )(
        pltpu.with_memory_space_constraint(inputs.reshape(8, 64, 128), pltpu.HBM),
        pltpu.with_memory_space_constraint(cotangent.reshape(8, 64, 128), pltpu.HBM),
        pltpu.with_memory_space_constraint(w_conv, pltpu.HBM),
        pltpu.with_memory_space_constraint(w_down, pltpu.HBM),
        pltpu.with_memory_space_constraint(w_up, pltpu.HBM),
    )
    grad_input, share = pl.pallas_call(
        kernel,
        out_shape=(
            jax.ShapeDtypeStruct((8, 64, 128), BF),
            jax.ShapeDtypeStruct((SHARE, 128), F32),
        ),
        in_specs=[pl.BlockSpec(memory_space=vmem)] * 9,
        out_specs=(pl.BlockSpec(memory_space=vmem), pl.BlockSpec(memory_space=vmem)),
        scratch_shapes=[
            vmem((3456, 128), BF),
            vmem((1024, 1152), BF),
            vmem((1152, 1024), BF),
            vmem((512, 128), F32),
            vmem((16, TILES, 8, 128), BF),
            vmem((4, 4, 64, 128), BF),
            vmem((2, 4, 64, 128), BF),
            vmem((4, 4, 4, 8, 8, 128), BF),
            vmem((4, 4, 4, 8, 8, 128), BF),
            vmem((4, 3, 4, 8, 8, 128), BF),
            vmem((4, 4, 8, 8, 128), BF),
            vmem((4, 3, 8, 8, 128), BF),
            vmem((4, 8, 8, 128), BF),
            vmem((7, 8, 8, 128), BF),
            vmem((2, 2, 8, 8, 128), BF),
            dma, dma((2,)), dma, dma, dma, dma,
            dma((4,)), dma((4,)), dma((4,)), dma((4,)), dma((4,)), dma((4,)), dma((4,)), dma, dma, dma,
        ],
        compiler_params=pltpu.CompilerParams(
            collective_id=1, has_side_effects=True, vmem_limit_bytes=48 * 1024 * 1024
        ),
        name="whole_step",
    )(*held)
    grad_input, share = pl.pallas_call(
        store_kernel,
        out_shape=(
            jax.ShapeDtypeStruct((8, 64, 128), BF),
            jax.ShapeDtypeStruct((SHARE, 128), F32),
        ),
        in_specs=[pl.BlockSpec(memory_space=pl.ANY)] * 2,
        out_specs=(pl.BlockSpec(memory_space=pl.ANY),) * 2,
        scratch_shapes=[dma((2,))],
        compiler_params=pltpu.CompilerParams(vmem_limit_bytes=1024 * 1024),
        name="store",
    )(grad_input, share)
    return (grad_input.reshape(inputs.shape), share.reshape(-1))


def solution(mesh):
    return jax.shard_map(
        per_device,
        mesh=mesh,
        in_specs=(P("dp", "sp", None, None, None), P("dp", "sp", None, None, None), P(), P(), P()),
        out_specs=(P("dp", "sp", None, None, None), P("dp")),
        check_vma=False,
    )
```
